256 devices in a mesh: seq: 64 (over z, x, core), tp: 4 (over y).
Axes of the slice: x: 4, y: 4, z: 8, core: 2. Of those that a mesh axis runs over, the one named last changes fastest.
Arguments:
- layer_input: bfloat16 [16384, 2048], P('seq'), may hold values from -1.5 to 1.5
- norm_gain: float32 [2048], replicated, may hold values from 0.5 to 1.5
- w_query: bfloat16 [2048, 2048], P(None, 'tp')
- key_weight: bfloat16 [2048, 1024], P(None, 'tp')
- value_weight: bfloat16 [2048, 1024], P(None, 'tp'), may hold values from -0.125 to 0.125
- w_out: bfloat16 [2048, 2048], P('tp'), may hold values from -1 to 1
- query_gain: float32 [128], replicated, may hold values from 0.6 to 6, as said below
- key_gain: float32 [128], replicated, may hold values from 0.6 to 6, as said below
- seg_ids: int32 [16384], P('seq'), may hold values from 0 to 7, as said below
- positions: int32 [16384], P('seq'), may hold values from 0 to 13106, as said below
- post_gain: float32 [2048], replicated, may hold values from 0.5 to 1.5
- w_gate: bfloat16 [2048, 3072], P('seq', 'tp'), may hold values from -0.125 to 0.125
- w_up: bfloat16 [2048, 3072], P('seq', 'tp'), may hold values from -0.125 to 0.125
- w_down: bfloat16 [3072, 2048], P('tp', 'seq'), may hold values from -0.21875 to 0.21875
Outputs:
- hidden: bfloat16 [16384, 2048], P('seq')
- key_cache: bfloat16 [16384, 1024], P('seq', 'tp')
- value_cache: bfloat16 [16384, 1024], P('seq', 'tp')
The draws below stay inside these ranges and needn't reach their ends.
Inputs may be any that keep to these rules, and one draw needn't show every extreme that they name: `seg_ids`: prompt numbers never fall along the stream; each of the 8 prompts is a contiguous run of one or more tokens, and one prompt has exactly 13107 tokens. `positions`: each token's place in its prompt, counting from 0 at the prompt's first token. `query_gain`: positive gains. `key_gain`: positive gains.
All inputs are finite; a program needn't handle non-finite values.
Results may differ from the reference program's by a relative error of at most 0.02.
Values may be sent and summed in bfloat16 or wider, within the bound.
A program may use at most 128 MiB of HBM per device.

```python
import math
import jax
import jax.numpy as jnp
from jax import lax

MODEL_WIDTH = 2048
QUERY_HEADS = 16
KEY_VALUE_HEADS = 8
HEAD_DIM = 128
FF = 3072
SEGS = 8
PACKED_TOKENS = 16384
LEN_MAX = 13107


def tied_pair(key):
    query_slice = jax.random.normal(jax.random.fold_in(key, 101), (MODEL_WIDTH, QUERY_HEADS * HEAD_DIM), jnp.float32) / math.sqrt(MODEL_WIDTH)
    key_slice = jax.random.normal(jax.random.fold_in(key, 102), (MODEL_WIDTH, KEY_VALUE_HEADS * HEAD_DIM), jnp.float32) / math.sqrt(MODEL_WIDTH)
    return (query_slice, key_slice)


def draw_w_query(key, part):
    return tied_pair(key)[0].astype(jnp.bfloat16)


def draw_key_weight(key, part):
    return tied_pair(key)[1].astype(jnp.bfloat16)


def head_gains(key, salt):
    picked = jax.random.uniform(jax.random.fold_in(key, salt), (HEAD_DIM,), jnp.float32)
    return 0.6 + 0.8 * picked


def draw_query_gain(key, part):
    return head_gains(key, 201)


def draw_key_gain(key, part):
    return head_gains(key, 202)


def layout(key):
    longest = jax.random.randint(jax.random.fold_in(key, 11), (), 0, SEGS)
    index = jnp.arange(SEGS, dtype=jnp.int32)
    weights = jax.random.randint(jax.random.fold_in(key, 12), (SEGS,), 1, 101)
    weights = jnp.where(index == longest, 0, weights)
    extra = PACKED_TOKENS - LEN_MAX - (SEGS - 1)
    share = extra * weights // jnp.sum(weights)
    leftover = extra - jnp.sum(share)
    first_other = jnp.where(longest == 0, 1, 0)
    share = share + jnp.where(index == first_other, leftover, 0)
    lengths = jnp.where(index == longest, LEN_MAX, 1 + share).astype(jnp.int32)
    ends = jnp.cumsum(lengths)
    starts = ends - lengths
    place = jnp.arange(PACKED_TOKENS, dtype=jnp.int32)
    segment = jnp.sum((place[:, None] >= ends[None, :]).astype(jnp.int32), axis=1)
    onehot = (segment[:, None] == index[None, :]).astype(jnp.int32)
    offset = place - jnp.sum(onehot * starts[None, :], axis=1)
    return (segment.astype(jnp.int32), offset.astype(jnp.int32))


def draw_seg_ids(key, part):
    return layout(key)[0]


def draw_positions(key, part):
    return layout(key)[1]


def levels(own_key, dims, cuts, least, high):
    def one(position, shards_of):
        heights = jax.random.uniform(jax.random.fold_in(jax.random.fold_in(own_key, 6), position), (shards_of,), jnp.float32, least / len(cuts), high / len(cuts))
        return jnp.repeat(jnp.exp(heights), dims[position] // shards_of).reshape((-1,) + (1,) * (len(dims) - position - 1))

    loudness = one(*cuts[0])
    for cut in cuts[1:]:
        loudness = loudness * one(*cut)
    return loudness


def normal_values(own_key, dims, deviation, most, cuts=(), kind=jnp.bfloat16):
    entries = jax.random.normal(own_key, dims, jnp.float32) * deviation
    if len(cuts) > 0:
        entries = levels(own_key, dims, cuts, -0.22, 0.18) * entries
    return jnp.clip(entries, min=-most, max=most).astype(kind)


def setup_inputs(seed: int = 0) -> dict:
    splits = jax.random.split(jax.random.key(seed), 15)
    return {
        "layer_input": normal_values(splits[0], (PACKED_TOKENS, MODEL_WIDTH), 0.25, 1.5, ((0, 64),)),
        "norm_gain": jnp.clip(1.0 + 0.1 * jax.random.normal(splits[1], (MODEL_WIDTH,), jnp.float32), 0.5, 1.5),
        "w_query": draw_w_query(jax.random.fold_in(splits[14], 71), 0),
        "key_weight": draw_key_weight(jax.random.fold_in(splits[14], 71), 0),
        "value_weight": normal_values(splits[4], (MODEL_WIDTH, KEY_VALUE_HEADS * HEAD_DIM), MODEL_WIDTH ** -0.5, 0.125, ((1, 4),)),
        "w_out": normal_values(splits[5], (QUERY_HEADS * HEAD_DIM, MODEL_WIDTH), (HEAD_DIM // 4) ** -0.5, 1.0, ((0, 4),)),
        "query_gain": draw_query_gain(jax.random.fold_in(splits[14], 71), 0),
        "key_gain": draw_key_gain(jax.random.fold_in(splits[14], 71), 0),
        "seg_ids": draw_seg_ids(jax.random.fold_in(splits[14], 71), 0),
        "positions": draw_positions(jax.random.fold_in(splits[14], 71), 0),
        "post_gain": jnp.clip(1.0 + 0.1 * jax.random.normal(splits[10], (MODEL_WIDTH,), jnp.float32), 0.5, 1.5),
        "w_gate": normal_values(splits[11], (MODEL_WIDTH, FF), MODEL_WIDTH ** -0.5, 0.125, ((0, 64), (1, 4))),
        "w_up": normal_values(splits[12], (MODEL_WIDTH, FF), MODEL_WIDTH ** -0.5, 0.125, ((0, 64), (1, 4))),
        "w_down": normal_values(splits[13], (FF, MODEL_WIDTH), (FF // 4) ** -0.5, 0.21875, ((0, 4), (1, 64))),
    }


def rms(v, gain):
    return v * lax.rsqrt(lax.optimization_barrier(jnp.mean(v * v, axis=-1, keepdims=True)) + 1e-06) * gain

def rope(v, place):
    half = v.shape[-1] // 2
    freqs = 1000000.0 ** (-2.0 * jnp.arange(half, dtype=jnp.float32) / v.shape[-1])
    angle = place.astype(jnp.float32)[:, None] * freqs[None, :]
    cosine = jnp.cos(angle)[:, None, :]
    sine = jnp.sin(angle)[:, None, :]
    block_start = v[..., :half]
    second = v[..., half:]
    return jnp.concatenate([block_start * cosine - second * sine, second * cosine + block_start * sine], axis=-1)

def reference(layer_input, norm_gain, w_query, key_weight, value_weight, w_out, query_gain, key_gain, seg_ids, positions, post_gain, w_gate, w_up, w_down):
    xf = layer_input.astype(jnp.float32)
    normed_input = rms(xf, norm_gain).astype(jnp.bfloat16)
    query_matrix = jnp.dot(normed_input, w_query, preferred_element_type=jnp.float32).reshape(PACKED_TOKENS, QUERY_HEADS, HEAD_DIM)
    query_matrix = rope(rms(query_matrix, query_gain), positions).astype(jnp.bfloat16)
    key_matrix = jnp.dot(normed_input, key_weight, preferred_element_type=jnp.float32).reshape(PACKED_TOKENS, KEY_VALUE_HEADS, HEAD_DIM)
    key_matrix = rope(rms(key_matrix, key_gain), positions).astype(jnp.bfloat16)
    value_matrix = jnp.dot(normed_input, value_weight, preferred_element_type=jnp.float32).astype(jnp.bfloat16)
    key_heads = key_matrix.transpose(1, 0, 2)
    heads_of_value = value_matrix.reshape(PACKED_TOKENS, KEY_VALUE_HEADS, HEAD_DIM).transpose(1, 0, 2)
    head_group = QUERY_HEADS // KEY_VALUE_HEADS
    scale = 1.0 / math.sqrt(HEAD_DIM)
    token_block = math.gcd(PACKED_TOKENS, 512)
    outputs = []
    for block_start in range(0, PACKED_TOKENS, token_block):
        block_end = block_start + token_block
        block_queries = query_matrix[block_start:block_end].reshape(token_block, KEY_VALUE_HEADS, head_group, HEAD_DIM).transpose(1, 0, 2, 3)
        allowed = (seg_ids[block_start:block_end][:, None] == seg_ids[:block_end][None, :]) & (positions[:block_end][None, :] <= positions[block_start:block_end][:, None])

        def one_head(items):
            qh, kh, vh = items
            s = jnp.einsum('qgd,kd->gqk', qh.astype(jnp.float32), kh.astype(jnp.float32)) * scale
            s = jnp.where(allowed[None], s, -1e+30)
            top = lax.optimization_barrier(jnp.max(s, axis=-1, keepdims=True))
            p = jnp.where(allowed[None], jnp.exp(s - top), 0.0)
            total = lax.optimization_barrier(jnp.sum(p, axis=-1, keepdims=True))
            pb = p.astype(jnp.bfloat16).astype(jnp.float32)
            return jnp.einsum('gqk,kd->qgd', pb, vh.astype(jnp.float32)) / total.transpose(1, 0, 2)
        heads = lax.map(one_head, (block_queries, key_heads[:, :block_end], heads_of_value[:, :block_end]))
        outputs.append(heads.transpose(1, 0, 2, 3).reshape(token_block, QUERY_HEADS * HEAD_DIM))
    attended = jnp.concatenate(outputs, axis=0).astype(jnp.bfloat16)
    mid = (xf + jnp.dot(attended, w_out, preferred_element_type=jnp.float32)).astype(jnp.bfloat16)
    mid_f = mid.astype(jnp.float32)
    post_normed = rms(mid_f, post_gain).astype(jnp.bfloat16)
    gate = jnp.dot(post_normed, w_gate, preferred_element_type=jnp.float32)
    up = jnp.dot(post_normed, w_up, preferred_element_type=jnp.float32)
    act = (jax.nn.silu(gate) * up).astype(jnp.bfloat16)
    hidden = (mid_f + jnp.dot(act, w_down, preferred_element_type=jnp.float32)).astype(jnp.bfloat16)
    return (hidden, key_matrix.reshape(PACKED_TOKENS, KEY_VALUE_HEADS * HEAD_DIM), value_matrix)
```

```python
import math

import jax
import jax.numpy as jnp
from jax import lax
from jax.sharding import PartitionSpec as P


def rms(v, gain):
    return v * lax.rsqrt(jnp.mean(v * v, axis=-1, keepdims=True) + 1e-06) * gain


def rope(v, place):
    half = v.shape[-1] // 2
    freqs = 1000000.0 ** (-2.0 * jnp.arange(half, dtype=jnp.float32) / v.shape[-1])
    angle = place.astype(jnp.float32)[:, None] * freqs[None, :]
    cosine = jnp.cos(angle)[:, None, :]
    sine = jnp.sin(angle)[:, None, :]
    block_start = v[..., :half]
    second = v[..., half:]
    return jnp.concatenate(
        [block_start * cosine - second * sine, second * cosine + block_start * sine], axis=-1
    )


def body(
    layer_input,
    norm_gain,
    w_query,
    key_weight,
    value_weight,
    w_out,
    query_gain,
    key_gain,
    seg_ids,
    positions,
    post_gain,
    w_gate,
    w_up,
    w_down,
):
    rows = layer_input.shape[0]
    head_size = query_gain.shape[0]
    query_local = w_query.shape[1] // head_size
    kv_local = key_weight.shape[1] // head_size
    kv_cols = kv_local * head_size
    head_group = query_local // kv_local
    scale = 1.0 / math.sqrt(head_size)
    shards = lax.axis_size("seq")
    xf = layer_input.astype(jnp.float32)
    normed_input = rms(xf, norm_gain).astype(jnp.bfloat16)
    query_matrix = jnp.dot(normed_input, w_query, preferred_element_type=jnp.float32).reshape(
        rows, query_local, head_size
    )
    query_matrix = rope(rms(query_matrix, query_gain), positions).astype(jnp.bfloat16)
    key_matrix = jnp.dot(normed_input, key_weight, preferred_element_type=jnp.float32).reshape(
        rows, kv_local, head_size
    )
    key_matrix = rope(rms(key_matrix, key_gain), positions).astype(jnp.bfloat16)
    key_cache = key_matrix.reshape(rows, kv_cols)
    value_cache = jnp.dot(normed_input, value_weight, preferred_element_type=jnp.float32).astype(
        jnp.bfloat16
    )

    width_all = 2 * kv_cols
    ff_rows, ff_local = w_gate.shape
    w_rows = ff_rows * ff_local // width_all
    packed = jnp.concatenate(
        [
            jnp.concatenate([key_cache, value_cache], axis=1),
            w_gate.reshape(w_rows, width_all),
            w_up.reshape(w_rows, width_all),
            w_down.T.reshape(w_rows, width_all),
        ],
        axis=0,
    )
    gathered = lax.all_gather(packed, "seq", axis=0, tiled=False)
    kv_rows = gathered[:, :rows].reshape(shards * rows, width_all)
    key_rows = kv_rows[:, :kv_cols]
    value_rows = kv_rows[:, kv_cols:]

    def weight_part(k):
        lo = rows + k * w_rows
        return gathered[:, lo : lo + w_rows].reshape(shards * ff_rows, ff_local)

    gate_w = weight_part(0)
    up_w = weight_part(1)
    down_wt = weight_part(2)

    grouped = query_matrix.reshape(rows, kv_local, head_group, head_size).transpose(1, 2, 0, 3)
    me = lax.axis_index("seq")
    first = me * rows
    my_last = first + rows - 1
    q_index = first + jnp.arange(rows, dtype=jnp.int32)
    q_start = q_index - positions
    my_start = q_start[0]

    def update(state, key_blk, value_blk, k_index):
        top, total, acc = state
        count = key_blk.shape[0]
        s = (
            jnp.einsum(
                "hgqd,khd->hgqk",
                grouped,
                key_blk.reshape(count, kv_local, head_size),
                preferred_element_type=jnp.float32,
            )
            * scale
        )
        allowed = (k_index[None, :] <= q_index[:, None]) & (k_index[None, :] >= q_start[:, None])
        s = jnp.where(allowed, s, -1e30)
        new_top = jnp.maximum(top, jnp.max(s, axis=-1))
        p = jnp.where(allowed, jnp.exp(s - new_top[..., None]), 0.0)
        decay = jnp.exp(top - new_top)
        total = total * decay + jnp.sum(p, axis=-1)
        acc = acc * decay[..., None] + jnp.einsum(
            "hgqk,khd->hgqd",
            p.astype(jnp.bfloat16),
            value_blk.reshape(count, kv_local, head_size),
            preferred_element_type=jnp.float32,
        )
        return (new_top, total, acc)

    start_state = (
        jnp.full((kv_local, head_group, rows), -1e30, jnp.float32),
        jnp.zeros((kv_local, head_group, rows), jnp.float32),
        jnp.zeros((kv_local, head_group, rows, head_size), jnp.float32),
    )
    count = key_rows.shape[0]
    limit = max(1, 1024 // rows)
    factor = 1
    for trial in range(1, limit + 1):
        if shards % trial == 0:
            factor = trial
    width = rows * factor

    def one_block(step, inner):
        offset = step * width
        kb = lax.dynamic_slice_in_dim(key_rows, offset, width, 0)
        vb = lax.dynamic_slice_in_dim(value_rows, offset, width, 0)
        k_index = offset + jnp.arange(width, dtype=jnp.int32)
        skip = (offset > my_last) | (offset + width - 1 < my_start)
        return lax.cond(skip, lambda c: c, lambda c: update(c, kb, vb, k_index), inner)

    top, total, acc = lax.fori_loop(0, count // width, one_block, start_state)
    attended = (acc / total[..., None]).astype(jnp.bfloat16)
    attended = attended.transpose(2, 0, 1, 3).reshape(rows, query_local * head_size)
    partial_out = jnp.dot(attended, w_out, preferred_element_type=jnp.float32)
    summed = lax.psum(partial_out.astype(jnp.bfloat16), "tp").astype(jnp.float32)
    mid = (xf + summed).astype(jnp.bfloat16)
    mid_f = mid.astype(jnp.float32)
    post_normed = rms(mid_f, post_gain).astype(jnp.bfloat16)
    gate = jnp.dot(post_normed, gate_w, preferred_element_type=jnp.float32)
    up = jnp.dot(post_normed, up_w, preferred_element_type=jnp.float32)
    act = (jax.nn.silu(gate) * up).astype(jnp.bfloat16)
    terms = lax.dot_general(
        act, down_wt, (((1,), (1,)), ((), ())), preferred_element_type=jnp.float32
    )
    ffn_total = lax.psum(terms.astype(jnp.bfloat16), "tp").astype(jnp.float32)
    hidden = (mid_f + ffn_total).astype(jnp.bfloat16)
    return (hidden, key_cache, value_cache)


def solution(mesh):
    in_specs = (
        P("seq", None),
        P(),
        P(None, "tp"),
        P(None, "tp"),
        P(None, "tp"),
        P("tp", None),
        P(),
        P(),
        P("seq"),
        P("seq"),
        P(),
        P("seq", "tp"),
        P("seq", "tp"),
        P("tp", "seq"),
    )
    out_specs = (P("seq", None), P("seq", "tp"), P("seq", "tp"))
    return jax.shard_map(body, mesh=mesh, in_specs=in_specs, out_specs=out_specs, check_vma=False)
```

```python
import functools
import math

import jax
import jax.numpy as jnp
from jax import lax
from jax.experimental import pallas as pl
from jax.experimental.pallas import tpu as pltpu
from jax.sharding import PartitionSpec as P

MESH = pl.DeviceIdType.MESH


def rms(v, gain):
    return v * lax.rsqrt(jnp.mean(v * v, axis=-1, keepdims=True) + 1e-06) * gain


def rope(v, place):
    half = v.shape[-1] // 2
    freqs = 1000000.0 ** (-2.0 * jnp.arange(half, dtype=jnp.float32) / v.shape[-1])
    angle = place.astype(jnp.float32)[:, None] * freqs[None, :]
    cosine = jnp.cos(angle)[:, None, :]
    sine = jnp.sin(angle)[:, None, :]
    block_start = v[..., :half]
    second = v[..., half:]
    return jnp.concatenate(
        [block_start * cosine - second * sine, second * cosine + block_start * sine], axis=-1
    )


def tp_sum_kernel(n, x_ref, out_ref, slots, reduced, send1, recv1, send2, recv2):
    me = lax.axis_index("tp")
    row = lax.axis_index("seq")
    cols = x_ref.shape[1] // n

    barrier = pltpu.get_barrier_semaphore()
    for k in range(1, n):
        pl.semaphore_signal(barrier, inc=1, device_id=(row, lax.rem(me + k, n)), device_id_type=MESH)
    pl.semaphore_wait(barrier, n - 1)

    def block(ref, owner):
        return ref.at[:, pl.ds(pl.multiple_of(owner * cols, cols), cols)]

    first = []
    for k in range(1, n):
        peer = lax.rem(me + k, n)
        copy = pltpu.make_async_remote_copy(
            src_ref=block(x_ref, peer),
            dst_ref=slots.at[k],
            send_sem=send1.at[k],
            recv_sem=recv1.at[k],
            device_id=(row, peer),
            device_id_type=MESH,
        )
        copy.start()
        first.append(copy)
    for copy in first:
        copy.wait()
    total = block(x_ref, me)[...].astype(jnp.float32)
    for k in range(1, n):
        total = total + slots[k].astype(jnp.float32)
    reduced[...] = total.astype(reduced.dtype)
    block(out_ref, me)[...] = reduced[...]

    second = []
    for k in range(1, n):
        peer = lax.rem(me + k, n)
        copy = pltpu.make_async_remote_copy(
            src_ref=reduced,
            dst_ref=block(out_ref, me),
            send_sem=send2.at[k],
            recv_sem=recv2.at[k],
            device_id=(row, peer),
            device_id_type=MESH,
        )
        copy.start()
        second.append(copy)
    for copy in second:
        copy.wait()


def tp_sum(x, collective_id):
    n = lax.axis_size("tp")
    rows, width = x.shape
    cols = width // n
    return pl.pallas_call(
        functools.partial(tp_sum_kernel, n),
        out_shape=jax.ShapeDtypeStruct((rows, width), x.dtype),
        in_specs=[pl.BlockSpec(memory_space=pltpu.VMEM)],
        out_specs=pl.BlockSpec(memory_space=pltpu.VMEM),
        scratch_shapes=[
            pltpu.VMEM((n, rows, cols), x.dtype),
            pltpu.VMEM((rows, cols), x.dtype),
            pltpu.SemaphoreType.DMA((n,)),
            pltpu.SemaphoreType.DMA((n,)),
            pltpu.SemaphoreType.DMA((n,)),
            pltpu.SemaphoreType.DMA((n,)),
        ],
        compiler_params=pltpu.CompilerParams(collective_id=collective_id, has_side_effects=True),
    )(x)


def body(
    layer_input,
    norm_gain,
    w_query,
    key_weight,
    value_weight,
    w_out,
    query_gain,
    key_gain,
    seg_ids,
    positions,
    post_gain,
    w_gate,
    w_up,
    w_down,
):
    rows = layer_input.shape[0]
    head_size = query_gain.shape[0]
    query_local = w_query.shape[1] // head_size
    kv_local = key_weight.shape[1] // head_size
    kv_cols = kv_local * head_size
    head_group = query_local // kv_local
    scale = 1.0 / math.sqrt(head_size)
    shards = lax.axis_size("seq")
    xf = layer_input.astype(jnp.float32)
    normed_input = rms(xf, norm_gain).astype(jnp.bfloat16)
    query_matrix = jnp.dot(normed_input, w_query, preferred_element_type=jnp.float32).reshape(
        rows, query_local, head_size
    )
    query_matrix = rope(rms(query_matrix, query_gain), positions).astype(jnp.bfloat16)
    key_matrix = jnp.dot(normed_input, key_weight, preferred_element_type=jnp.float32).reshape(
        rows, kv_local, head_size
    )
    key_matrix = rope(rms(key_matrix, key_gain), positions).astype(jnp.bfloat16)
    key_cache = key_matrix.reshape(rows, kv_cols)
    value_cache = jnp.dot(normed_input, value_weight, preferred_element_type=jnp.float32).astype(
        jnp.bfloat16
    )

    width_all = 2 * kv_cols
    ff_rows, ff_local = w_gate.shape
    w_rows = ff_rows * ff_local // width_all
    packed = jnp.concatenate(
        [
            jnp.concatenate([key_cache, value_cache], axis=1),
            w_gate.reshape(w_rows, width_all),
            w_up.reshape(w_rows, width_all),
            w_down.T.reshape(w_rows, width_all),
        ],
        axis=0,
    )
    gathered = lax.all_gather(packed, "seq", axis=0, tiled=False)
    kv_rows = gathered[:, :rows].reshape(shards * rows, width_all)
    key_rows = kv_rows[:, :kv_cols]
    value_rows = kv_rows[:, kv_cols:]

    def weight_part(k):
        lo = rows + k * w_rows
        return gathered[:, lo : lo + w_rows].reshape(shards * ff_rows, ff_local)

    gate_w = weight_part(0)
    up_w = weight_part(1)
    down_wt = weight_part(2)

    grouped = query_matrix.reshape(rows, kv_local, head_group, head_size).transpose(1, 2, 0, 3)
    me = lax.axis_index("seq")
    first = me * rows
    my_last = first + rows - 1
    q_index = first + jnp.arange(rows, dtype=jnp.int32)
    q_start = q_index - positions
    my_start = q_start[0]

    def update(state, key_blk, value_blk, k_index):
        top, total, acc = state
        count = key_blk.shape[0]
        s = (
            jnp.einsum(
                "hgqd,khd->hgqk",
                grouped,
                key_blk.reshape(count, kv_local, head_size),
                preferred_element_type=jnp.float32,
            )
            * scale
        )
        allowed = (k_index[None, :] <= q_index[:, None]) & (k_index[None, :] >= q_start[:, None])
        s = jnp.where(allowed, s, -1e30)
        new_top = jnp.maximum(top, jnp.max(s, axis=-1))
        p = jnp.where(allowed, jnp.exp(s - new_top[..., None]), 0.0)
        decay = jnp.exp(top - new_top)
        total = total * decay + jnp.sum(p, axis=-1)
        acc = acc * decay[..., None] + jnp.einsum(
            "hgqk,khd->hgqd",
            p.astype(jnp.bfloat16),
            value_blk.reshape(count, kv_local, head_size),
            preferred_element_type=jnp.float32,
        )
        return (new_top, total, acc)

    start_state = (
        jnp.full((kv_local, head_group, rows), -1e30, jnp.float32),
        jnp.zeros((kv_local, head_group, rows), jnp.float32),
        jnp.zeros((kv_local, head_group, rows, head_size), jnp.float32),
    )
    count = key_rows.shape[0]
    limit = max(1, 1024 // rows)
    factor = 1
    for trial in range(1, limit + 1):
        if shards % trial == 0:
            factor = trial
    width = rows * factor

    def one_block(step, inner):
        offset = step * width
        kb = lax.dynamic_slice_in_dim(key_rows, offset, width, 0)
        vb = lax.dynamic_slice_in_dim(value_rows, offset, width, 0)
        k_index = offset + jnp.arange(width, dtype=jnp.int32)
        skip = (offset > my_last) | (offset + width - 1 < my_start)
        return lax.cond(skip, lambda c: c, lambda c: update(c, kb, vb, k_index), inner)

    top, total, acc = lax.fori_loop(0, count // width, one_block, start_state)
    attended = (acc / total[..., None]).astype(jnp.bfloat16)
    attended = attended.transpose(2, 0, 1, 3).reshape(rows, query_local * head_size)
    partial_out = jnp.dot(attended, w_out, preferred_element_type=jnp.float32)
    summed = tp_sum(partial_out.astype(jnp.bfloat16), 0).astype(jnp.float32)
    mid = (xf + summed).astype(jnp.bfloat16)
    mid_f = mid.astype(jnp.float32)
    post_normed = rms(mid_f, post_gain).astype(jnp.bfloat16)
    gate = jnp.dot(post_normed, gate_w, preferred_element_type=jnp.float32)
    up = jnp.dot(post_normed, up_w, preferred_element_type=jnp.float32)
    act = (jax.nn.silu(gate) * up).astype(jnp.bfloat16)
    terms = lax.dot_general(
        act, down_wt, (((1,), (1,)), ((), ())), preferred_element_type=jnp.float32
    )
    ffn_total = tp_sum(terms.astype(jnp.bfloat16), 1).astype(jnp.float32)
    hidden = (mid_f + ffn_total).astype(jnp.bfloat16)
    return (hidden, key_cache, value_cache)


def solution(mesh):
    in_specs = (
        P("seq", None),
        P(),
        P(None, "tp"),
        P(None, "tp"),
        P(None, "tp"),
        P("tp", None),
        P(),
        P(),
        P("seq"),
        P("seq"),
        P(),
        P("seq", "tp"),
        P("seq", "tp"),
        P("tp", "seq"),
    )
    out_specs = (P("seq", None), P("seq", "tp"), P("seq", "tp"))
    return jax.shard_map(body, mesh=mesh, in_specs=in_specs, out_specs=out_specs, check_vma=False)
```

```python
import functools
import math

import jax
import jax.numpy as jnp
from jax import lax
from jax.experimental import pallas as pl
from jax.experimental.pallas import tpu as pltpu
from jax.sharding import PartitionSpec as P

MESH = pl.DeviceIdType.MESH


def rms(v, gain):
    return v * lax.rsqrt(jnp.mean(v * v, axis=-1, keepdims=True) + 1e-06) * gain


def rope(v, place):
    half = v.shape[-1] // 2
    freqs = 1000000.0 ** (-2.0 * jnp.arange(half, dtype=jnp.float32) / v.shape[-1])
    angle = place.astype(jnp.float32)[:, None] * freqs[None, :]
    cosine = jnp.cos(angle)[:, None, :]
    sine = jnp.sin(angle)[:, None, :]
    block_start = v[..., :half]
    second = v[..., half:]
    return jnp.concatenate(
        [block_start * cosine - second * sine, second * cosine + block_start * sine], axis=-1
    )


def tp_sum_kernel(n, x_ref, out_ref, slots, reduced, send1, recv1, send2, recv2):
    me = lax.axis_index("tp")
    row = lax.axis_index("seq")
    cols = x_ref.shape[1] // n

    barrier = pltpu.get_barrier_semaphore()
    for k in range(1, n):
        pl.semaphore_signal(barrier, inc=1, device_id=(row, lax.rem(me + k, n)), device_id_type=MESH)
    pl.semaphore_wait(barrier, n - 1)

    def block(ref, owner):
        return ref.at[:, pl.ds(pl.multiple_of(owner * cols, cols), cols)]

    first = []
    for k in range(1, n):
        peer = lax.rem(me + k, n)
        copy = pltpu.make_async_remote_copy(
            src_ref=block(x_ref, peer),
            dst_ref=slots.at[k],
            send_sem=send1.at[k],
            recv_sem=recv1.at[k],
            device_id=(row, peer),
            device_id_type=MESH,
        )
        copy.start()
        first.append(copy)
    for copy in first:
        copy.wait()
    total = block(x_ref, me)[...].astype(jnp.float32)
    for k in range(1, n):
        total = total + slots[k].astype(jnp.float32)
    reduced[...] = total.astype(reduced.dtype)
    block(out_ref, me)[...] = reduced[...]

    second = []
    for k in range(1, n):
        peer = lax.rem(me + k, n)
        copy = pltpu.make_async_remote_copy(
            src_ref=reduced,
            dst_ref=block(out_ref, me),
            send_sem=send2.at[k],
            recv_sem=recv2.at[k],
            device_id=(row, peer),
            device_id_type=MESH,
        )
        copy.start()
        second.append(copy)
    for copy in second:
        copy.wait()


def tp_sum(x, collective_id):
    n = lax.axis_size("tp")
    rows, width = x.shape
    cols = width // n
    return pl.pallas_call(
        functools.partial(tp_sum_kernel, n),
        out_shape=jax.ShapeDtypeStruct((rows, width), x.dtype),
        in_specs=[pl.BlockSpec(memory_space=pltpu.VMEM)],
        out_specs=pl.BlockSpec(memory_space=pltpu.VMEM),
        scratch_shapes=[
            pltpu.VMEM((n, rows, cols), x.dtype),
            pltpu.VMEM((rows, cols), x.dtype),
            pltpu.SemaphoreType.DMA((n,)),
            pltpu.SemaphoreType.DMA((n,)),
            pltpu.SemaphoreType.DMA((n,)),
            pltpu.SemaphoreType.DMA((n,)),
        ],
        compiler_params=pltpu.CompilerParams(collective_id=collective_id, has_side_effects=True),
    )(x)


def attention_kernel(info, q_ref, q_last_ref, q_first_ref, kv_ref, o_ref, top_ref, total_ref, acc_ref):
    step = pl.program_id(0)
    groups, rows_all, head_size = q_ref.shape
    shards_per, rows, _ = kv_ref.shape
    width = shards_per * rows
    half = kv_ref.shape[2] // 2
    rows_q = o_ref.shape[0]
    per_group = rows_all // rows_q
    scale = 1.0 / math.sqrt(head_size)

    @pl.when(step == 0)
    def _():
        top_ref[...] = jnp.full(top_ref.shape, -1e30, jnp.float32)
        total_ref[...] = jnp.zeros(total_ref.shape, jnp.float32)
        acc_ref[...] = jnp.zeros(acc_ref.shape, jnp.float32)

    offset = step * width
    needed = (step >= info[0]) & (step <= info[1])
    whole = (offset >= info[2]) & (offset + width - 1 <= info[3])

    def run(masked):
        for g in range(groups):
            q = q_ref[g]
            k = kv_ref[:, :, g * head_size : (g + 1) * head_size].reshape(width, head_size)
            v = kv_ref[:, :, half + g * head_size : half + (g + 1) * head_size].reshape(width, head_size)
            s = lax.dot_general(q, k, (((1,), (1,)), ((), ())), preferred_element_type=jnp.float32) * scale
            if masked:
                k_index = offset + lax.broadcasted_iota(jnp.int32, s.shape, 1)
                allowed = (k_index <= q_last_ref[...]) & (k_index >= q_first_ref[...])
                s = jnp.where(allowed, s, -1e30)
            top = top_ref[g]
            new_top = jnp.maximum(top, jnp.max(s, axis=-1, keepdims=True))
            p = jnp.exp(s - new_top)
            if masked:
                p = jnp.where(allowed, p, 0.0)
            decay = jnp.exp(top - new_top)
            total_ref[g] = total_ref[g] * decay + jnp.sum(p, axis=-1, keepdims=True)
            acc_ref[g] = acc_ref[g] * decay + jnp.dot(
                p.astype(jnp.bfloat16), v, preferred_element_type=jnp.float32
            )
            top_ref[g] = new_top

    @pl.when(needed & whole)
    def _():
        run(False)

    @pl.when(needed & jnp.logical_not(whole))
    def _():
        run(True)

    @pl.when(step == pl.num_programs(0) - 1)
    def _():
        for g in range(groups):
            out = acc_ref[g] / total_ref[g]
            for h in range(per_group):
                col = (g * per_group + h) * head_size
                o_ref[:, col : col + head_size] = out[h * rows_q : (h + 1) * rows_q].astype(o_ref.dtype)


def attention(q_grouped, q_last, q_first, gathered, info, rows, kv_rows_per_shard, shards_per):
    groups, rows_all, head_size = q_grouped.shape
    shards, _, width_all = gathered.shape
    blocks = shards // shards_per
    out_cols = rows_all // rows * groups * head_size

    def kv_map(j, info):
        return (jnp.minimum(jnp.maximum(j, info[0]), info[1]), 0, 0)

    grid_spec = pltpu.PrefetchScalarGridSpec(
        num_scalar_prefetch=1,
        grid=(blocks,),
        in_specs=[
            pl.BlockSpec((groups, rows_all, head_size), lambda j, info: (0, 0, 0)),
            pl.BlockSpec((rows_all, 1), lambda j, info: (0, 0)),
            pl.BlockSpec((rows_all, 1), lambda j, info: (0, 0)),
            pl.BlockSpec((shards_per, kv_rows_per_shard, width_all), kv_map),
        ],
        out_specs=pl.BlockSpec((rows, out_cols), lambda j, info: (0, 0)),
        scratch_shapes=[
            pltpu.VMEM((groups, rows_all, 1), jnp.float32),
            pltpu.VMEM((groups, rows_all, 1), jnp.float32),
            pltpu.VMEM((groups, rows_all, head_size), jnp.float32),
        ],
    )
    return pl.pallas_call(
        attention_kernel,
        out_shape=jax.ShapeDtypeStruct((rows, out_cols), jnp.bfloat16),
        grid_spec=grid_spec,
        compiler_params=pltpu.CompilerParams(dimension_semantics=("arbitrary",)),
    )(info, q_grouped, q_last, q_first, gathered)


def body(
    layer_input,
    norm_gain,
    w_query,
    key_weight,
    value_weight,
    w_out,
    query_gain,
    key_gain,
    seg_ids,
    positions,
    post_gain,
    w_gate,
    w_up,
    w_down,
):
    rows = layer_input.shape[0]
    head_size = query_gain.shape[0]
    query_local = w_query.shape[1] // head_size
    kv_local = key_weight.shape[1] // head_size
    kv_cols = kv_local * head_size
    head_group = query_local // kv_local
    scale = 1.0 / math.sqrt(head_size)
    shards = lax.axis_size("seq")
    xf = layer_input.astype(jnp.float32)
    normed_input = rms(xf, norm_gain).astype(jnp.bfloat16)
    query_matrix = jnp.dot(normed_input, w_query, preferred_element_type=jnp.float32).reshape(
        rows, query_local, head_size
    )
    query_matrix = rope(rms(query_matrix, query_gain), positions).astype(jnp.bfloat16)
    key_matrix = jnp.dot(normed_input, key_weight, preferred_element_type=jnp.float32).reshape(
        rows, kv_local, head_size
    )
    key_matrix = rope(rms(key_matrix, key_gain), positions).astype(jnp.bfloat16)
    key_cache = key_matrix.reshape(rows, kv_cols)
    value_cache = jnp.dot(normed_input, value_weight, preferred_element_type=jnp.float32).astype(
        jnp.bfloat16
    )

    width_all = 2 * kv_cols
    ff_rows, ff_local = w_gate.shape
    w_rows = ff_rows * ff_local // width_all
    packed = jnp.concatenate(
        [
            jnp.concatenate([key_cache, value_cache], axis=1),
            w_gate.reshape(w_rows, width_all),
            w_up.reshape(w_rows, width_all),
            w_down.T.reshape(w_rows, width_all),
        ],
        axis=0,
    )
    gathered = lax.all_gather(packed, "seq", axis=0, tiled=False)
    def weight_part(k):
        lo = rows + k * w_rows
        return gathered[:, lo : lo + w_rows].reshape(shards * ff_rows, ff_local)

    gate_w = weight_part(0)
    up_w = weight_part(1)
    down_wt = weight_part(2)

    me = lax.axis_index("seq")
    first = me * rows
    my_last = first + rows - 1
    q_index = first + jnp.arange(rows, dtype=jnp.int32)
    q_start = q_index - positions
    shards_per = 1
    for trial in range(1, max(1, 1024 // rows) + 1):
        if shards % trial == 0:
            shards_per = trial
    width = rows * shards_per
    info = jnp.stack([q_start[0] // width, my_last // width, q_start[rows - 1], first])
    q_grouped = (
        query_matrix.reshape(rows, kv_local, head_group, head_size)
        .transpose(1, 2, 0, 3)
        .reshape(kv_local, head_group * rows, head_size)
    )
    q_last = jnp.tile(q_index, head_group).reshape(head_group * rows, 1)
    q_first = jnp.tile(q_start, head_group).reshape(head_group * rows, 1)
    attended = attention(q_grouped, q_last, q_first, gathered, info, rows, rows, shards_per)
    partial_out = jnp.dot(attended, w_out, preferred_element_type=jnp.float32)
    summed = tp_sum(partial_out.astype(jnp.bfloat16), 0).astype(jnp.float32)
    mid = (xf + summed).astype(jnp.bfloat16)
    mid_f = mid.astype(jnp.float32)
    post_normed = rms(mid_f, post_gain).astype(jnp.bfloat16)
    gate = jnp.dot(post_normed, gate_w, preferred_element_type=jnp.float32)
    up = jnp.dot(post_normed, up_w, preferred_element_type=jnp.float32)
    act = (jax.nn.silu(gate) * up).astype(jnp.bfloat16)
    terms = lax.dot_general(
        act, down_wt, (((1,), (1,)), ((), ())), preferred_element_type=jnp.float32
    )
    ffn_total = tp_sum(terms.astype(jnp.bfloat16), 1).astype(jnp.float32)
    hidden = (mid_f + ffn_total).astype(jnp.bfloat16)
    return (hidden, key_cache, value_cache)


def solution(mesh):
    in_specs = (
        P("seq", None),
        P(),
        P(None, "tp"),
        P(None, "tp"),
        P(None, "tp"),
        P("tp", None),
        P(),
        P(),
        P("seq"),
        P("seq"),
        P(),
        P("seq", "tp"),
        P("seq", "tp"),
        P("tp", "seq"),
    )
    out_specs = (P("seq", None), P("seq", "tp"), P("seq", "tp"))
    return jax.shard_map(body, mesh=mesh, in_specs=in_specs, out_specs=out_specs, check_vma=False)
```

```python
import functools
import math

import jax
import jax.numpy as jnp
from jax import lax
from jax.experimental import pallas as pl
from jax.experimental.pallas import tpu as pltpu
from jax.sharding import PartitionSpec as P

MESH = pl.DeviceIdType.MESH


def rms(v, gain):
    return v * lax.rsqrt(jnp.mean(v * v, axis=-1, keepdims=True) + 1e-06) * gain


def rope(v, place):
    half = v.shape[-1] // 2
    freqs = 1000000.0 ** (-2.0 * jnp.arange(half, dtype=jnp.float32) / v.shape[-1])
    angle = place.astype(jnp.float32)[:, None] * freqs[None, :]
    cosine = jnp.cos(angle)[:, None, :]
    sine = jnp.sin(angle)[:, None, :]
    block_start = v[..., :half]
    second = v[..., half:]
    return jnp.concatenate(
        [block_start * cosine - second * sine, second * cosine + block_start * sine], axis=-1
    )


def tp_sum_kernel(n, x_ref, out_ref, slots, reduced, send1, recv1, send2, recv2):
    me = lax.axis_index("tp")
    row = lax.axis_index("seq")
    cols = x_ref.shape[1] // n

    barrier = pltpu.get_barrier_semaphore()
    for k in range(1, n):
        pl.semaphore_signal(barrier, inc=1, device_id=(row, lax.rem(me + k, n)), device_id_type=MESH)
    pl.semaphore_wait(barrier, n - 1)

    def block(ref, owner):
        return ref.at[:, pl.ds(pl.multiple_of(owner * cols, cols), cols)]

    first = []
    for k in range(1, n):
        peer = lax.rem(me + k, n)
        copy = pltpu.make_async_remote_copy(
            src_ref=block(x_ref, peer),
            dst_ref=slots.at[k],
            send_sem=send1.at[k],
            recv_sem=recv1.at[k],
            device_id=(row, peer),
            device_id_type=MESH,
        )
        copy.start()
        first.append(copy)
    for copy in first:
        copy.wait()
    total = block(x_ref, me)[...].astype(jnp.float32)
    for k in range(1, n):
        total = total + slots[k].astype(jnp.float32)
    reduced[...] = total.astype(reduced.dtype)
    block(out_ref, me)[...] = reduced[...]

    second = []
    for k in range(1, n):
        peer = lax.rem(me + k, n)
        copy = pltpu.make_async_remote_copy(
            src_ref=reduced,
            dst_ref=block(out_ref, me),
            send_sem=send2.at[k],
            recv_sem=recv2.at[k],
            device_id=(row, peer),
            device_id_type=MESH,
        )
        copy.start()
        second.append(copy)
    for copy in second:
        copy.wait()


def tp_sum(x, collective_id):
    n = lax.axis_size("tp")
    rows, width = x.shape
    cols = width // n
    return pl.pallas_call(
        functools.partial(tp_sum_kernel, n),
        out_shape=jax.ShapeDtypeStruct((rows, width), x.dtype),
        in_specs=[pl.BlockSpec(memory_space=pltpu.VMEM)],
        out_specs=pl.BlockSpec(memory_space=pltpu.VMEM),
        scratch_shapes=[
            pltpu.VMEM((n, rows, cols), x.dtype),
            pltpu.VMEM((rows, cols), x.dtype),
            pltpu.SemaphoreType.DMA((n,)),
            pltpu.SemaphoreType.DMA((n,)),
            pltpu.SemaphoreType.DMA((n,)),
            pltpu.SemaphoreType.DMA((n,)),
        ],
        compiler_params=pltpu.CompilerParams(collective_id=collective_id, has_side_effects=True),
    )(x)


def attention_kernel(info, q_ref, q_last_ref, q_first_ref, kv_ref, o_ref, top_ref, total_ref, acc_ref):
    step = pl.program_id(0)
    groups, rows_all, head_size = q_ref.shape
    shards_per, rows, _ = kv_ref.shape
    width = shards_per * rows
    half = kv_ref.shape[2] // 2
    rows_q = o_ref.shape[0]
    per_group = rows_all // rows_q
    scale = 1.0 / math.sqrt(head_size)

    @pl.when(step == 0)
    def _():
        top_ref[...] = jnp.full(top_ref.shape, -1e30, jnp.float32)
        total_ref[...] = jnp.zeros(total_ref.shape, jnp.float32)
        acc_ref[...] = jnp.zeros(acc_ref.shape, jnp.float32)

    offset = step * width
    needed = (step >= info[0]) & (step <= info[1])
    whole = (offset >= info[2]) & (offset + width - 1 <= info[3])

    def run(masked):
        for g in range(groups):
            q = q_ref[g]
            k = kv_ref[:, :, g * head_size : (g + 1) * head_size].reshape(width, head_size)
            v = kv_ref[:, :, half + g * head_size : half + (g + 1) * head_size].reshape(width, head_size)
            s = lax.dot_general(q, k, (((1,), (1,)), ((), ())), preferred_element_type=jnp.float32) * scale
            if masked:
                k_index = offset + lax.broadcasted_iota(jnp.int32, s.shape, 1)
                allowed = (k_index <= q_last_ref[...]) & (k_index >= q_first_ref[...])
                s = jnp.where(allowed, s, -1e30)
            top = top_ref[g]
            new_top = jnp.maximum(top, jnp.max(s, axis=-1, keepdims=True))
            p = jnp.exp(s - new_top)
            if masked:
                p = jnp.where(allowed, p, 0.0)
            decay = jnp.exp(top - new_top)
            total_ref[g] = total_ref[g] * decay + jnp.sum(p, axis=-1, keepdims=True)
            acc_ref[g] = acc_ref[g] * decay + jnp.dot(
                p.astype(jnp.bfloat16), v, preferred_element_type=jnp.float32
            )
            top_ref[g] = new_top

    @pl.when(needed & whole)
    def _():
        run(False)

    @pl.when(needed & jnp.logical_not(whole))
    def _():
        run(True)

    @pl.when(step == pl.num_programs(0) - 1)
    def _():
        for g in range(groups):
            out = acc_ref[g] / total_ref[g]
            for h in range(per_group):
                col = (g * per_group + h) * head_size
                o_ref[:, col : col + head_size] = out[h * rows_q : (h + 1) * rows_q].astype(o_ref.dtype)


def attention(q_grouped, q_last, q_first, gathered, info, rows, kv_rows_per_shard, shards_per):
    groups, rows_all, head_size = q_grouped.shape
    shards, _, width_all = gathered.shape
    blocks = shards // shards_per
    out_cols = rows_all // rows * groups * head_size

    def kv_map(j, info):
        return (jnp.minimum(jnp.maximum(j, info[0]), info[1]), 0, 0)

    grid_spec = pltpu.PrefetchScalarGridSpec(
        num_scalar_prefetch=1,
        grid=(blocks,),
        in_specs=[
            pl.BlockSpec((groups, rows_all, head_size), lambda j, info: (0, 0, 0)),
            pl.BlockSpec((rows_all, 1), lambda j, info: (0, 0)),
            pl.BlockSpec((rows_all, 1), lambda j, info: (0, 0)),
            pl.BlockSpec((shards_per, kv_rows_per_shard, width_all), kv_map),
        ],
        out_specs=pl.BlockSpec((rows, out_cols), lambda j, info: (0, 0)),
        scratch_shapes=[
            pltpu.VMEM((groups, rows_all, 1), jnp.float32),
            pltpu.VMEM((groups, rows_all, 1), jnp.float32),
            pltpu.VMEM((groups, rows_all, head_size), jnp.float32),
        ],
    )
    return pl.pallas_call(
        attention_kernel,
        out_shape=jax.ShapeDtypeStruct((rows, out_cols), jnp.bfloat16),
        grid_spec=grid_spec,
        compiler_params=pltpu.CompilerParams(dimension_semantics=("arbitrary",)),
    )(info, q_grouped, q_last, q_first, gathered)


def body(
    layer_input,
    norm_gain,
    w_query,
    key_weight,
    value_weight,
    w_out,
    query_gain,
    key_gain,
    seg_ids,
    positions,
    post_gain,
    w_gate,
    w_up,
    w_down,
):
    rows = layer_input.shape[0]
    head_size = query_gain.shape[0]
    query_local = w_query.shape[1] // head_size
    kv_local = key_weight.shape[1] // head_size
    kv_cols = kv_local * head_size
    head_group = query_local // kv_local
    scale = 1.0 / math.sqrt(head_size)
    shards = lax.axis_size("seq")
    xf = layer_input.astype(jnp.float32)
    normed_input = rms(xf, norm_gain).astype(jnp.bfloat16)
    query_matrix = jnp.dot(normed_input, w_query, preferred_element_type=jnp.float32).reshape(
        rows, query_local, head_size
    )
    query_matrix = rope(rms(query_matrix, query_gain), positions).astype(jnp.bfloat16)
    key_matrix = jnp.dot(normed_input, key_weight, preferred_element_type=jnp.float32).reshape(
        rows, kv_local, head_size
    )
    key_matrix = rope(rms(key_matrix, key_gain), positions).astype(jnp.bfloat16)
    key_cache = key_matrix.reshape(rows, kv_cols)
    value_cache = jnp.dot(normed_input, value_weight, preferred_element_type=jnp.float32).astype(
        jnp.bfloat16
    )

    width_all = 2 * kv_cols
    ff_rows, ff_local = w_gate.shape
    rest = ff_local - width_all
    down_t = w_down.T
    packed = jnp.concatenate(
        [
            jnp.concatenate([key_cache, value_cache], axis=1),
            w_gate[:, :width_all],
            w_up[:, :width_all],
            down_t[:, :width_all],
            jnp.concatenate([w_gate[:, width_all:], w_up[:, width_all:]], axis=1),
            jnp.concatenate(
                [down_t[:, width_all:], jnp.zeros((ff_rows, 2 * width_all - ff_local), down_t.dtype)],
                axis=1,
            ),
        ],
        axis=0,
    )
    gathered = lax.all_gather(packed, "seq", axis=0, tiled=False)

    def weight_part(k, lo, hi):
        top = rows + k * ff_rows
        return gathered[:, top : top + ff_rows, lo:hi].reshape(shards * ff_rows, hi - lo)

    gate_a = weight_part(0, 0, width_all)
    up_a = weight_part(1, 0, width_all)
    down_a = weight_part(2, 0, width_all)
    gate_b = weight_part(3, 0, rest)
    up_b = weight_part(3, rest, 2 * rest)
    down_b = weight_part(4, 0, rest)

    me = lax.axis_index("seq")
    first = me * rows
    my_last = first + rows - 1
    q_index = first + jnp.arange(rows, dtype=jnp.int32)
    q_start = q_index - positions
    shards_per = 1
    for trial in range(1, max(1, 1024 // rows) + 1):
        if shards % trial == 0:
            shards_per = trial
    width = rows * shards_per
    info = jnp.stack([q_start[0] // width, my_last // width, q_start[rows - 1], first])
    q_grouped = (
        query_matrix.reshape(rows, kv_local, head_group, head_size)
        .transpose(1, 2, 0, 3)
        .reshape(kv_local, head_group * rows, head_size)
    )
    q_last = jnp.tile(q_index, head_group).reshape(head_group * rows, 1)
    q_first = jnp.tile(q_start, head_group).reshape(head_group * rows, 1)
    attended = attention(q_grouped, q_last, q_first, gathered, info, rows, rows, shards_per)
    partial_out = jnp.dot(attended, w_out, preferred_element_type=jnp.float32)
    summed = tp_sum(partial_out.astype(jnp.bfloat16), 0).astype(jnp.float32)
    mid = (xf + summed).astype(jnp.bfloat16)
    mid_f = mid.astype(jnp.float32)
    post_normed = rms(mid_f, post_gain).astype(jnp.bfloat16)
    def ffn_piece(gate_w, up_w, down_w):
        gate = jnp.dot(post_normed, gate_w, preferred_element_type=jnp.float32)
        up = jnp.dot(post_normed, up_w, preferred_element_type=jnp.float32)
        act = (jax.nn.silu(gate) * up).astype(jnp.bfloat16)
        return lax.dot_general(
            act, down_w, (((1,), (1,)), ((), ())), preferred_element_type=jnp.float32
        )

    terms = ffn_piece(gate_a, up_a, down_a) + ffn_piece(gate_b, up_b, down_b)
    ffn_total = tp_sum(terms.astype(jnp.bfloat16), 1).astype(jnp.float32)
    hidden = (mid_f + ffn_total).astype(jnp.bfloat16)
    return (hidden, key_cache, value_cache)


def solution(mesh):
    in_specs = (
        P("seq", None),
        P(),
        P(None, "tp"),
        P(None, "tp"),
        P(None, "tp"),
        P("tp", None),
        P(),
        P(),
        P("seq"),
        P("seq"),
        P(),
        P("seq", "tp"),
        P("seq", "tp"),
        P("tp", "seq"),
    )
    out_specs = (P("seq", None), P("seq", "tp"), P("seq", "tp"))
    return jax.shard_map(body, mesh=mesh, in_specs=in_specs, out_specs=out_specs, check_vma=False)
```

```python
import functools
import math

import jax
import jax.numpy as jnp
from jax import lax
from jax.experimental import pallas as pl
from jax.experimental.pallas import tpu as pltpu
from jax.sharding import PartitionSpec as P

MESH = pl.DeviceIdType.MESH


def rms(v, gain):
    return v * lax.rsqrt(jnp.mean(v * v, axis=-1, keepdims=True) + 1e-06) * gain


def rope(v, place):
    half = v.shape[-1] // 2
    freqs = 1000000.0 ** (-2.0 * jnp.arange(half, dtype=jnp.float32) / v.shape[-1])
    angle = place.astype(jnp.float32)[:, None] * freqs[None, :]
    cosine = jnp.cos(angle)[:, None, :]
    sine = jnp.sin(angle)[:, None, :]
    block_start = v[..., :half]
    second = v[..., half:]
    return jnp.concatenate(
        [block_start * cosine - second * sine, second * cosine + block_start * sine], axis=-1
    )


def tp_sum_kernel(n, x_ref, out_ref, slots, reduced, send1, recv1, send2, recv2):
    me = lax.axis_index("tp")
    chip = lax.axis_index("chip")
    core = lax.axis_index("core")
    cols = x_ref.shape[1] // n

    barrier = pltpu.get_barrier_semaphore()
    for k in range(1, n):
        pl.semaphore_signal(barrier, inc=1, device_id=(chip, core, lax.rem(me + k, n)), device_id_type=MESH)
    pl.semaphore_wait(barrier, n - 1)

    def block(ref, owner):
        return ref.at[:, pl.ds(pl.multiple_of(owner * cols, cols), cols)]

    first = []
    for k in range(1, n):
        peer = lax.rem(me + k, n)
        copy = pltpu.make_async_remote_copy(
            src_ref=block(x_ref, peer),
            dst_ref=slots.at[k],
            send_sem=send1.at[k],
            recv_sem=recv1.at[k],
            device_id=(chip, core, peer),
            device_id_type=MESH,
        )
        copy.start()
        first.append(copy)
    for copy in first:
        copy.wait()
    total = block(x_ref, me)[...].astype(jnp.float32)
    for k in range(1, n):
        total = total + slots[k].astype(jnp.float32)
    reduced[...] = total.astype(reduced.dtype)
    block(out_ref, me)[...] = reduced[...]

    second = []
    for k in range(1, n):
        peer = lax.rem(me + k, n)
        copy = pltpu.make_async_remote_copy(
            src_ref=reduced,
            dst_ref=block(out_ref, me),
            send_sem=send2.at[k],
            recv_sem=recv2.at[k],
            device_id=(chip, core, peer),
            device_id_type=MESH,
        )
        copy.start()
        second.append(copy)
    for copy in second:
        copy.wait()


def tp_sum(x, collective_id):
    n = lax.axis_size("tp")
    rows, width = x.shape
    cols = width // n
    return pl.pallas_call(
        functools.partial(tp_sum_kernel, n),
        out_shape=jax.ShapeDtypeStruct((rows, width), x.dtype),
        in_specs=[pl.BlockSpec(memory_space=pltpu.VMEM)],
        out_specs=pl.BlockSpec(memory_space=pltpu.VMEM),
        scratch_shapes=[
            pltpu.VMEM((n, rows, cols), x.dtype),
            pltpu.VMEM((rows, cols), x.dtype),
            pltpu.SemaphoreType.DMA((n,)),
            pltpu.SemaphoreType.DMA((n,)),
            pltpu.SemaphoreType.DMA((n,)),
            pltpu.SemaphoreType.DMA((n,)),
        ],
        compiler_params=pltpu.CompilerParams(collective_id=collective_id, has_side_effects=True),
    )(x)


def attention_kernel(info, q_ref, q_last_ref, q_first_ref, kv_ref, o_ref, top_ref, total_ref, acc_ref):
    step = pl.program_id(0)
    groups, rows_all, head_size = q_ref.shape
    shards_per, rows, _ = kv_ref.shape
    width = shards_per * rows
    half = kv_ref.shape[2] // 2
    rows_q = o_ref.shape[0]
    per_group = rows_all // rows_q
    scale = 1.0 / math.sqrt(head_size)

    @pl.when(step == 0)
    def _():
        top_ref[...] = jnp.full(top_ref.shape, -1e30, jnp.float32)
        total_ref[...] = jnp.zeros(total_ref.shape, jnp.float32)
        acc_ref[...] = jnp.zeros(acc_ref.shape, jnp.float32)

    offset = step * width
    needed = (step >= info[0]) & (step <= info[1])
    whole = (offset >= info[2]) & (offset + width - 1 <= info[3])

    def run(masked):
        for g in range(groups):
            q = q_ref[g]
            k = kv_ref[:, :, g * head_size : (g + 1) * head_size].reshape(width, head_size)
            v = kv_ref[:, :, half + g * head_size : half + (g + 1) * head_size].reshape(width, head_size)
            s = lax.dot_general(q, k, (((1,), (1,)), ((), ())), preferred_element_type=jnp.float32) * scale
            if masked:
                k_index = offset + lax.broadcasted_iota(jnp.int32, s.shape, 1)
                allowed = (k_index <= q_last_ref[...]) & (k_index >= q_first_ref[...])
                s = jnp.where(allowed, s, -1e30)
            top = top_ref[g]
            new_top = jnp.maximum(top, jnp.max(s, axis=-1, keepdims=True))
            p = jnp.exp(s - new_top)
            if masked:
                p = jnp.where(allowed, p, 0.0)
            decay = jnp.exp(top - new_top)
            total_ref[g] = total_ref[g] * decay + jnp.sum(p, axis=-1, keepdims=True)
            acc_ref[g] = acc_ref[g] * decay + jnp.dot(
                p.astype(jnp.bfloat16), v, preferred_element_type=jnp.float32
            )
            top_ref[g] = new_top

    @pl.when(needed & whole)
    def _():
        run(False)

    @pl.when(needed & jnp.logical_not(whole))
    def _():
        run(True)

    @pl.when(step == pl.num_programs(0) - 1)
    def _():
        for g in range(groups):
            out = acc_ref[g] / total_ref[g]
            for h in range(per_group):
                col = (g * per_group + h) * head_size
                o_ref[:, col : col + head_size] = out[h * rows_q : (h + 1) * rows_q].astype(o_ref.dtype)


def attention(q_grouped, q_last, q_first, gathered, info, rows, kv_rows_per_shard, shards_per):
    groups, rows_all, head_size = q_grouped.shape
    shards, _, width_all = gathered.shape
    blocks = shards // shards_per
    out_cols = rows_all // rows * groups * head_size

    def kv_map(j, info):
        return (jnp.minimum(jnp.maximum(j, info[0]), info[1]), 0, 0)

    grid_spec = pltpu.PrefetchScalarGridSpec(
        num_scalar_prefetch=1,
        grid=(blocks,),
        in_specs=[
            pl.BlockSpec((groups, rows_all, head_size), lambda j, info: (0, 0, 0)),
            pl.BlockSpec((rows_all, 1), lambda j, info: (0, 0)),
            pl.BlockSpec((rows_all, 1), lambda j, info: (0, 0)),
            pl.BlockSpec((shards_per, kv_rows_per_shard, width_all), kv_map),
        ],
        out_specs=pl.BlockSpec((rows, out_cols), lambda j, info: (0, 0)),
        scratch_shapes=[
            pltpu.VMEM((groups, rows_all, 1), jnp.float32),
            pltpu.VMEM((groups, rows_all, 1), jnp.float32),
            pltpu.VMEM((groups, rows_all, head_size), jnp.float32),
        ],
    )
    return pl.pallas_call(
        attention_kernel,
        out_shape=jax.ShapeDtypeStruct((rows, out_cols), jnp.bfloat16),
        grid_spec=grid_spec,
        compiler_params=pltpu.CompilerParams(dimension_semantics=("arbitrary",)),
    )(info, q_grouped, q_last, q_first, gathered)


def body(
    layer_input,
    norm_gain,
    w_query,
    key_weight,
    value_weight,
    w_out,
    query_gain,
    key_gain,
    seg_ids,
    positions,
    post_gain,
    w_gate,
    w_up,
    w_down,
):
    rows = layer_input.shape[0]
    head_size = query_gain.shape[0]
    query_local = w_query.shape[1] // head_size
    kv_local = key_weight.shape[1] // head_size
    kv_cols = kv_local * head_size
    head_group = query_local // kv_local
    scale = 1.0 / math.sqrt(head_size)
    shards = lax.axis_size("chip") * lax.axis_size("core")
    xf = layer_input.astype(jnp.float32)
    normed_input = rms(xf, norm_gain).astype(jnp.bfloat16)
    query_matrix = jnp.dot(normed_input, w_query, preferred_element_type=jnp.float32).reshape(
        rows, query_local, head_size
    )
    query_matrix = rope(rms(query_matrix, query_gain), positions).astype(jnp.bfloat16)
    key_matrix = jnp.dot(normed_input, key_weight, preferred_element_type=jnp.float32).reshape(
        rows, kv_local, head_size
    )
    key_matrix = rope(rms(key_matrix, key_gain), positions).astype(jnp.bfloat16)
    key_cache = key_matrix.reshape(rows, kv_cols)
    value_cache = jnp.dot(normed_input, value_weight, preferred_element_type=jnp.float32).astype(
        jnp.bfloat16
    )

    width_all = 2 * kv_cols
    ff_rows, ff_local = w_gate.shape
    rest = ff_local - width_all
    down_t = w_down.T
    packed = jnp.concatenate(
        [
            jnp.concatenate([key_cache, value_cache], axis=1),
            w_gate[:, :width_all],
            w_up[:, :width_all],
            down_t[:, :width_all],
            jnp.concatenate([w_gate[:, width_all:], w_up[:, width_all:]], axis=1),
            jnp.concatenate(
                [down_t[:, width_all:], jnp.zeros((ff_rows, 2 * width_all - ff_local), down_t.dtype)],
                axis=1,
            ),
        ],
        axis=0,
    )
    half_gathered = lax.all_gather(packed, "chip", axis=0, tiled=False)
    gathered = lax.all_gather(half_gathered, "core", axis=1, tiled=False).reshape(
        (shards,) + packed.shape
    )

    def weight_part(k, lo, hi):
        top = rows + k * ff_rows
        return gathered[:, top : top + ff_rows, lo:hi].reshape(shards * ff_rows, hi - lo)

    gate_a = weight_part(0, 0, width_all)
    up_a = weight_part(1, 0, width_all)
    down_a = weight_part(2, 0, width_all)
    gate_b = weight_part(3, 0, rest)
    up_b = weight_part(3, rest, 2 * rest)
    down_b = weight_part(4, 0, rest)

    me = lax.axis_index("chip") * lax.axis_size("core") + lax.axis_index("core")
    first = me * rows
    my_last = first + rows - 1
    q_index = first + jnp.arange(rows, dtype=jnp.int32)
    q_start = q_index - positions
    shards_per = 1
    for trial in range(1, max(1, 1024 // rows) + 1):
        if shards % trial == 0:
            shards_per = trial
    width = rows * shards_per
    info = jnp.stack([q_start[0] // width, my_last // width, q_start[rows - 1], first])
    q_grouped = (
        query_matrix.reshape(rows, kv_local, head_group, head_size)
        .transpose(1, 2, 0, 3)
        .reshape(kv_local, head_group * rows, head_size)
    )
    q_last = jnp.tile(q_index, head_group).reshape(head_group * rows, 1)
    q_first = jnp.tile(q_start, head_group).reshape(head_group * rows, 1)
    attended = attention(q_grouped, q_last, q_first, gathered, info, rows, rows, shards_per)
    partial_out = jnp.dot(attended, w_out, preferred_element_type=jnp.float32)
    summed = tp_sum(partial_out.astype(jnp.bfloat16), 0).astype(jnp.float32)
    mid = (xf + summed).astype(jnp.bfloat16)
    mid_f = mid.astype(jnp.float32)
    post_normed = rms(mid_f, post_gain).astype(jnp.bfloat16)
    def ffn_piece(gate_w, up_w, down_w):
        gate = jnp.dot(post_normed, gate_w, preferred_element_type=jnp.float32)
        up = jnp.dot(post_normed, up_w, preferred_element_type=jnp.float32)
        act = (jax.nn.silu(gate) * up).astype(jnp.bfloat16)
        return lax.dot_general(
            act, down_w, (((1,), (1,)), ((), ())), preferred_element_type=jnp.float32
        )

    terms = ffn_piece(gate_a, up_a, down_a) + ffn_piece(gate_b, up_b, down_b)
    ffn_total = tp_sum(terms.astype(jnp.bfloat16), 1).astype(jnp.float32)
    hidden = (mid_f + ffn_total).astype(jnp.bfloat16)
    return (hidden, key_cache, value_cache)


def solution(mesh):
    devices = mesh.devices
    per_chip = 2
    split = jax.sharding.Mesh(
        devices.reshape(devices.shape[0] // per_chip, per_chip, devices.shape[1]), ("chip", "core", "tp")
    )
    seq = ("chip", "core")
    in_specs = (
        P(seq, None),
        P(),
        P(None, "tp"),
        P(None, "tp"),
        P(None, "tp"),
        P("tp", None),
        P(),
        P(),
        P(seq),
        P(seq),
        P(),
        P(seq, "tp"),
        P(seq, "tp"),
        P("tp", seq),
    )
    out_specs = (P(seq, None), P(seq, "tp"), P(seq, "tp"))
    return jax.shard_map(body, mesh=split, in_specs=in_specs, out_specs=out_specs, check_vma=False)
```

```python
import functools
import math

import jax
import jax.numpy as jnp
from jax import lax
from jax.experimental import pallas as pl
from jax.experimental.pallas import tpu as pltpu
from jax.sharding import PartitionSpec as P

MESH = pl.DeviceIdType.MESH


def rms(v, gain):
    return v * lax.rsqrt(jnp.mean(v * v, axis=-1, keepdims=True) + 1e-06) * gain


def rope(v, place):
    half = v.shape[-1] // 2
    freqs = 1000000.0 ** (-2.0 * jnp.arange(half, dtype=jnp.float32) / v.shape[-1])
    angle = place.astype(jnp.float32)[:, None] * freqs[None, :]
    cosine = jnp.cos(angle)[:, None, :]
    sine = jnp.sin(angle)[:, None, :]
    block_start = v[..., :half]
    second = v[..., half:]
    return jnp.concatenate(
        [block_start * cosine - second * sine, second * cosine + block_start * sine], axis=-1
    )


def tp_sum_kernel(n, x_ref, out_ref, slots, reduced, send1, recv1, send2, recv2):
    me = lax.axis_index("tp")
    row = lax.axis_index("seq")
    cols = x_ref.shape[1] // n

    barrier = pltpu.get_barrier_semaphore()
    for k in range(1, n):
        pl.semaphore_signal(barrier, inc=1, device_id=(row, lax.rem(me + k, n)), device_id_type=MESH)
    pl.semaphore_wait(barrier, n - 1)

    def block(ref, owner):
        return ref.at[:, pl.ds(pl.multiple_of(owner * cols, cols), cols)]

    first = []
    for k in range(1, n):
        peer = lax.rem(me + k, n)
        copy = pltpu.make_async_remote_copy(
            src_ref=block(x_ref, peer),
            dst_ref=slots.at[k],
            send_sem=send1.at[k],
            recv_sem=recv1.at[k],
            device_id=(row, peer),
            device_id_type=MESH,
        )
        copy.start()
        first.append(copy)
    for copy in first:
        copy.wait()
    total = block(x_ref, me)[...].astype(jnp.float32)
    for k in range(1, n):
        total = total + slots[k].astype(jnp.float32)
    reduced[...] = total.astype(reduced.dtype)
    block(out_ref, me)[...] = reduced[...]

    second = []
    for k in range(1, n):
        peer = lax.rem(me + k, n)
        copy = pltpu.make_async_remote_copy(
            src_ref=reduced,
            dst_ref=block(out_ref, me),
            send_sem=send2.at[k],
            recv_sem=recv2.at[k],
            device_id=(row, peer),
            device_id_type=MESH,
        )
        copy.start()
        second.append(copy)
    for copy in second:
        copy.wait()


def tp_sum(x, collective_id):
    n = lax.axis_size("tp")
    rows, width = x.shape
    cols = width // n
    return pl.pallas_call(
        functools.partial(tp_sum_kernel, n),
        out_shape=jax.ShapeDtypeStruct((rows, width), x.dtype),
        in_specs=[pl.BlockSpec(memory_space=pltpu.VMEM)],
        out_specs=pl.BlockSpec(memory_space=pltpu.VMEM),
        scratch_shapes=[
            pltpu.VMEM((n, rows, cols), x.dtype),
            pltpu.VMEM((rows, cols), x.dtype),
            pltpu.SemaphoreType.DMA((n,)),
            pltpu.SemaphoreType.DMA((n,)),
            pltpu.SemaphoreType.DMA((n,)),
            pltpu.SemaphoreType.DMA((n,)),
        ],
        compiler_params=pltpu.CompilerParams(collective_id=collective_id, has_side_effects=True),
    )(x)


def attention_kernel(info, q_ref, q_last_ref, q_first_ref, kv_ref, o_ref, top_ref, total_ref, acc_ref):
    step = pl.program_id(0)
    groups, rows_all, head_size = q_ref.shape
    shards_per, both, _ = kv_ref.shape
    rows = both // 2
    width = shards_per * rows
    rows_q = o_ref.shape[0]
    per_group = rows_all // rows_q
    scale = 1.0 / math.sqrt(head_size)

    @pl.when(step == 0)
    def _():
        top_ref[...] = jnp.full(top_ref.shape, -1e30, jnp.float32)
        total_ref[...] = jnp.zeros(total_ref.shape, jnp.float32)
        acc_ref[...] = jnp.zeros(acc_ref.shape, jnp.float32)

    offset = step * width
    needed = (step >= info[0]) & (step <= info[1])
    whole = (offset >= info[2]) & (offset + width - 1 <= info[3])

    def run(masked):
        for g in range(groups):
            q = q_ref[g]
            k = kv_ref[:, :rows, g * head_size : (g + 1) * head_size].reshape(width, head_size)
            v = kv_ref[:, rows:, g * head_size : (g + 1) * head_size].reshape(width, head_size)
            s = lax.dot_general(q, k, (((1,), (1,)), ((), ())), preferred_element_type=jnp.float32) * scale
            if masked:
                k_index = offset + lax.broadcasted_iota(jnp.int32, s.shape, 1)
                allowed = (k_index <= q_last_ref[...]) & (k_index >= q_first_ref[...])
                s = jnp.where(allowed, s, -1e30)
            top = top_ref[g]
            new_top = jnp.maximum(top, jnp.max(s, axis=-1, keepdims=True))
            p = jnp.exp(s - new_top)
            if masked:
                p = jnp.where(allowed, p, 0.0)
            decay = jnp.exp(top - new_top)
            total_ref[g] = total_ref[g] * decay + jnp.sum(p, axis=-1, keepdims=True)
            acc_ref[g] = acc_ref[g] * decay + jnp.dot(
                p.astype(jnp.bfloat16), v, preferred_element_type=jnp.float32
            )
            top_ref[g] = new_top

    @pl.when(needed & whole)
    def _():
        run(False)

    @pl.when(needed & jnp.logical_not(whole))
    def _():
        run(True)

    @pl.when(step == pl.num_programs(0) - 1)
    def _():
        for g in range(groups):
            out = acc_ref[g] / total_ref[g]
            for h in range(per_group):
                col = (g * per_group + h) * head_size
                o_ref[:, col : col + head_size] = out[h * rows_q : (h + 1) * rows_q].astype(o_ref.dtype)


def attention(q_grouped, q_last, q_first, gathered, info, rows, kv_rows_per_shard, shards_per):
    groups, rows_all, head_size = q_grouped.shape
    shards, _, width_all = gathered.shape
    blocks = shards // shards_per
    out_cols = rows_all // rows * groups * head_size

    def kv_map(j, info):
        return (jnp.minimum(jnp.maximum(j, info[0]), info[1]), 0, 0)

    grid_spec = pltpu.PrefetchScalarGridSpec(
        num_scalar_prefetch=1,
        grid=(blocks,),
        in_specs=[
            pl.BlockSpec((groups, rows_all, head_size), lambda j, info: (0, 0, 0)),
            pl.BlockSpec((rows_all, 1), lambda j, info: (0, 0)),
            pl.BlockSpec((rows_all, 1), lambda j, info: (0, 0)),
            pl.BlockSpec((shards_per, kv_rows_per_shard, width_all), kv_map),
        ],
        out_specs=pl.BlockSpec((rows, out_cols), lambda j, info: (0, 0)),
        scratch_shapes=[
            pltpu.VMEM((groups, rows_all, 1), jnp.float32),
            pltpu.VMEM((groups, rows_all, 1), jnp.float32),
            pltpu.VMEM((groups, rows_all, head_size), jnp.float32),
        ],
    )
    return pl.pallas_call(
        attention_kernel,
        out_shape=jax.ShapeDtypeStruct((rows, out_cols), jnp.bfloat16),
        grid_spec=grid_spec,
        compiler_params=pltpu.CompilerParams(dimension_semantics=("arbitrary",)),
    )(info, q_grouped, q_last, q_first, gathered)


def body(
    layer_input,
    norm_gain,
    w_query,
    key_weight,
    value_weight,
    w_out,
    query_gain,
    key_gain,
    seg_ids,
    positions,
    post_gain,
    w_gate,
    w_up,
    w_down,
):
    rows = layer_input.shape[0]
    head_size = query_gain.shape[0]
    query_local = w_query.shape[1] // head_size
    kv_local = key_weight.shape[1] // head_size
    kv_cols = kv_local * head_size
    head_group = query_local // kv_local
    scale = 1.0 / math.sqrt(head_size)
    shards = lax.axis_size("seq")
    xf = layer_input.astype(jnp.float32)
    normed_input = rms(xf, norm_gain).astype(jnp.bfloat16)
    query_matrix = jnp.dot(normed_input, w_query, preferred_element_type=jnp.float32).reshape(
        rows, query_local, head_size
    )
    query_matrix = rope(rms(query_matrix, query_gain), positions).astype(jnp.bfloat16)
    key_matrix = jnp.dot(normed_input, key_weight, preferred_element_type=jnp.float32).reshape(
        rows, kv_local, head_size
    )
    key_matrix = rope(rms(key_matrix, key_gain), positions).astype(jnp.bfloat16)
    key_cache = key_matrix.reshape(rows, kv_cols)
    value_cache = jnp.dot(normed_input, value_weight, preferred_element_type=jnp.float32).astype(
        jnp.bfloat16
    )

    width_all = 2 * kv_cols
    ff_rows, ff_local = w_gate.shape
    rest = ff_local - width_all
    down_t = w_down.T
    kv_packed = jnp.concatenate([key_cache, value_cache], axis=0)
    kv_gathered = lax.all_gather(kv_packed, "seq", axis=0, tiled=False)
    weights_packed = jnp.concatenate(
        [
            w_gate[:, :width_all],
            w_up[:, :width_all],
            down_t[:, :width_all],
            jnp.concatenate([w_gate[:, width_all:], w_up[:, width_all:]], axis=1),
            jnp.concatenate(
                [down_t[:, width_all:], jnp.zeros((ff_rows, 2 * width_all - ff_local), down_t.dtype)],
                axis=1,
            ),
        ],
        axis=0,
    )
    kv_gathered, weights_packed = lax.optimization_barrier((kv_gathered, weights_packed))
    w_gathered = lax.all_gather(weights_packed, "seq", axis=0, tiled=False)

    def weight_part(k, lo, hi):
        top = k * ff_rows
        return w_gathered[:, top : top + ff_rows, lo:hi].reshape(shards * ff_rows, hi - lo)

    gate_a = weight_part(0, 0, width_all)
    up_a = weight_part(1, 0, width_all)
    down_a = weight_part(2, 0, width_all)
    gate_b = weight_part(3, 0, rest)
    up_b = weight_part(3, rest, 2 * rest)
    down_b = weight_part(4, 0, rest)

    me = lax.axis_index("seq")
    first = me * rows
    my_last = first + rows - 1
    q_index = first + jnp.arange(rows, dtype=jnp.int32)
    q_start = q_index - positions
    shards_per = 1
    for trial in range(1, max(1, 1024 // rows) + 1):
        if shards % trial == 0:
            shards_per = trial
    width = rows * shards_per
    info = jnp.stack([q_start[0] // width, my_last // width, q_start[rows - 1], first])
    q_grouped = (
        query_matrix.reshape(rows, kv_local, head_group, head_size)
        .transpose(1, 2, 0, 3)
        .reshape(kv_local, head_group * rows, head_size)
    )
    q_last = jnp.tile(q_index, head_group).reshape(head_group * rows, 1)
    q_first = jnp.tile(q_start, head_group).reshape(head_group * rows, 1)
    attended = attention(q_grouped, q_last, q_first, kv_gathered, info, rows, 2 * rows, shards_per)
    partial_out = jnp.dot(attended, w_out, preferred_element_type=jnp.float32)
    summed = tp_sum(partial_out.astype(jnp.bfloat16), 0).astype(jnp.float32)
    mid = (xf + summed).astype(jnp.bfloat16)
    mid_f = mid.astype(jnp.float32)
    post_normed = rms(mid_f, post_gain).astype(jnp.bfloat16)
    def ffn_piece(gate_w, up_w, down_w):
        gate = jnp.dot(post_normed, gate_w, preferred_element_type=jnp.float32)
        up = jnp.dot(post_normed, up_w, preferred_element_type=jnp.float32)
        act = (jax.nn.silu(gate) * up).astype(jnp.bfloat16)
        return lax.dot_general(
            act, down_w, (((1,), (1,)), ((), ())), preferred_element_type=jnp.float32
        )

    terms = ffn_piece(gate_a, up_a, down_a) + ffn_piece(gate_b, up_b, down_b)
    ffn_total = tp_sum(terms.astype(jnp.bfloat16), 1).astype(jnp.float32)
    hidden = (mid_f + ffn_total).astype(jnp.bfloat16)
    return (hidden, key_cache, value_cache)


def solution(mesh):
    in_specs = (
        P("seq", None),
        P(),
        P(None, "tp"),
        P(None, "tp"),
        P(None, "tp"),
        P("tp", None),
        P(),
        P(),
        P("seq"),
        P("seq"),
        P(),
        P("seq", "tp"),
        P("seq", "tp"),
        P("tp", "seq"),
    )
    out_specs = (P("seq", None), P("seq", "tp"), P("seq", "tp"))
    return jax.shard_map(body, mesh=mesh, in_specs=in_specs, out_specs=out_specs, check_vma=False)
```

```python
import functools
import math

import jax
import jax.numpy as jnp
from jax import lax
from jax.experimental import pallas as pl
from jax.experimental.pallas import tpu as pltpu
from jax.sharding import PartitionSpec as P

MESH = pl.DeviceIdType.MESH


def rms(v, gain):
    return v * lax.rsqrt(jnp.mean(v * v, axis=-1, keepdims=True) + 1e-06) * gain


def rope(v, place):
    half = v.shape[-1] // 2
    freqs = 1000000.0 ** (-2.0 * jnp.arange(half, dtype=jnp.float32) / v.shape[-1])
    angle = place.astype(jnp.float32)[:, None] * freqs[None, :]
    cosine = jnp.cos(angle)[:, None, :]
    sine = jnp.sin(angle)[:, None, :]
    block_start = v[..., :half]
    second = v[..., half:]
    return jnp.concatenate(
        [block_start * cosine - second * sine, second * cosine + block_start * sine], axis=-1
    )


def tp_sum_kernel(n, x_ref, out_ref, slots, reduced, send1, recv1, send2, recv2):
    me = lax.axis_index("tp")
    row = lax.axis_index("seq")
    cols = x_ref.shape[1] // n

    barrier = pltpu.get_barrier_semaphore()
    for k in range(1, n):
        pl.semaphore_signal(barrier, inc=1, device_id=(row, lax.rem(me + k, n)), device_id_type=MESH)
    pl.semaphore_wait(barrier, n - 1)

    def block(ref, owner):
        return ref.at[:, pl.ds(pl.multiple_of(owner * cols, cols), cols)]

    first = []
    for k in range(1, n):
        peer = lax.rem(me + k, n)
        copy = pltpu.make_async_remote_copy(
            src_ref=block(x_ref, peer),
            dst_ref=slots.at[k],
            send_sem=send1.at[k],
            recv_sem=recv1.at[k],
            device_id=(row, peer),
            device_id_type=MESH,
        )
        copy.start()
        first.append(copy)
    for copy in first:
        copy.wait()
    total = block(x_ref, me)[...].astype(jnp.float32)
    for k in range(1, n):
        total = total + slots[k].astype(jnp.float32)
    reduced[...] = total.astype(reduced.dtype)
    block(out_ref, me)[...] = reduced[...]

    second = []
    for k in range(1, n):
        peer = lax.rem(me + k, n)
        copy = pltpu.make_async_remote_copy(
            src_ref=reduced,
            dst_ref=block(out_ref, me),
            send_sem=send2.at[k],
            recv_sem=recv2.at[k],
            device_id=(row, peer),
            device_id_type=MESH,
        )
        copy.start()
        second.append(copy)
    for copy in second:
        copy.wait()


def tp_sum(x, collective_id):
    n = lax.axis_size("tp")
    rows, width = x.shape
    cols = width // n
    return pl.pallas_call(
        functools.partial(tp_sum_kernel, n),
        out_shape=jax.ShapeDtypeStruct((rows, width), x.dtype),
        in_specs=[pl.BlockSpec(memory_space=pltpu.VMEM)],
        out_specs=pl.BlockSpec(memory_space=pltpu.VMEM),
        scratch_shapes=[
            pltpu.VMEM((n, rows, cols), x.dtype),
            pltpu.VMEM((rows, cols), x.dtype),
            pltpu.SemaphoreType.DMA((n,)),
            pltpu.SemaphoreType.DMA((n,)),
            pltpu.SemaphoreType.DMA((n,)),
            pltpu.SemaphoreType.DMA((n,)),
        ],
        compiler_params=pltpu.CompilerParams(collective_id=collective_id, has_side_effects=True),
    )(x)


def attention_kernel(info, q_ref, q_last_ref, q_first_ref, kv_ref, o_ref, top_ref, total_ref, acc_ref):
    step = pl.program_id(0)
    groups, rows_all, head_size = q_ref.shape
    shards_per, both, _ = kv_ref.shape
    rows = both // 2
    width = shards_per * rows
    rows_q = o_ref.shape[0]
    per_group = rows_all // rows_q
    scale = 1.0 / math.sqrt(head_size)

    @pl.when(step == 0)
    def _():
        top_ref[...] = jnp.full(top_ref.shape, -1e30, jnp.float32)
        total_ref[...] = jnp.zeros(total_ref.shape, jnp.float32)
        acc_ref[...] = jnp.zeros(acc_ref.shape, jnp.float32)

    offset = step * width
    needed = (step >= info[0]) & (step <= info[1])
    whole = (offset >= info[2]) & (offset + width - 1 <= info[3])

    def run(masked):
        for g in range(groups):
            q = q_ref[g]
            k = kv_ref[:, :rows, g * head_size : (g + 1) * head_size].reshape(width, head_size)
            v = kv_ref[:, rows:, g * head_size : (g + 1) * head_size].reshape(width, head_size)
            s = lax.dot_general(q, k, (((1,), (1,)), ((), ())), preferred_element_type=jnp.float32) * scale
            if masked:
                k_index = offset + lax.broadcasted_iota(jnp.int32, s.shape, 1)
                allowed = (k_index <= q_last_ref[...]) & (k_index >= q_first_ref[...])
                s = jnp.where(allowed, s, -1e30)
            top = top_ref[g]
            new_top = jnp.maximum(top, jnp.max(s, axis=-1, keepdims=True))
            p = jnp.exp(s - new_top)
            if masked:
                p = jnp.where(allowed, p, 0.0)
            decay = jnp.exp(top - new_top)
            total_ref[g] = total_ref[g] * decay + jnp.sum(p, axis=-1, keepdims=True)
            acc_ref[g] = acc_ref[g] * decay + jnp.dot(
                p.astype(jnp.bfloat16), v, preferred_element_type=jnp.float32
            )
            top_ref[g] = new_top

    @pl.when(needed & whole)
    def _():
        run(False)

    @pl.when(needed & jnp.logical_not(whole))
    def _():
        run(True)

    @pl.when(step == pl.num_programs(0) - 1)
    def _():
        for g in range(groups):
            out = acc_ref[g] / total_ref[g]
            for h in range(per_group):
                col = (g * per_group + h) * head_size
                o_ref[:, col : col + head_size] = out[h * rows_q : (h + 1) * rows_q].astype(o_ref.dtype)


def attention(q_grouped, q_last, q_first, gathered, info, rows, kv_rows_per_shard, shards_per):
    groups, rows_all, head_size = q_grouped.shape
    shards, _, width_all = gathered.shape
    blocks = shards // shards_per
    out_cols = rows_all // rows * groups * head_size

    def kv_map(j, info):
        return (jnp.minimum(jnp.maximum(j, info[0]), info[1]), 0, 0)

    grid_spec = pltpu.PrefetchScalarGridSpec(
        num_scalar_prefetch=1,
        grid=(blocks,),
        in_specs=[
            pl.BlockSpec((groups, rows_all, head_size), lambda j, info: (0, 0, 0)),
            pl.BlockSpec((rows_all, 1), lambda j, info: (0, 0)),
            pl.BlockSpec((rows_all, 1), lambda j, info: (0, 0)),
            pl.BlockSpec((shards_per, kv_rows_per_shard, width_all), kv_map),
        ],
        out_specs=pl.BlockSpec((rows, out_cols), lambda j, info: (0, 0)),
        scratch_shapes=[
            pltpu.VMEM((groups, rows_all, 1), jnp.float32),
            pltpu.VMEM((groups, rows_all, 1), jnp.float32),
            pltpu.VMEM((groups, rows_all, head_size), jnp.float32),
        ],
    )
    return pl.pallas_call(
        attention_kernel,
        out_shape=jax.ShapeDtypeStruct((rows, out_cols), jnp.bfloat16),
        grid_spec=grid_spec,
        compiler_params=pltpu.CompilerParams(dimension_semantics=("arbitrary",)),
    )(info, q_grouped, q_last, q_first, gathered)


def body(
    layer_input,
    norm_gain,
    w_query,
    key_weight,
    value_weight,
    w_out,
    query_gain,
    key_gain,
    seg_ids,
    positions,
    post_gain,
    w_gate,
    w_up,
    w_down,
):
    rows = layer_input.shape[0]
    head_size = query_gain.shape[0]
    query_local = w_query.shape[1] // head_size
    kv_local = key_weight.shape[1] // head_size
    kv_cols = kv_local * head_size
    head_group = query_local // kv_local
    scale = 1.0 / math.sqrt(head_size)
    shards = lax.axis_size("seq")
    xf = layer_input.astype(jnp.float32)
    normed_input = rms(xf, norm_gain).astype(jnp.bfloat16)
    query_matrix = jnp.dot(normed_input, w_query, preferred_element_type=jnp.float32).reshape(
        rows, query_local, head_size
    )
    query_matrix = rope(rms(query_matrix, query_gain), positions).astype(jnp.bfloat16)
    key_matrix = jnp.dot(normed_input, key_weight, preferred_element_type=jnp.float32).reshape(
        rows, kv_local, head_size
    )
    key_matrix = rope(rms(key_matrix, key_gain), positions).astype(jnp.bfloat16)
    key_cache = key_matrix.reshape(rows, kv_cols)
    value_cache = jnp.dot(normed_input, value_weight, preferred_element_type=jnp.float32).astype(
        jnp.bfloat16
    )

    width_all = 2 * kv_cols
    ff_rows, ff_local = w_gate.shape
    rest = ff_local - width_all
    down_t = w_down.T
    kv_packed = jnp.concatenate([key_cache, value_cache], axis=0)
    kv_gathered = lax.all_gather(kv_packed, "seq", axis=0, tiled=False)
    weights_packed = jnp.concatenate(
        [
            w_gate[:, :width_all],
            w_up[:, :width_all],
            down_t[:, :width_all],
            jnp.concatenate([w_gate[:, width_all:], w_up[:, width_all:]], axis=1),
            jnp.concatenate(
                [down_t[:, width_all:], jnp.zeros((ff_rows, 2 * width_all - ff_local), down_t.dtype)],
                axis=1,
            ),
        ],
        axis=0,
    )

    def weight_part(k, lo, hi):
        top = k * ff_rows
        return w_gathered[:, top : top + ff_rows, lo:hi].reshape(shards * ff_rows, hi - lo)


    me = lax.axis_index("seq")
    first = me * rows
    my_last = first + rows - 1
    q_index = first + jnp.arange(rows, dtype=jnp.int32)
    q_start = q_index - positions
    shards_per = 1
    for trial in range(1, max(1, 1024 // rows) + 1):
        if shards % trial == 0:
            shards_per = trial
    width = rows * shards_per
    info = jnp.stack([q_start[0] // width, my_last // width, q_start[rows - 1], first])
    q_grouped = (
        query_matrix.reshape(rows, kv_local, head_group, head_size)
        .transpose(1, 2, 0, 3)
        .reshape(kv_local, head_group * rows, head_size)
    )
    q_last = jnp.tile(q_index, head_group).reshape(head_group * rows, 1)
    q_first = jnp.tile(q_start, head_group).reshape(head_group * rows, 1)
    kv_gathered, weights_packed, q_grouped, q_last, q_first, info = lax.optimization_barrier(
        (kv_gathered, weights_packed, q_grouped, q_last, q_first, info)
    )
    w_gathered = lax.all_gather(weights_packed, "seq", axis=0, tiled=False)
    gate_a = weight_part(0, 0, width_all)
    up_a = weight_part(1, 0, width_all)
    down_a = weight_part(2, 0, width_all)
    gate_b = weight_part(3, 0, rest)
    up_b = weight_part(3, rest, 2 * rest)
    down_b = weight_part(4, 0, rest)
    attended = attention(q_grouped, q_last, q_first, kv_gathered, info, rows, 2 * rows, shards_per)
    partial_out = jnp.dot(attended, w_out, preferred_element_type=jnp.float32)
    summed = tp_sum(partial_out.astype(jnp.bfloat16), 0).astype(jnp.float32)
    mid = (xf + summed).astype(jnp.bfloat16)
    mid_f = mid.astype(jnp.float32)
    post_normed = rms(mid_f, post_gain).astype(jnp.bfloat16)
    def ffn_piece(gate_w, up_w, down_w):
        gate = jnp.dot(post_normed, gate_w, preferred_element_type=jnp.float32)
        up = jnp.dot(post_normed, up_w, preferred_element_type=jnp.float32)
        act = (jax.nn.silu(gate) * up).astype(jnp.bfloat16)
        return lax.dot_general(
            act, down_w, (((1,), (1,)), ((), ())), preferred_element_type=jnp.float32
        )

    terms = ffn_piece(gate_a, up_a, down_a) + ffn_piece(gate_b, up_b, down_b)
    ffn_total = tp_sum(terms.astype(jnp.bfloat16), 1).astype(jnp.float32)
    hidden = (mid_f + ffn_total).astype(jnp.bfloat16)
    return (hidden, key_cache, value_cache)


def solution(mesh):
    in_specs = (
        P("seq", None),
        P(),
        P(None, "tp"),
        P(None, "tp"),
        P(None, "tp"),
        P("tp", None),
        P(),
        P(),
        P("seq"),
        P("seq"),
        P(),
        P("seq", "tp"),
        P("seq", "tp"),
        P("tp", "seq"),
    )
    out_specs = (P("seq", None), P("seq", "tp"), P("seq", "tp"))
    return jax.shard_map(body, mesh=mesh, in_specs=in_specs, out_specs=out_specs, check_vma=False)
```

```python
import functools
import math

import jax
import jax.numpy as jnp
from jax import lax
from jax.experimental import pallas as pl
from jax.experimental.pallas import tpu as pltpu
from jax.sharding import PartitionSpec as P

MESH = pl.DeviceIdType.MESH


def rms(v, gain):
    return v * lax.rsqrt(jnp.mean(v * v, axis=-1, keepdims=True) + 1e-06) * gain


def rope(v, place):
    half = v.shape[-1] // 2
    freqs = 1000000.0 ** (-2.0 * jnp.arange(half, dtype=jnp.float32) / v.shape[-1])
    angle = place.astype(jnp.float32)[:, None] * freqs[None, :]
    cosine = jnp.cos(angle)[:, None, :]
    sine = jnp.sin(angle)[:, None, :]
    block_start = v[..., :half]
    second = v[..., half:]
    return jnp.concatenate(
        [block_start * cosine - second * sine, second * cosine + block_start * sine], axis=-1
    )


def tp_sum_kernel(n, x_ref, out_ref, slots, reduced, send1, recv1, send2, recv2):
    me = lax.axis_index("tp")
    row = lax.axis_index("seq")
    cols = x_ref.shape[1] // n

    barrier = pltpu.get_barrier_semaphore()
    for k in range(1, n):
        pl.semaphore_signal(barrier, inc=1, device_id=(row, lax.rem(me + k, n)), device_id_type=MESH)
    pl.semaphore_wait(barrier, n - 1)

    def block(ref, owner):
        return ref.at[:, pl.ds(pl.multiple_of(owner * cols, cols), cols)]

    first = []
    for k in range(1, n):
        peer = lax.rem(me + k, n)
        copy = pltpu.make_async_remote_copy(
            src_ref=block(x_ref, peer),
            dst_ref=slots.at[k],
            send_sem=send1.at[k],
            recv_sem=recv1.at[k],
            device_id=(row, peer),
            device_id_type=MESH,
        )
        copy.start()
        first.append(copy)
    for copy in first:
        copy.wait()
    total = block(x_ref, me)[...].astype(jnp.float32)
    for k in range(1, n):
        total = total + slots[k].astype(jnp.float32)
    reduced[...] = total.astype(reduced.dtype)
    block(out_ref, me)[...] = reduced[...]

    second = []
    for k in range(1, n):
        peer = lax.rem(me + k, n)
        copy = pltpu.make_async_remote_copy(
            src_ref=reduced,
            dst_ref=block(out_ref, me),
            send_sem=send2.at[k],
            recv_sem=recv2.at[k],
            device_id=(row, peer),
            device_id_type=MESH,
        )
        copy.start()
        second.append(copy)
    for copy in second:
        copy.wait()


def tp_sum4_kernel(x_ref, out_ref, slots, relay, reduced, send_sem, recv_sem):
    n = 4
    me = lax.axis_index("tp")
    row = lax.axis_index("seq")
    cols = x_ref.shape[1] // n
    half = cols // 2
    right, left, far = lax.rem(me + 1, n), lax.rem(me + n - 1, n), lax.rem(me + 2, n)

    barrier = pltpu.get_barrier_semaphore()
    for k in range(1, n):
        pl.semaphore_signal(barrier, inc=1, device_id=(row, lax.rem(me + k, n)), device_id_type=MESH)
    pl.semaphore_wait(barrier, n - 1)

    def block(ref, owner):
        return ref.at[:, pl.ds(pl.multiple_of(owner * cols, cols), cols)]

    def part(ref, lo):
        return ref.at[:, lo : lo + half]

    def copy(src, dst, index, device):
        c = pltpu.make_async_remote_copy(
            src_ref=src,
            dst_ref=dst,
            send_sem=send_sem.at[index],
            recv_sem=recv_sem.at[index],
            device_id=(row, device),
            device_id_type=MESH,
        )
        c.start()
        return c

    def exchange(phase, src_of, dst_of, relay_base):
        s = phase * 6
        base = relay_base
        direct = [
            copy(src_of(right), dst_of(me, 1), s + 0, right),
            copy(src_of(left), dst_of(me, 3), s + 1, left),
        ]
        first = [
            copy(part(src_of(far), 0), relay.at[base + 0], s + 2, right),
            copy(part(src_of(far), half), relay.at[base + 1], s + 3, left),
        ]
        for c in first:
            c.wait()
        second = [
            copy(relay.at[base + 0], part(dst_of(left, 2), 0), s + 4, right),
            copy(relay.at[base + 1], part(dst_of(right, 2), half), s + 5, left),
        ]
        for c in direct + second:
            c.wait()

    exchange(0, lambda peer: block(x_ref, peer), lambda origin, k: slots.at[k], 0)
    total = block(x_ref, me)[...].astype(jnp.float32)
    for k in range(1, n):
        total = total + slots[k].astype(jnp.float32)
    reduced[...] = total.astype(reduced.dtype)
    block(out_ref, me)[...] = reduced[...]
    exchange(1, lambda peer: reduced, lambda origin, k: block(out_ref, origin), 2)


def tp_sum(x, collective_id):
    n = lax.axis_size("tp")
    rows, width = x.shape
    cols = width // n
    if n == 4 and cols % 256 == 0:
        return pl.pallas_call(
            tp_sum4_kernel,
            out_shape=jax.ShapeDtypeStruct((rows, width), x.dtype),
            in_specs=[pl.BlockSpec(memory_space=pltpu.VMEM)],
            out_specs=pl.BlockSpec(memory_space=pltpu.VMEM),
            scratch_shapes=[
                pltpu.VMEM((n, rows, cols), x.dtype),
                pltpu.VMEM((4, rows, cols // 2), x.dtype),
                pltpu.VMEM((rows, cols), x.dtype),
                pltpu.SemaphoreType.DMA((12,)),
                pltpu.SemaphoreType.DMA((12,)),
            ],
            compiler_params=pltpu.CompilerParams(collective_id=collective_id, has_side_effects=True),
        )(x)
    return pl.pallas_call(
        functools.partial(tp_sum_kernel, n),
        out_shape=jax.ShapeDtypeStruct((rows, width), x.dtype),
        in_specs=[pl.BlockSpec(memory_space=pltpu.VMEM)],
        out_specs=pl.BlockSpec(memory_space=pltpu.VMEM),
        scratch_shapes=[
            pltpu.VMEM((n, rows, cols), x.dtype),
            pltpu.VMEM((rows, cols), x.dtype),
            pltpu.SemaphoreType.DMA((n,)),
            pltpu.SemaphoreType.DMA((n,)),
            pltpu.SemaphoreType.DMA((n,)),
            pltpu.SemaphoreType.DMA((n,)),
        ],
        compiler_params=pltpu.CompilerParams(collective_id=collective_id, has_side_effects=True),
    )(x)


def attention_kernel(info, q_ref, q_last_ref, q_first_ref, kv_ref, o_ref, top_ref, total_ref, acc_ref):
    step = pl.program_id(0)
    groups, rows_all, head_size = q_ref.shape
    shards_per, both, _ = kv_ref.shape
    rows = both // 2
    width = shards_per * rows
    rows_q = o_ref.shape[0]
    per_group = rows_all // rows_q
    scale = 1.0 / math.sqrt(head_size)

    @pl.when(step == 0)
    def _():
        top_ref[...] = jnp.full(top_ref.shape, -1e30, jnp.float32)
        total_ref[...] = jnp.zeros(total_ref.shape, jnp.float32)
        acc_ref[...] = jnp.zeros(acc_ref.shape, jnp.float32)

    offset = step * width
    needed = (step >= info[0]) & (step <= info[1])
    whole = (offset >= info[2]) & (offset + width - 1 <= info[3])

    def run(masked):
        for g in range(groups):
            q = q_ref[g]
            k = kv_ref[:, :rows, g * head_size : (g + 1) * head_size].reshape(width, head_size)
            v = kv_ref[:, rows:, g * head_size : (g + 1) * head_size].reshape(width, head_size)
            s = lax.dot_general(q, k, (((1,), (1,)), ((), ())), preferred_element_type=jnp.float32) * scale
            if masked:
                k_index = offset + lax.broadcasted_iota(jnp.int32, s.shape, 1)
                allowed = (k_index <= q_last_ref[...]) & (k_index >= q_first_ref[...])
                s = jnp.where(allowed, s, -1e30)
            top = top_ref[g]
            new_top = jnp.maximum(top, jnp.max(s, axis=-1, keepdims=True))
            p = jnp.exp(s - new_top)
            if masked:
                p = jnp.where(allowed, p, 0.0)
            decay = jnp.exp(top - new_top)
            total_ref[g] = total_ref[g] * decay + jnp.sum(p, axis=-1, keepdims=True)
            acc_ref[g] = acc_ref[g] * decay + jnp.dot(
                p.astype(jnp.bfloat16), v, preferred_element_type=jnp.float32
            )
            top_ref[g] = new_top

    @pl.when(needed & whole)
    def _():
        run(False)

    @pl.when(needed & jnp.logical_not(whole))
    def _():
        run(True)

    @pl.when(step == pl.num_programs(0) - 1)
    def _():
        for g in range(groups):
            out = acc_ref[g] / total_ref[g]
            for h in range(per_group):
                col = (g * per_group + h) * head_size
                o_ref[:, col : col + head_size] = out[h * rows_q : (h + 1) * rows_q].astype(o_ref.dtype)


def attention(q_grouped, q_last, q_first, gathered, info, rows, kv_rows_per_shard, shards_per):
    groups, rows_all, head_size = q_grouped.shape
    shards, _, width_all = gathered.shape
    blocks = shards // shards_per
    out_cols = rows_all // rows * groups * head_size

    def kv_map(j, info):
        return (jnp.minimum(jnp.maximum(j, info[0]), info[1]), 0, 0)

    grid_spec = pltpu.PrefetchScalarGridSpec(
        num_scalar_prefetch=1,
        grid=(blocks,),
        in_specs=[
            pl.BlockSpec((groups, rows_all, head_size), lambda j, info: (0, 0, 0)),
            pl.BlockSpec((rows_all, 1), lambda j, info: (0, 0)),
            pl.BlockSpec((rows_all, 1), lambda j, info: (0, 0)),
            pl.BlockSpec((shards_per, kv_rows_per_shard, width_all), kv_map),
        ],
        out_specs=pl.BlockSpec((rows, out_cols), lambda j, info: (0, 0)),
        scratch_shapes=[
            pltpu.VMEM((groups, rows_all, 1), jnp.float32),
            pltpu.VMEM((groups, rows_all, 1), jnp.float32),
            pltpu.VMEM((groups, rows_all, head_size), jnp.float32),
        ],
    )
    return pl.pallas_call(
        attention_kernel,
        out_shape=jax.ShapeDtypeStruct((rows, out_cols), jnp.bfloat16),
        grid_spec=grid_spec,
        compiler_params=pltpu.CompilerParams(dimension_semantics=("arbitrary",)),
    )(info, q_grouped, q_last, q_first, gathered)


def body(
    layer_input,
    norm_gain,
    w_query,
    key_weight,
    value_weight,
    w_out,
    query_gain,
    key_gain,
    seg_ids,
    positions,
    post_gain,
    w_gate,
    w_up,
    w_down,
):
    rows = layer_input.shape[0]
    head_size = query_gain.shape[0]
    query_local = w_query.shape[1] // head_size
    kv_local = key_weight.shape[1] // head_size
    kv_cols = kv_local * head_size
    head_group = query_local // kv_local
    scale = 1.0 / math.sqrt(head_size)
    shards = lax.axis_size("seq")
    xf = layer_input.astype(jnp.float32)
    normed_input = rms(xf, norm_gain).astype(jnp.bfloat16)
    query_matrix = jnp.dot(normed_input, w_query, preferred_element_type=jnp.float32).reshape(
        rows, query_local, head_size
    )
    query_matrix = rope(rms(query_matrix, query_gain), positions).astype(jnp.bfloat16)
    key_matrix = jnp.dot(normed_input, key_weight, preferred_element_type=jnp.float32).reshape(
        rows, kv_local, head_size
    )
    key_matrix = rope(rms(key_matrix, key_gain), positions).astype(jnp.bfloat16)
    key_cache = key_matrix.reshape(rows, kv_cols)
    value_cache = jnp.dot(normed_input, value_weight, preferred_element_type=jnp.float32).astype(
        jnp.bfloat16
    )

    width_all = 2 * kv_cols
    ff_rows, ff_local = w_gate.shape
    rest = ff_local - width_all
    down_t = w_down.T
    kv_packed = jnp.concatenate([key_cache, value_cache], axis=0)
    kv_gathered = lax.all_gather(kv_packed, "seq", axis=0, tiled=False)
    weights_packed = jnp.concatenate(
        [
            w_gate[:, :width_all],
            w_up[:, :width_all],
            down_t[:, :width_all],
            jnp.concatenate([w_gate[:, width_all:], w_up[:, width_all:]], axis=1),
            jnp.concatenate(
                [down_t[:, width_all:], jnp.zeros((ff_rows, 2 * width_all - ff_local), down_t.dtype)],
                axis=1,
            ),
        ],
        axis=0,
    )

    def weight_part(k, lo, hi):
        top = k * ff_rows
        return w_gathered[:, top : top + ff_rows, lo:hi].reshape(shards * ff_rows, hi - lo)


    me = lax.axis_index("seq")
    first = me * rows
    my_last = first + rows - 1
    q_index = first + jnp.arange(rows, dtype=jnp.int32)
    q_start = q_index - positions
    shards_per = 1
    for trial in range(1, max(1, 1024 // rows) + 1):
        if shards % trial == 0:
            shards_per = trial
    width = rows * shards_per
    info = jnp.stack([q_start[0] // width, my_last // width, q_start[rows - 1], first])
    q_grouped = (
        query_matrix.reshape(rows, kv_local, head_group, head_size)
        .transpose(1, 2, 0, 3)
        .reshape(kv_local, head_group * rows, head_size)
    )
    q_last = jnp.tile(q_index, head_group).reshape(head_group * rows, 1)
    q_first = jnp.tile(q_start, head_group).reshape(head_group * rows, 1)
    kv_gathered, weights_packed, q_grouped, q_last, q_first, info = lax.optimization_barrier(
        (kv_gathered, weights_packed, q_grouped, q_last, q_first, info)
    )
    w_gathered = lax.all_gather(weights_packed, "seq", axis=0, tiled=False)
    gate_a = weight_part(0, 0, width_all)
    up_a = weight_part(1, 0, width_all)
    down_a = weight_part(2, 0, width_all)
    gate_b = weight_part(3, 0, rest)
    up_b = weight_part(3, rest, 2 * rest)
    down_b = weight_part(4, 0, rest)
    attended = attention(q_grouped, q_last, q_first, kv_gathered, info, rows, 2 * rows, shards_per)
    partial_out = jnp.dot(attended, w_out, preferred_element_type=jnp.float32)
    summed = tp_sum(partial_out.astype(jnp.bfloat16), 0).astype(jnp.float32)
    mid = (xf + summed).astype(jnp.bfloat16)
    mid_f = mid.astype(jnp.float32)
    post_normed = rms(mid_f, post_gain).astype(jnp.bfloat16)
    def ffn_piece(gate_w, up_w, down_w):
        gate = jnp.dot(post_normed, gate_w, preferred_element_type=jnp.float32)
        up = jnp.dot(post_normed, up_w, preferred_element_type=jnp.float32)
        act = (jax.nn.silu(gate) * up).astype(jnp.bfloat16)
        return lax.dot_general(
            act, down_w, (((1,), (1,)), ((), ())), preferred_element_type=jnp.float32
        )

    terms = ffn_piece(gate_a, up_a, down_a) + ffn_piece(gate_b, up_b, down_b)
    ffn_total = tp_sum(terms.astype(jnp.bfloat16), 1).astype(jnp.float32)
    hidden = (mid_f + ffn_total).astype(jnp.bfloat16)
    return (hidden, key_cache, value_cache)


def solution(mesh):
    in_specs = (
        P("seq", None),
        P(),
        P(None, "tp"),
        P(None, "tp"),
        P(None, "tp"),
        P("tp", None),
        P(),
        P(),
        P("seq"),
        P("seq"),
        P(),
        P("seq", "tp"),
        P("seq", "tp"),
        P("tp", "seq"),
    )
    out_specs = (P("seq", None), P("seq", "tp"), P("seq", "tp"))
    return jax.shard_map(body, mesh=mesh, in_specs=in_specs, out_specs=out_specs, check_vma=False)
```

```python
import functools
import math

import jax
import jax.numpy as jnp
from jax import lax
from jax.experimental import pallas as pl
from jax.experimental.pallas import tpu as pltpu
from jax.sharding import PartitionSpec as P

MESH = pl.DeviceIdType.MESH


def rms(v, gain):
    return v * lax.rsqrt(jnp.mean(v * v, axis=-1, keepdims=True) + 1e-06) * gain


def rope(v, place):
    half = v.shape[-1] // 2
    freqs = 1000000.0 ** (-2.0 * jnp.arange(half, dtype=jnp.float32) / v.shape[-1])
    angle = place.astype(jnp.float32)[:, None] * freqs[None, :]
    cosine = jnp.cos(angle)[:, None, :]
    sine = jnp.sin(angle)[:, None, :]
    block_start = v[..., :half]
    second = v[..., half:]
    return jnp.concatenate(
        [block_start * cosine - second * sine, second * cosine + block_start * sine], axis=-1
    )


def tp_sum_kernel(n, x_ref, out_ref, slots, reduced, send1, recv1, send2, recv2):
    me = lax.axis_index("tp")
    row = lax.axis_index("seq")
    cols = x_ref.shape[1] // n

    barrier = pltpu.get_barrier_semaphore()
    for k in range(1, n):
        pl.semaphore_signal(barrier, inc=1, device_id=(row, lax.rem(me + k, n)), device_id_type=MESH)
    pl.semaphore_wait(barrier, n - 1)

    def block(ref, owner):
        return ref.at[:, pl.ds(pl.multiple_of(owner * cols, cols), cols)]

    first = []
    for k in range(1, n):
        peer = lax.rem(me + k, n)
        copy = pltpu.make_async_remote_copy(
            src_ref=block(x_ref, peer),
            dst_ref=slots.at[k],
            send_sem=send1.at[k],
            recv_sem=recv1.at[k],
            device_id=(row, peer),
            device_id_type=MESH,
        )
        copy.start()
        first.append(copy)
    for copy in first:
        copy.wait()
    total = block(x_ref, me)[...].astype(jnp.float32)
    for k in range(1, n):
        total = total + slots[k].astype(jnp.float32)
    reduced[...] = total.astype(reduced.dtype)
    block(out_ref, me)[...] = reduced[...]

    second = []
    for k in range(1, n):
        peer = lax.rem(me + k, n)
        copy = pltpu.make_async_remote_copy(
            src_ref=reduced,
            dst_ref=block(out_ref, me),
            send_sem=send2.at[k],
            recv_sem=recv2.at[k],
            device_id=(row, peer),
            device_id_type=MESH,
        )
        copy.start()
        second.append(copy)
    for copy in second:
        copy.wait()


def tp_sum(x, collective_id):
    n = lax.axis_size("tp")
    rows, width = x.shape
    cols = width // n
    return pl.pallas_call(
        functools.partial(tp_sum_kernel, n),
        out_shape=jax.ShapeDtypeStruct((rows, width), x.dtype),
        in_specs=[pl.BlockSpec(memory_space=pltpu.VMEM)],
        out_specs=pl.BlockSpec(memory_space=pltpu.VMEM),
        scratch_shapes=[
            pltpu.VMEM((n, rows, cols), x.dtype),
            pltpu.VMEM((rows, cols), x.dtype),
            pltpu.SemaphoreType.DMA((n,)),
            pltpu.SemaphoreType.DMA((n,)),
            pltpu.SemaphoreType.DMA((n,)),
            pltpu.SemaphoreType.DMA((n,)),
        ],
        compiler_params=pltpu.CompilerParams(collective_id=collective_id, has_side_effects=True),
    )(x)


def attention_kernel(info, q_ref, q_last_ref, q_first_ref, kv_ref, o_ref, top_ref, total_ref, acc_ref):
    step = pl.program_id(0)
    groups, rows_all, head_size = q_ref.shape
    shards_per, both, _ = kv_ref.shape
    rows = both // 2
    width = shards_per * rows
    rows_q = o_ref.shape[0]
    per_group = rows_all // rows_q
    scale = 1.0 / math.sqrt(head_size)

    @pl.when(step == 0)
    def _():
        top_ref[...] = jnp.full(top_ref.shape, -1e30, jnp.float32)
        total_ref[...] = jnp.zeros(total_ref.shape, jnp.float32)
        acc_ref[...] = jnp.zeros(acc_ref.shape, jnp.float32)

    offset = step * width
    needed = (step >= info[0]) & (step <= info[1])
    whole = (offset >= info[2]) & (offset + width - 1 <= info[3])

    def run(masked):
        for g in range(groups):
            q = q_ref[g]
            k = kv_ref[:, :rows, g * head_size : (g + 1) * head_size].reshape(width, head_size)
            v = kv_ref[:, rows:, g * head_size : (g + 1) * head_size].reshape(width, head_size)
            s = lax.dot_general(q, k, (((1,), (1,)), ((), ())), preferred_element_type=jnp.float32) * scale
            if masked:
                k_index = offset + lax.broadcasted_iota(jnp.int32, s.shape, 1)
                allowed = (k_index <= q_last_ref[...]) & (k_index >= q_first_ref[...])
                s = jnp.where(allowed, s, -1e30)
            top = top_ref[g]
            new_top = jnp.maximum(top, jnp.max(s, axis=-1, keepdims=True))
            p = jnp.exp(s - new_top)
            if masked:
                p = jnp.where(allowed, p, 0.0)
            decay = jnp.exp(top - new_top)
            total_ref[g] = total_ref[g] * decay + jnp.sum(p, axis=-1, keepdims=True)
            acc_ref[g] = acc_ref[g] * decay + jnp.dot(
                p.astype(jnp.bfloat16), v, preferred_element_type=jnp.float32
            )
            top_ref[g] = new_top

    @pl.when(needed & whole)
    def _():
        run(False)

    @pl.when(needed & jnp.logical_not(whole))
    def _():
        run(True)

    @pl.when(step == pl.num_programs(0) - 1)
    def _():
        for g in range(groups):
            out = acc_ref[g] / total_ref[g]
            for h in range(per_group):
                col = (g * per_group + h) * head_size
                o_ref[:, col : col + head_size] = out[h * rows_q : (h + 1) * rows_q].astype(o_ref.dtype)


def attention(q_grouped, q_last, q_first, gathered, info, rows, kv_rows_per_shard, shards_per):
    groups, rows_all, head_size = q_grouped.shape
    shards, _, width_all = gathered.shape
    blocks = shards // shards_per
    out_cols = rows_all // rows * groups * head_size

    def kv_map(j, info):
        return (jnp.minimum(jnp.maximum(j, info[0]), info[1]), 0, 0)

    grid_spec = pltpu.PrefetchScalarGridSpec(
        num_scalar_prefetch=1,
        grid=(blocks,),
        in_specs=[
            pl.BlockSpec((groups, rows_all, head_size), lambda j, info: (0, 0, 0)),
            pl.BlockSpec((rows_all, 1), lambda j, info: (0, 0)),
            pl.BlockSpec((rows_all, 1), lambda j, info: (0, 0)),
            pl.BlockSpec((shards_per, kv_rows_per_shard, width_all), kv_map),
        ],
        out_specs=pl.BlockSpec((rows, out_cols), lambda j, info: (0, 0)),
        scratch_shapes=[
            pltpu.VMEM((groups, rows_all, 1), jnp.float32),
            pltpu.VMEM((groups, rows_all, 1), jnp.float32),
            pltpu.VMEM((groups, rows_all, head_size), jnp.float32),
        ],
    )
    return pl.pallas_call(
        attention_kernel,
        out_shape=jax.ShapeDtypeStruct((rows, out_cols), jnp.bfloat16),
        grid_spec=grid_spec,
        compiler_params=pltpu.CompilerParams(dimension_semantics=("arbitrary",)),
    )(info, q_grouped, q_last, q_first, gathered)


def body(
    layer_input,
    norm_gain,
    w_query,
    key_weight,
    value_weight,
    w_out,
    query_gain,
    key_gain,
    seg_ids,
    positions,
    post_gain,
    w_gate,
    w_up,
    w_down,
):
    rows = layer_input.shape[0]
    head_size = query_gain.shape[0]
    query_local = w_query.shape[1] // head_size
    kv_local = key_weight.shape[1] // head_size
    kv_cols = kv_local * head_size
    head_group = query_local // kv_local
    scale = 1.0 / math.sqrt(head_size)
    shards = lax.axis_size("seq")
    xf = layer_input.astype(jnp.float32)
    normed_input = rms(xf, norm_gain).astype(jnp.bfloat16)
    query_matrix = jnp.dot(normed_input, w_query, preferred_element_type=jnp.float32).reshape(
        rows, query_local, head_size
    )
    query_matrix = rope(rms(query_matrix, query_gain), positions).astype(jnp.bfloat16)
    key_matrix = jnp.dot(normed_input, key_weight, preferred_element_type=jnp.float32).reshape(
        rows, kv_local, head_size
    )
    key_matrix = rope(rms(key_matrix, key_gain), positions).astype(jnp.bfloat16)
    key_cache = key_matrix.reshape(rows, kv_cols)
    value_cache = jnp.dot(normed_input, value_weight, preferred_element_type=jnp.float32).astype(
        jnp.bfloat16
    )

    width_all = 2 * kv_cols
    ff_rows, ff_local = w_gate.shape
    rest = ff_local - width_all
    down_t = w_down.T
    kv_packed = jnp.concatenate([key_cache, value_cache], axis=0)
    kv_gathered = lax.all_gather(kv_packed, "seq", axis=0, tiled=False)
    pad = -(3 * ff_local) % width_all
    weights_packed = jnp.concatenate(
        [w_gate, w_up, down_t, jnp.zeros((ff_rows, pad), down_t.dtype)], axis=1
    )

    me = lax.axis_index("seq")
    first = me * rows
    my_last = first + rows - 1
    q_index = first + jnp.arange(rows, dtype=jnp.int32)
    q_start = q_index - positions
    shards_per = 1
    for trial in range(1, max(1, 1024 // rows) + 1):
        if shards % trial == 0:
            shards_per = trial
    width = rows * shards_per
    info = jnp.stack([q_start[0] // width, my_last // width, q_start[rows - 1], first])
    q_grouped = (
        query_matrix.reshape(rows, kv_local, head_group, head_size)
        .transpose(1, 2, 0, 3)
        .reshape(kv_local, head_group * rows, head_size)
    )
    q_last = jnp.tile(q_index, head_group).reshape(head_group * rows, 1)
    q_first = jnp.tile(q_start, head_group).reshape(head_group * rows, 1)
    kv_gathered, weights_packed, q_grouped, q_last, q_first, info = lax.optimization_barrier(
        (kv_gathered, weights_packed, q_grouped, q_last, q_first, info)
    )
    w_gathered = lax.all_gather(weights_packed, "seq", axis=0, tiled=False).reshape(
        shards * ff_rows, weights_packed.shape[1]
    )
    attended = attention(q_grouped, q_last, q_first, kv_gathered, info, rows, 2 * rows, shards_per)
    partial_out = jnp.dot(attended, w_out, preferred_element_type=jnp.float32)
    summed = tp_sum(partial_out.astype(jnp.bfloat16), 0).astype(jnp.float32)
    mid = (xf + summed).astype(jnp.bfloat16)
    mid_f = mid.astype(jnp.float32)
    post_normed = rms(mid_f, post_gain).astype(jnp.bfloat16)
    gate_up = jnp.dot(post_normed, w_gathered[:, : 2 * ff_local], preferred_element_type=jnp.float32)
    act = (jax.nn.silu(gate_up[:, :ff_local]) * gate_up[:, ff_local:]).astype(jnp.bfloat16)
    terms = lax.dot_general(
        act,
        w_gathered[:, 2 * ff_local : 3 * ff_local],
        (((1,), (1,)), ((), ())),
        preferred_element_type=jnp.float32,
    )
    ffn_total = tp_sum(terms.astype(jnp.bfloat16), 1).astype(jnp.float32)
    hidden = (mid_f + ffn_total).astype(jnp.bfloat16)
    return (hidden, key_cache, value_cache)


def solution(mesh):
    in_specs = (
        P("seq", None),
        P(),
        P(None, "tp"),
        P(None, "tp"),
        P(None, "tp"),
        P("tp", None),
        P(),
        P(),
        P("seq"),
        P("seq"),
        P(),
        P("seq", "tp"),
        P("seq", "tp"),
        P("tp", "seq"),
    )
    out_specs = (P("seq", None), P("seq", "tp"), P("seq", "tp"))
    return jax.shard_map(body, mesh=mesh, in_specs=in_specs, out_specs=out_specs, check_vma=False)
```

```python
import functools
import math

import jax
import jax.numpy as jnp
from jax import lax
from jax.experimental import pallas as pl
from jax.experimental.pallas import tpu as pltpu
from jax.sharding import PartitionSpec as P

MESH = pl.DeviceIdType.MESH


def rms(v, gain):
    return v * lax.rsqrt(jnp.mean(v * v, axis=-1, keepdims=True) + 1e-06) * gain


def rope(v, place):
    half = v.shape[-1] // 2
    freqs = 1000000.0 ** (-2.0 * jnp.arange(half, dtype=jnp.float32) / v.shape[-1])
    angle = place.astype(jnp.float32)[:, None] * freqs[None, :]
    cosine = jnp.cos(angle)[:, None, :]
    sine = jnp.sin(angle)[:, None, :]
    block_start = v[..., :half]
    second = v[..., half:]
    return jnp.concatenate(
        [block_start * cosine - second * sine, second * cosine + block_start * sine], axis=-1
    )


def tp_sum_kernel(n, x_ref, out_ref, slots, reduced, send1, recv1, send2, recv2):
    me = lax.axis_index("tp")
    row = lax.axis_index("seq")
    cols = x_ref.shape[1] // n

    barrier = pltpu.get_barrier_semaphore()
    for k in range(1, n):
        pl.semaphore_signal(barrier, inc=1, device_id=(row, lax.rem(me + k, n)), device_id_type=MESH)
    pl.semaphore_wait(barrier, n - 1)

    def block(ref, owner):
        return ref.at[:, pl.ds(pl.multiple_of(owner * cols, cols), cols)]

    first = []
    for k in range(1, n):
        peer = lax.rem(me + k, n)
        copy = pltpu.make_async_remote_copy(
            src_ref=block(x_ref, peer),
            dst_ref=slots.at[k],
            send_sem=send1.at[k],
            recv_sem=recv1.at[k],
            device_id=(row, peer),
            device_id_type=MESH,
        )
        copy.start()
        first.append(copy)
    for copy in first:
        copy.wait()
    total = block(x_ref, me)[...].astype(jnp.float32)
    for k in range(1, n):
        total = total + slots[k].astype(jnp.float32)
    reduced[...] = total.astype(reduced.dtype)
    block(out_ref, me)[...] = reduced[...]

    second = []
    for k in range(1, n):
        peer = lax.rem(me + k, n)
        copy = pltpu.make_async_remote_copy(
            src_ref=reduced,
            dst_ref=block(out_ref, me),
            send_sem=send2.at[k],
            recv_sem=recv2.at[k],
            device_id=(row, peer),
            device_id_type=MESH,
        )
        copy.start()
        second.append(copy)
    for copy in second:
        copy.wait()


def tp_sum(x, collective_id):
    n = lax.axis_size("tp")
    rows, width = x.shape
    cols = width // n
    return pl.pallas_call(
        functools.partial(tp_sum_kernel, n),
        out_shape=jax.ShapeDtypeStruct((rows, width), x.dtype),
        in_specs=[pl.BlockSpec(memory_space=pltpu.VMEM)],
        out_specs=pl.BlockSpec(memory_space=pltpu.VMEM),
        scratch_shapes=[
            pltpu.VMEM((n, rows, cols), x.dtype),
            pltpu.VMEM((rows, cols), x.dtype),
            pltpu.SemaphoreType.DMA((n,)),
            pltpu.SemaphoreType.DMA((n,)),
            pltpu.SemaphoreType.DMA((n,)),
            pltpu.SemaphoreType.DMA((n,)),
        ],
        compiler_params=pltpu.CompilerParams(collective_id=collective_id, has_side_effects=True),
    )(x)


def attention_kernel(info, q_ref, q_last_ref, q_first_ref, kv_ref, o_ref, top_ref, total_ref, acc_ref):
    step = pl.program_id(0)
    groups, rows_all, head_size = q_ref.shape
    shards_per, both, _ = kv_ref.shape
    rows = both // 2
    width = shards_per * rows
    rows_q = o_ref.shape[0]
    per_group = rows_all // rows_q
    scale = 1.0 / math.sqrt(head_size)

    @pl.when(step == 0)
    def _():
        top_ref[...] = jnp.full(top_ref.shape, -1e30, jnp.float32)
        total_ref[...] = jnp.zeros(total_ref.shape, jnp.float32)
        acc_ref[...] = jnp.zeros(acc_ref.shape, jnp.float32)

    offset = step * width
    needed = (step >= info[0]) & (step <= info[1])
    whole = (offset >= info[2]) & (offset + width - 1 <= info[3])

    def run(masked):
        for g in range(groups):
            q = q_ref[g]
            k = kv_ref[:, :rows, g * head_size : (g + 1) * head_size].reshape(width, head_size)
            v = kv_ref[:, rows:, g * head_size : (g + 1) * head_size].reshape(width, head_size)
            s = lax.dot_general(q, k, (((1,), (1,)), ((), ())), preferred_element_type=jnp.float32) * scale
            if masked:
                k_index = offset + lax.broadcasted_iota(jnp.int32, s.shape, 1)
                allowed = (k_index <= q_last_ref[:, :1]) & (k_index >= q_first_ref[:, :1])
                s = jnp.where(allowed, s, -1e30)
            top = top_ref[g]
            new_top = jnp.maximum(top, jnp.max(s, axis=-1, keepdims=True))
            p = jnp.exp(s - new_top)
            if masked:
                p = jnp.where(allowed, p, 0.0)
            decay = jnp.exp(top - new_top)
            total_ref[g] = total_ref[g] * decay + jnp.sum(p, axis=-1, keepdims=True)
            acc_ref[g] = acc_ref[g] * decay + jnp.dot(
                p.astype(jnp.bfloat16), v, preferred_element_type=jnp.float32
            )
            top_ref[g] = new_top

    @pl.when(needed & whole)
    def _():
        run(False)

    @pl.when(needed & jnp.logical_not(whole))
    def _():
        run(True)

    @pl.when(step == pl.num_programs(0) - 1)
    def _():
        for g in range(groups):
            out = acc_ref[g] / total_ref[g]
            for h in range(per_group):
                col = (g * per_group + h) * head_size
                o_ref[:, col : col + head_size] = out[h * rows_q : (h + 1) * rows_q].astype(o_ref.dtype)


def attention(q_grouped, q_last, q_first, gathered, info, rows, kv_rows_per_shard, shards_per):
    groups, rows_all, head_size = q_grouped.shape
    shards, _, width_all = gathered.shape
    blocks = shards // shards_per
    out_cols = rows_all // rows * groups * head_size

    def kv_map(j, info):
        return (jnp.minimum(jnp.maximum(j, info[0]), info[1]), 0, 0)

    grid_spec = pltpu.PrefetchScalarGridSpec(
        num_scalar_prefetch=1,
        grid=(blocks,),
        in_specs=[
            pl.BlockSpec((groups, rows_all, head_size), lambda j, info: (0, 0, 0)),
            pl.BlockSpec(q_last.shape, lambda j, info: (0, 0)),
            pl.BlockSpec(q_first.shape, lambda j, info: (0, 0)),
            pl.BlockSpec((shards_per, kv_rows_per_shard, width_all), kv_map),
        ],
        out_specs=pl.BlockSpec((rows, out_cols), lambda j, info: (0, 0)),
        scratch_shapes=[
            pltpu.VMEM((groups, rows_all, 1), jnp.float32),
            pltpu.VMEM((groups, rows_all, 1), jnp.float32),
            pltpu.VMEM((groups, rows_all, head_size), jnp.float32),
        ],
    )
    return pl.pallas_call(
        attention_kernel,
        out_shape=jax.ShapeDtypeStruct((rows, out_cols), jnp.bfloat16),
        grid_spec=grid_spec,
        compiler_params=pltpu.CompilerParams(dimension_semantics=("arbitrary",)),
    )(info, q_grouped, q_last, q_first, gathered)


def body(
    layer_input,
    norm_gain,
    w_query,
    key_weight,
    value_weight,
    w_out,
    query_gain,
    key_gain,
    seg_ids,
    positions,
    post_gain,
    w_gate,
    w_up,
    w_down,
):
    rows = layer_input.shape[0]
    head_size = query_gain.shape[0]
    query_local = w_query.shape[1] // head_size
    kv_local = key_weight.shape[1] // head_size
    kv_cols = kv_local * head_size
    head_group = query_local // kv_local
    scale = 1.0 / math.sqrt(head_size)
    shards = lax.axis_size("seq")
    xf = layer_input.astype(jnp.float32)
    normed_input = rms(xf, norm_gain).astype(jnp.bfloat16)
    query_matrix = jnp.dot(normed_input, w_query, preferred_element_type=jnp.float32).reshape(
        rows, query_local, head_size
    )
    query_matrix = rope(rms(query_matrix, query_gain), positions).astype(jnp.bfloat16)
    key_matrix = jnp.dot(normed_input, key_weight, preferred_element_type=jnp.float32).reshape(
        rows, kv_local, head_size
    )
    key_matrix = rope(rms(key_matrix, key_gain), positions).astype(jnp.bfloat16)
    key_cache = key_matrix.reshape(rows, kv_cols)
    value_cache = jnp.dot(normed_input, value_weight, preferred_element_type=jnp.float32).astype(
        jnp.bfloat16
    )

    width_all = 2 * kv_cols
    ff_rows, ff_local = w_gate.shape
    rest = ff_local - width_all
    down_t = w_down.T
    kv_packed = jnp.concatenate([key_cache, value_cache], axis=0)
    kv_gathered = lax.all_gather(kv_packed, "seq", axis=0, tiled=False)
    weights_packed = jnp.concatenate([w_gate, w_up, down_t], axis=1)

    me = lax.axis_index("seq")
    first = me * rows
    my_last = first + rows - 1
    q_index = first + jnp.arange(rows, dtype=jnp.int32)
    q_start = q_index - positions
    shards_per = 1
    for trial in range(1, max(1, 1024 // rows) + 1):
        if shards % trial == 0:
            shards_per = trial
    width = rows * shards_per
    info = jnp.stack([q_start[0] // width, my_last // width, q_start[rows - 1], first])
    q_grouped = (
        query_matrix.reshape(rows, kv_local, head_group, head_size)
        .transpose(1, 2, 0, 3)
        .reshape(kv_local, head_group * rows, head_size)
    )
    lanes = 128
    q_last = jnp.broadcast_to(jnp.tile(q_index, head_group)[:, None], (head_group * rows, lanes))
    q_first = jnp.broadcast_to(jnp.tile(q_start, head_group)[:, None], (head_group * rows, lanes))
    kv_gathered, weights_packed, q_grouped, q_last, q_first, info = lax.optimization_barrier(
        (kv_gathered, weights_packed, q_grouped, q_last, q_first, info)
    )
    w_gathered = lax.all_gather(weights_packed, "seq", axis=0, tiled=False).reshape(
        shards * ff_rows, weights_packed.shape[1]
    )
    attended = attention(q_grouped, q_last, q_first, kv_gathered, info, rows, 2 * rows, shards_per)
    partial_out = jnp.dot(attended, w_out, preferred_element_type=jnp.float32)
    summed = tp_sum(partial_out.astype(jnp.bfloat16), 0).astype(jnp.float32)
    mid = (xf + summed).astype(jnp.bfloat16)
    mid_f = mid.astype(jnp.float32)
    post_normed = rms(mid_f, post_gain).astype(jnp.bfloat16)
    gate_up = jnp.dot(post_normed, w_gathered[:, : 2 * ff_local], preferred_element_type=jnp.float32)
    act = (jax.nn.silu(gate_up[:, :ff_local]) * gate_up[:, ff_local:]).astype(jnp.bfloat16)
    terms = lax.dot_general(
        act,
        w_gathered[:, 2 * ff_local : 3 * ff_local],
        (((1,), (1,)), ((), ())),
        preferred_element_type=jnp.float32,
    )
    ffn_total = tp_sum(terms.astype(jnp.bfloat16), 1).astype(jnp.float32)
    hidden = (mid_f + ffn_total).astype(jnp.bfloat16)
    return (hidden, key_cache, value_cache)


def solution(mesh):
    in_specs = (
        P("seq", None),
        P(),
        P(None, "tp"),
        P(None, "tp"),
        P(None, "tp"),
        P("tp", None),
        P(),
        P(),
        P("seq"),
        P("seq"),
        P(),
        P("seq", "tp"),
        P("seq", "tp"),
        P("tp", "seq"),
    )
    out_specs = (P("seq", None), P("seq", "tp"), P("seq", "tp"))
    return jax.shard_map(body, mesh=mesh, in_specs=in_specs, out_specs=out_specs, check_vma=False)
```

```python
import functools
import math

import jax
import jax.numpy as jnp
from jax import lax
from jax.experimental import pallas as pl
from jax.experimental.pallas import tpu as pltpu
from jax.sharding import PartitionSpec as P

MESH = pl.DeviceIdType.MESH


def rms(v, gain):
    return v * lax.rsqrt(jnp.mean(v * v, axis=-1, keepdims=True) + 1e-06) * gain


def rope(v, place):
    half = v.shape[-1] // 2
    freqs = 1000000.0 ** (-2.0 * jnp.arange(half, dtype=jnp.float32) / v.shape[-1])
    angle = place.astype(jnp.float32)[:, None] * freqs[None, :]
    cosine = jnp.cos(angle)[:, None, :]
    sine = jnp.sin(angle)[:, None, :]
    block_start = v[..., :half]
    second = v[..., half:]
    return jnp.concatenate(
        [block_start * cosine - second * sine, second * cosine + block_start * sine], axis=-1
    )


def tp_sum_kernel(n, with_base, *refs):
    if with_base:
        x_ref, base_ref, out_ref, slots, reduced, send1, recv1, send2, recv2 = refs
    else:
        x_ref, out_ref, slots, reduced, send1, recv1, send2, recv2 = refs
    me = lax.axis_index("tp")
    row = lax.axis_index("seq")
    cols = x_ref.shape[1] // n

    barrier = pltpu.get_barrier_semaphore()
    for k in range(1, n):
        pl.semaphore_signal(barrier, inc=1, device_id=(row, lax.rem(me + k, n)), device_id_type=MESH)
    pl.semaphore_wait(barrier, n - 1)

    def block(ref, owner):
        return ref.at[:, pl.ds(pl.multiple_of(owner * cols, cols), cols)]

    first = []
    for k in range(1, n):
        peer = lax.rem(me + k, n)
        copy = pltpu.make_async_remote_copy(
            src_ref=block(x_ref, peer),
            dst_ref=slots.at[k],
            send_sem=send1.at[k],
            recv_sem=recv1.at[k],
            device_id=(row, peer),
            device_id_type=MESH,
        )
        copy.start()
        first.append(copy)
    for copy in first:
        copy.wait()
    total = block(x_ref, me)[...].astype(jnp.float32)
    for k in range(1, n):
        total = total + slots[k].astype(jnp.float32)
    reduced[...] = total.astype(reduced.dtype)
    block(out_ref, me)[...] = reduced[...]

    second = []
    for k in range(1, n):
        peer = lax.rem(me + k, n)
        copy = pltpu.make_async_remote_copy(
            src_ref=reduced,
            dst_ref=block(out_ref, me),
            send_sem=send2.at[k],
            recv_sem=recv2.at[k],
            device_id=(row, peer),
            device_id_type=MESH,
        )
        copy.start()
        second.append(copy)
    for copy in second:
        copy.wait()
    if with_base:
        out_ref[...] = (base_ref[...].astype(jnp.float32) + out_ref[...].astype(jnp.float32)).astype(
            out_ref.dtype
        )


def tp_sum(x, collective_id, base=None):
    n = lax.axis_size("tp")
    rows, width = x.shape
    cols = width // n
    operands = (x,) if base is None else (x, base)
    return pl.pallas_call(
        functools.partial(tp_sum_kernel, n, base is not None),
        out_shape=jax.ShapeDtypeStruct((rows, width), x.dtype),
        in_specs=[pl.BlockSpec(memory_space=pltpu.VMEM)] * len(operands),
        out_specs=pl.BlockSpec(memory_space=pltpu.VMEM),
        scratch_shapes=[
            pltpu.VMEM((n, rows, cols), x.dtype),
            pltpu.VMEM((rows, cols), x.dtype),
            pltpu.SemaphoreType.DMA((n,)),
            pltpu.SemaphoreType.DMA((n,)),
            pltpu.SemaphoreType.DMA((n,)),
            pltpu.SemaphoreType.DMA((n,)),
        ],
        compiler_params=pltpu.CompilerParams(collective_id=collective_id, has_side_effects=True),
    )(*operands)


def attention_kernel(info, q_ref, q_last_ref, q_first_ref, kv_ref, o_ref, top_ref, total_ref, acc_ref):
    step = pl.program_id(0)
    groups, rows_all, head_size = q_ref.shape
    shards_per, both, _ = kv_ref.shape
    rows = both // 2
    width = shards_per * rows
    rows_q = o_ref.shape[0]
    per_group = rows_all // rows_q
    scale = 1.0 / math.sqrt(head_size)

    @pl.when(step == 0)
    def _():
        top_ref[...] = jnp.full(top_ref.shape, -1e30, jnp.float32)
        total_ref[...] = jnp.zeros(total_ref.shape, jnp.float32)
        acc_ref[...] = jnp.zeros(acc_ref.shape, jnp.float32)

    offset = step * width
    needed = (step >= info[0]) & (step <= info[1])
    whole = (offset >= info[2]) & (offset + width - 1 <= info[3])

    def run(masked):
        for g in range(groups):
            q = q_ref[g]
            k = kv_ref[:, :rows, g * head_size : (g + 1) * head_size].reshape(width, head_size)
            v = kv_ref[:, rows:, g * head_size : (g + 1) * head_size].reshape(width, head_size)
            s = lax.dot_general(q, k, (((1,), (1,)), ((), ())), preferred_element_type=jnp.float32) * scale
            if masked:
                k_index = offset + lax.broadcasted_iota(jnp.int32, s.shape, 1)
                allowed = (k_index <= q_last_ref[:, :1]) & (k_index >= q_first_ref[:, :1])
                s = jnp.where(allowed, s, -1e30)
            top = top_ref[g]
            new_top = jnp.maximum(top, jnp.max(s, axis=-1, keepdims=True))
            p = jnp.exp(s - new_top)
            if masked:
                p = jnp.where(allowed, p, 0.0)
            decay = jnp.exp(top - new_top)
            total_ref[g] = total_ref[g] * decay + jnp.sum(p, axis=-1, keepdims=True)
            acc_ref[g] = acc_ref[g] * decay + jnp.dot(
                p.astype(jnp.bfloat16), v, preferred_element_type=jnp.float32
            )
            top_ref[g] = new_top

    @pl.when(needed & whole)
    def _():
        run(False)

    @pl.when(needed & jnp.logical_not(whole))
    def _():
        run(True)

    @pl.when(step == pl.num_programs(0) - 1)
    def _():
        for g in range(groups):
            out = acc_ref[g] / total_ref[g]
            for h in range(per_group):
                col = (g * per_group + h) * head_size
                o_ref[:, col : col + head_size] = out[h * rows_q : (h + 1) * rows_q].astype(o_ref.dtype)


def attention(q_grouped, q_last, q_first, gathered, info, rows, kv_rows_per_shard, shards_per):
    groups, rows_all, head_size = q_grouped.shape
    shards, _, width_all = gathered.shape
    blocks = shards // shards_per
    out_cols = rows_all // rows * groups * head_size

    def kv_map(j, info):
        return (jnp.minimum(jnp.maximum(j, info[0]), info[1]), 0, 0)

    grid_spec = pltpu.PrefetchScalarGridSpec(
        num_scalar_prefetch=1,
        grid=(blocks,),
        in_specs=[
            pl.BlockSpec((groups, rows_all, head_size), lambda j, info: (0, 0, 0)),
            pl.BlockSpec(q_last.shape, lambda j, info: (0, 0)),
            pl.BlockSpec(q_first.shape, lambda j, info: (0, 0)),
            pl.BlockSpec((shards_per, kv_rows_per_shard, width_all), kv_map),
        ],
        out_specs=pl.BlockSpec((rows, out_cols), lambda j, info: (0, 0)),
        scratch_shapes=[
            pltpu.VMEM((groups, rows_all, 1), jnp.float32),
            pltpu.VMEM((groups, rows_all, 1), jnp.float32),
            pltpu.VMEM((groups, rows_all, head_size), jnp.float32),
        ],
    )
    return pl.pallas_call(
        attention_kernel,
        out_shape=jax.ShapeDtypeStruct((rows, out_cols), jnp.bfloat16),
        grid_spec=grid_spec,
        compiler_params=pltpu.CompilerParams(dimension_semantics=("arbitrary",)),
    )(info, q_grouped, q_last, q_first, gathered)


def body(
    layer_input,
    norm_gain,
    w_query,
    key_weight,
    value_weight,
    w_out,
    query_gain,
    key_gain,
    seg_ids,
    positions,
    post_gain,
    w_gate,
    w_up,
    w_down,
):
    rows = layer_input.shape[0]
    head_size = query_gain.shape[0]
    query_local = w_query.shape[1] // head_size
    kv_local = key_weight.shape[1] // head_size
    kv_cols = kv_local * head_size
    head_group = query_local // kv_local
    scale = 1.0 / math.sqrt(head_size)
    shards = lax.axis_size("seq")
    xf = layer_input.astype(jnp.float32)
    normed_input = rms(xf, norm_gain).astype(jnp.bfloat16)
    query_matrix = jnp.dot(normed_input, w_query, preferred_element_type=jnp.float32).reshape(
        rows, query_local, head_size
    )
    query_matrix = rope(rms(query_matrix, query_gain), positions).astype(jnp.bfloat16)
    key_matrix = jnp.dot(normed_input, key_weight, preferred_element_type=jnp.float32).reshape(
        rows, kv_local, head_size
    )
    key_matrix = rope(rms(key_matrix, key_gain), positions).astype(jnp.bfloat16)
    key_cache = key_matrix.reshape(rows, kv_cols)
    value_cache = jnp.dot(normed_input, value_weight, preferred_element_type=jnp.float32).astype(
        jnp.bfloat16
    )

    width_all = 2 * kv_cols
    ff_rows, ff_local = w_gate.shape
    rest = ff_local - width_all
    down_t = w_down.T
    kv_packed = jnp.concatenate([key_cache, value_cache], axis=0)
    kv_gathered = lax.all_gather(kv_packed, "seq", axis=0, tiled=False)
    weights_packed = jnp.concatenate([w_gate, w_up, down_t], axis=1)

    me = lax.axis_index("seq")
    first = me * rows
    my_last = first + rows - 1
    q_index = first + jnp.arange(rows, dtype=jnp.int32)
    q_start = q_index - positions
    shards_per = 1
    for trial in range(1, max(1, 1024 // rows) + 1):
        if shards % trial == 0:
            shards_per = trial
    width = rows * shards_per
    info = jnp.stack([q_start[0] // width, my_last // width, q_start[rows - 1], first])
    q_grouped = (
        query_matrix.reshape(rows, kv_local, head_group, head_size)
        .transpose(1, 2, 0, 3)
        .reshape(kv_local, head_group * rows, head_size)
    )
    lanes = 128
    q_last = jnp.broadcast_to(jnp.tile(q_index, head_group)[:, None], (head_group * rows, lanes))
    q_first = jnp.broadcast_to(jnp.tile(q_start, head_group)[:, None], (head_group * rows, lanes))
    kv_gathered, weights_packed, q_grouped, q_last, q_first, info = lax.optimization_barrier(
        (kv_gathered, weights_packed, q_grouped, q_last, q_first, info)
    )
    w_gathered = lax.all_gather(weights_packed, "seq", axis=0, tiled=False).reshape(
        shards * ff_rows, weights_packed.shape[1]
    )
    attended = attention(q_grouped, q_last, q_first, kv_gathered, info, rows, 2 * rows, shards_per)
    partial_out = jnp.dot(attended, w_out, preferred_element_type=jnp.float32)
    summed = tp_sum(partial_out.astype(jnp.bfloat16), 0).astype(jnp.float32)
    mid = (xf + summed).astype(jnp.bfloat16)
    mid_f = mid.astype(jnp.float32)
    post_normed = rms(mid_f, post_gain).astype(jnp.bfloat16)
    gate_up = jnp.dot(post_normed, w_gathered[:, : 2 * ff_local], preferred_element_type=jnp.float32)
    act = (jax.nn.silu(gate_up[:, :ff_local]) * gate_up[:, ff_local:]).astype(jnp.bfloat16)
    terms = lax.dot_general(
        act,
        w_gathered[:, 2 * ff_local : 3 * ff_local],
        (((1,), (1,)), ((), ())),
        preferred_element_type=jnp.float32,
    )
    hidden = tp_sum(terms.astype(jnp.bfloat16), 1, mid)
    return (hidden, key_cache, value_cache)


def solution(mesh):
    in_specs = (
        P("seq", None),
        P(),
        P(None, "tp"),
        P(None, "tp"),
        P(None, "tp"),
        P("tp", None),
        P(),
        P(),
        P("seq"),
        P("seq"),
        P(),
        P("seq", "tp"),
        P("seq", "tp"),
        P("tp", "seq"),
    )
    out_specs = (P("seq", None), P("seq", "tp"), P("seq", "tp"))
    return jax.shard_map(body, mesh=mesh, in_specs=in_specs, out_specs=out_specs, check_vma=False)
```

```python
import functools
import math

import jax
import jax.numpy as jnp
from jax import lax
from jax.experimental import pallas as pl
from jax.experimental.pallas import tpu as pltpu
from jax.sharding import PartitionSpec as P

MESH = pl.DeviceIdType.MESH


def rms(v, gain):
    return v * lax.rsqrt(jnp.mean(v * v, axis=-1, keepdims=True) + 1e-06) * gain


def rope(v, place):
    half = v.shape[-1] // 2
    freqs = 1000000.0 ** (-2.0 * jnp.arange(half, dtype=jnp.float32) / v.shape[-1])
    angle = place.astype(jnp.float32)[:, None] * freqs[None, :]
    cosine = jnp.cos(angle)[:, None, :]
    sine = jnp.sin(angle)[:, None, :]
    block_start = v[..., :half]
    second = v[..., half:]
    return jnp.concatenate(
        [block_start * cosine - second * sine, second * cosine + block_start * sine], axis=-1
    )


def tp_sum_kernel(n, with_base, *refs):
    if with_base:
        x_ref, base_ref, out_ref, slots, reduced, send1, recv1, send2, recv2 = refs
    else:
        x_ref, out_ref, slots, reduced, send1, recv1, send2, recv2 = refs
    me = lax.axis_index("tp")
    row = lax.axis_index("seq")
    cols = x_ref.shape[1] // n

    barrier = pltpu.get_barrier_semaphore()
    for k in range(1, n):
        pl.semaphore_signal(barrier, inc=1, device_id=(row, lax.rem(me + k, n)), device_id_type=MESH)
    pl.semaphore_wait(barrier, n - 1)

    def block(ref, owner):
        return ref.at[:, pl.ds(pl.multiple_of(owner * cols, cols), cols)]

    first = []
    for k in range(1, n):
        peer = lax.rem(me + k, n)
        copy = pltpu.make_async_remote_copy(
            src_ref=block(x_ref, peer),
            dst_ref=slots.at[k],
            send_sem=send1.at[k],
            recv_sem=recv1.at[k],
            device_id=(row, peer),
            device_id_type=MESH,
        )
        copy.start()
        first.append(copy)
    for copy in first:
        copy.wait()
    total = block(x_ref, me)[...].astype(jnp.float32)
    for k in range(1, n):
        total = total + slots[k].astype(jnp.float32)
    reduced[...] = total.astype(reduced.dtype)
    block(out_ref, me)[...] = reduced[...]

    second = []
    for k in range(1, n):
        peer = lax.rem(me + k, n)
        copy = pltpu.make_async_remote_copy(
            src_ref=reduced,
            dst_ref=block(out_ref, me),
            send_sem=send2.at[k],
            recv_sem=recv2.at[k],
            device_id=(row, peer),
            device_id_type=MESH,
        )
        copy.start()
        second.append(copy)
    for copy in second:
        copy.wait()
    if with_base:
        out_ref[...] = (base_ref[...].astype(jnp.float32) + out_ref[...].astype(jnp.float32)).astype(
            out_ref.dtype
        )


def tp_sum(x, collective_id, base=None):
    n = lax.axis_size("tp")
    rows, width = x.shape
    cols = width // n
    operands = (x,) if base is None else (x, base)
    return pl.pallas_call(
        functools.partial(tp_sum_kernel, n, base is not None),
        out_shape=jax.ShapeDtypeStruct((rows, width), x.dtype),
        in_specs=[pl.BlockSpec(memory_space=pltpu.VMEM)] * len(operands),
        out_specs=pl.BlockSpec(memory_space=pltpu.VMEM),
        scratch_shapes=[
            pltpu.VMEM((n, rows, cols), x.dtype),
            pltpu.VMEM((rows, cols), x.dtype),
            pltpu.SemaphoreType.DMA((n,)),
            pltpu.SemaphoreType.DMA((n,)),
            pltpu.SemaphoreType.DMA((n,)),
            pltpu.SemaphoreType.DMA((n,)),
        ],
        compiler_params=pltpu.CompilerParams(collective_id=collective_id, has_side_effects=True),
    )(*operands)


def attention_kernel(info, q_ref, q_last_ref, q_first_ref, kv_ref, o_ref, top_ref, total_ref, acc_ref):
    step = pl.program_id(0)
    groups, rows_all, head_size = q_ref.shape
    shards_per, both, _ = kv_ref.shape
    rows = both // 2
    width = shards_per * rows
    rows_q = o_ref.shape[0]
    per_group = rows_all // rows_q
    scale = 1.0 / math.sqrt(head_size)

    @pl.when(step == 0)
    def _():
        top_ref[...] = jnp.full(top_ref.shape, -1e30, jnp.float32)
        total_ref[...] = jnp.zeros(total_ref.shape, jnp.float32)
        acc_ref[...] = jnp.zeros(acc_ref.shape, jnp.float32)

    offset = step * width
    needed = (step >= info[0]) & (step <= info[1])
    whole = (offset >= info[2]) & (offset + width - 1 <= info[3])

    def run(masked):
        for g in range(groups):
            q = q_ref[g]
            k = kv_ref[:, :rows, g * head_size : (g + 1) * head_size].reshape(width, head_size)
            v = kv_ref[:, rows:, g * head_size : (g + 1) * head_size].reshape(width, head_size)
            s = lax.dot_general(q, k, (((1,), (1,)), ((), ())), preferred_element_type=jnp.float32) * scale
            if masked:
                k_index = offset + lax.broadcasted_iota(jnp.int32, s.shape, 1)
                allowed = (k_index <= q_last_ref[:, :1]) & (k_index >= q_first_ref[:, :1])
                s = jnp.where(allowed, s, -1e30)
            top = top_ref[g]
            new_top = jnp.maximum(top, jnp.max(s, axis=-1, keepdims=True))
            p = jnp.exp(s - new_top)
            if masked:
                p = jnp.where(allowed, p, 0.0)
            decay = jnp.exp(top - new_top)
            total_ref[g] = total_ref[g] * decay + jnp.sum(p, axis=-1, keepdims=True)
            acc_ref[g] = acc_ref[g] * decay + jnp.dot(
                p.astype(jnp.bfloat16), v, preferred_element_type=jnp.float32
            )
            top_ref[g] = new_top

    @pl.when(needed & whole)
    def _():
        run(False)

    @pl.when(needed & jnp.logical_not(whole))
    def _():
        run(True)

    @pl.when(step == pl.num_programs(0) - 1)
    def _():
        for g in range(groups):
            out = acc_ref[g] / total_ref[g]
            for h in range(per_group):
                col = (g * per_group + h) * head_size
                o_ref[:, col : col + head_size] = out[h * rows_q : (h + 1) * rows_q].astype(o_ref.dtype)


def attention(q_grouped, q_last, q_first, gathered, info, rows, kv_rows_per_shard, shards_per):
    groups, rows_all, head_size = q_grouped.shape
    shards, _, width_all = gathered.shape
    blocks = shards // shards_per
    out_cols = rows_all // rows * groups * head_size

    def kv_map(j, info):
        return (jnp.minimum(jnp.maximum(j, info[0]), info[1]), 0, 0)

    grid_spec = pltpu.PrefetchScalarGridSpec(
        num_scalar_prefetch=1,
        grid=(blocks,),
        in_specs=[
            pl.BlockSpec((groups, rows_all, head_size), lambda j, info: (0, 0, 0)),
            pl.BlockSpec(q_last.shape, lambda j, info: (0, 0)),
            pl.BlockSpec(q_first.shape, lambda j, info: (0, 0)),
            pl.BlockSpec((shards_per, kv_rows_per_shard, width_all), kv_map),
        ],
        out_specs=pl.BlockSpec((rows, out_cols), lambda j, info: (0, 0)),
        scratch_shapes=[
            pltpu.VMEM((groups, rows_all, 1), jnp.float32),
            pltpu.VMEM((groups, rows_all, 1), jnp.float32),
            pltpu.VMEM((groups, rows_all, head_size), jnp.float32),
        ],
    )
    return pl.pallas_call(
        attention_kernel,
        out_shape=jax.ShapeDtypeStruct((rows, out_cols), jnp.bfloat16),
        grid_spec=grid_spec,
        compiler_params=pltpu.CompilerParams(dimension_semantics=("arbitrary",)),
    )(info, q_grouped, q_last, q_first, gathered)


def body(
    layer_input,
    norm_gain,
    w_query,
    key_weight,
    value_weight,
    w_out,
    query_gain,
    key_gain,
    seg_ids,
    positions,
    post_gain,
    w_gate,
    w_up,
    w_down,
):
    rows = layer_input.shape[0]
    head_size = query_gain.shape[0]
    query_local = w_query.shape[1] // head_size
    kv_local = key_weight.shape[1] // head_size
    kv_cols = kv_local * head_size
    head_group = query_local // kv_local
    scale = 1.0 / math.sqrt(head_size)
    shards = lax.axis_size("seq")
    xf = layer_input.astype(jnp.float32)
    normed_input = rms(xf, norm_gain).astype(jnp.bfloat16)
    query_matrix = jnp.dot(normed_input, w_query, preferred_element_type=jnp.float32).reshape(
        rows, query_local, head_size
    )
    query_matrix = rope(rms(query_matrix, query_gain), positions).astype(jnp.bfloat16)
    key_matrix = jnp.dot(normed_input, key_weight, preferred_element_type=jnp.float32).reshape(
        rows, kv_local, head_size
    )
    key_matrix = rope(rms(key_matrix, key_gain), positions).astype(jnp.bfloat16)
    key_cache = key_matrix.reshape(rows, kv_cols)
    value_cache = jnp.dot(normed_input, value_weight, preferred_element_type=jnp.float32).astype(
        jnp.bfloat16
    )

    width_all = 2 * kv_cols
    ff_rows, ff_local = w_gate.shape
    rest = ff_local - width_all
    down_t = w_down.T
    kv_packed = jnp.concatenate([key_cache, value_cache], axis=0)
    kv_gathered = lax.all_gather(kv_packed, "seq", axis=0, tiled=False)
    weights_packed = jnp.concatenate([w_gate, w_up, down_t], axis=1)

    me = lax.axis_index("seq")
    first = me * rows
    my_last = first + rows - 1
    q_index = first + jnp.arange(rows, dtype=jnp.int32)
    q_start = q_index - positions
    shards_per = 1
    for trial in range(1, max(1, 1024 // rows) + 1):
        if shards % trial == 0:
            shards_per = trial
    width = rows * shards_per
    info = jnp.stack([q_start[0] // width, my_last // width, q_start[rows - 1], first])
    q_grouped = (
        query_matrix.reshape(rows, kv_local, head_group, head_size)
        .transpose(1, 2, 0, 3)
        .reshape(kv_local, head_group * rows, head_size)
    )
    lanes = 128
    q_last = jnp.broadcast_to(jnp.tile(q_index, head_group)[:, None], (head_group * rows, lanes))
    q_first = jnp.broadcast_to(jnp.tile(q_start, head_group)[:, None], (head_group * rows, lanes))
    kv_gathered, weights_packed, q_grouped, q_last, q_first, info = lax.optimization_barrier(
        (kv_gathered, weights_packed, q_grouped, q_last, q_first, info)
    )
    w_gathered = lax.all_gather(weights_packed, "seq", axis=0, tiled=False).reshape(
        shards * ff_rows, weights_packed.shape[1]
    )
    attended = attention(q_grouped, q_last, q_first, kv_gathered, info, rows, 2 * rows, shards_per)
    partial_out = jnp.dot(attended, w_out, preferred_element_type=jnp.float32)
    summed = tp_sum(partial_out.astype(jnp.bfloat16), 0).astype(jnp.float32)
    mid = (xf + summed).astype(jnp.bfloat16)
    mid_f = mid.astype(jnp.float32)
    post_normed = lax.optimization_barrier(rms(mid_f, post_gain).astype(jnp.bfloat16))
    gate_up = jnp.dot(post_normed, w_gathered[:, : 2 * ff_local], preferred_element_type=jnp.float32)
    act = (jax.nn.silu(gate_up[:, :ff_local]) * gate_up[:, ff_local:]).astype(jnp.bfloat16)
    terms = lax.dot_general(
        act,
        w_gathered[:, 2 * ff_local : 3 * ff_local],
        (((1,), (1,)), ((), ())),
        preferred_element_type=jnp.float32,
    )
    hidden = tp_sum(terms.astype(jnp.bfloat16), 1, mid)
    return (hidden, key_cache, value_cache)


def solution(mesh):
    in_specs = (
        P("seq", None),
        P(),
        P(None, "tp"),
        P(None, "tp"),
        P(None, "tp"),
        P("tp", None),
        P(),
        P(),
        P("seq"),
        P("seq"),
        P(),
        P("seq", "tp"),
        P("seq", "tp"),
        P("tp", "seq"),
    )
    out_specs = (P("seq", None), P("seq", "tp"), P("seq", "tp"))
    return jax.shard_map(body, mesh=mesh, in_specs=in_specs, out_specs=out_specs, check_vma=False)
```

```python
import functools
import math

import jax
import jax.numpy as jnp
from jax import lax
from jax.experimental import pallas as pl
from jax.experimental.pallas import tpu as pltpu
from jax.sharding import PartitionSpec as P

MESH = pl.DeviceIdType.MESH


def rms(v, gain):
    return v * lax.rsqrt(jnp.mean(v * v, axis=-1, keepdims=True) + 1e-06) * gain


def rope(v, place):
    half = v.shape[-1] // 2
    freqs = 1000000.0 ** (-2.0 * jnp.arange(half, dtype=jnp.float32) / v.shape[-1])
    angle = place.astype(jnp.float32)[:, None] * freqs[None, :]
    cosine = jnp.cos(angle)[:, None, :]
    sine = jnp.sin(angle)[:, None, :]
    block_start = v[..., :half]
    second = v[..., half:]
    return jnp.concatenate(
        [block_start * cosine - second * sine, second * cosine + block_start * sine], axis=-1
    )


def tp_sum_kernel(n, parts, with_base, *refs):
    if with_base:
        x_ref, base_ref, out_ref, slots, reduced, send1, recv1, send2, recv2 = refs
    else:
        x_ref, out_ref, slots, reduced, send1, recv1, send2, recv2 = refs
    me = lax.axis_index("tp")
    row = lax.axis_index("seq")
    cols = x_ref.shape[1] // n
    rows_p = x_ref.shape[0] // parts

    barrier = pltpu.get_barrier_semaphore()
    for k in range(1, n):
        pl.semaphore_signal(barrier, inc=1, device_id=(row, lax.rem(me + k, n)), device_id_type=MESH)
    pl.semaphore_wait(barrier, n - 1)

    def cols_of(owner):
        return pl.ds(pl.multiple_of(owner * cols, cols), cols)

    def rows_of(c):
        return pl.ds(c * rows_p, rows_p)

    first = []
    for c in range(parts):
        part = []
        for k in range(1, n):
            peer = lax.rem(me + k, n)
            copy = pltpu.make_async_remote_copy(
                src_ref=x_ref.at[rows_of(c), cols_of(peer)],
                dst_ref=slots.at[k, rows_of(c)],
                send_sem=send1.at[c, k],
                recv_sem=recv1.at[c, k],
                device_id=(row, peer),
                device_id_type=MESH,
            )
            copy.start()
            part.append(copy)
        first.append(part)

    second = []
    for c in range(parts):
        for copy in first[c]:
            copy.wait()
        total = x_ref[rows_of(c), cols_of(me)].astype(jnp.float32)
        for k in range(1, n):
            total = total + slots[k, rows_of(c)].astype(jnp.float32)
        reduced[rows_of(c)] = total.astype(reduced.dtype)
        out_ref[rows_of(c), cols_of(me)] = reduced[rows_of(c)]
        for k in range(1, n):
            peer = lax.rem(me + k, n)
            copy = pltpu.make_async_remote_copy(
                src_ref=reduced.at[rows_of(c)],
                dst_ref=out_ref.at[rows_of(c), cols_of(me)],
                send_sem=send2.at[c, k],
                recv_sem=recv2.at[c, k],
                device_id=(row, peer),
                device_id_type=MESH,
            )
            copy.start()
            second.append(copy)
    for copy in second:
        copy.wait()
    if with_base:
        out_ref[...] = (base_ref[...].astype(jnp.float32) + out_ref[...].astype(jnp.float32)).astype(
            out_ref.dtype
        )


def tp_sum(x, collective_id, base=None):
    n = lax.axis_size("tp")
    rows, width = x.shape
    cols = width // n
    operands = (x,) if base is None else (x, base)
    parts = 2 if rows % 32 == 0 else 1
    return pl.pallas_call(
        functools.partial(tp_sum_kernel, n, parts, base is not None),
        out_shape=jax.ShapeDtypeStruct((rows, width), x.dtype),
        in_specs=[pl.BlockSpec(memory_space=pltpu.VMEM)] * len(operands),
        out_specs=pl.BlockSpec(memory_space=pltpu.VMEM),
        scratch_shapes=[
            pltpu.VMEM((n, rows, cols), x.dtype),
            pltpu.VMEM((rows, cols), x.dtype),
            pltpu.SemaphoreType.DMA((parts, n)),
            pltpu.SemaphoreType.DMA((parts, n)),
            pltpu.SemaphoreType.DMA((parts, n)),
            pltpu.SemaphoreType.DMA((parts, n)),
        ],
        compiler_params=pltpu.CompilerParams(collective_id=collective_id, has_side_effects=True),
    )(*operands)


def attention_kernel(info, q_ref, q_last_ref, q_first_ref, kv_ref, o_ref, top_ref, total_ref, acc_ref):
    step = pl.program_id(0)
    groups, rows_all, head_size = q_ref.shape
    shards_per, both, _ = kv_ref.shape
    rows = both // 2
    width = shards_per * rows
    rows_q = o_ref.shape[0]
    per_group = rows_all // rows_q
    scale = 1.0 / math.sqrt(head_size)

    @pl.when(step == 0)
    def _():
        top_ref[...] = jnp.full(top_ref.shape, -1e30, jnp.float32)
        total_ref[...] = jnp.zeros(total_ref.shape, jnp.float32)
        acc_ref[...] = jnp.zeros(acc_ref.shape, jnp.float32)

    offset = step * width
    needed = (step >= info[0]) & (step <= info[1])
    whole = (offset >= info[2]) & (offset + width - 1 <= info[3])

    def run(masked):
        for g in range(groups):
            q = q_ref[g]
            k = kv_ref[:, :rows, g * head_size : (g + 1) * head_size].reshape(width, head_size)
            v = kv_ref[:, rows:, g * head_size : (g + 1) * head_size].reshape(width, head_size)
            s = lax.dot_general(q, k, (((1,), (1,)), ((), ())), preferred_element_type=jnp.float32) * scale
            if masked:
                k_index = offset + lax.broadcasted_iota(jnp.int32, s.shape, 1)
                allowed = (k_index <= q_last_ref[:, :1]) & (k_index >= q_first_ref[:, :1])
                s = jnp.where(allowed, s, -1e30)
            top = top_ref[g]
            new_top = jnp.maximum(top, jnp.max(s, axis=-1, keepdims=True))
            p = jnp.exp(s - new_top)
            if masked:
                p = jnp.where(allowed, p, 0.0)
            decay = jnp.exp(top - new_top)
            total_ref[g] = total_ref[g] * decay + jnp.sum(p, axis=-1, keepdims=True)
            acc_ref[g] = acc_ref[g] * decay + jnp.dot(
                p.astype(jnp.bfloat16), v, preferred_element_type=jnp.float32
            )
            top_ref[g] = new_top

    @pl.when(needed & whole)
    def _():
        run(False)

    @pl.when(needed & jnp.logical_not(whole))
    def _():
        run(True)

    @pl.when(step == pl.num_programs(0) - 1)
    def _():
        for g in range(groups):
            out = acc_ref[g] / total_ref[g]
            for h in range(per_group):
                col = (g * per_group + h) * head_size
                o_ref[:, col : col + head_size] = out[h * rows_q : (h + 1) * rows_q].astype(o_ref.dtype)


def attention(q_grouped, q_last, q_first, gathered, info, rows, kv_rows_per_shard, shards_per):
    groups, rows_all, head_size = q_grouped.shape
    shards, _, width_all = gathered.shape
    blocks = shards // shards_per
    out_cols = rows_all // rows * groups * head_size

    def kv_map(j, info):
        return (jnp.minimum(jnp.maximum(j, info[0]), info[1]), 0, 0)

    grid_spec = pltpu.PrefetchScalarGridSpec(
        num_scalar_prefetch=1,
        grid=(blocks,),
        in_specs=[
            pl.BlockSpec((groups, rows_all, head_size), lambda j, info: (0, 0, 0)),
            pl.BlockSpec(q_last.shape, lambda j, info: (0, 0)),
            pl.BlockSpec(q_first.shape, lambda j, info: (0, 0)),
            pl.BlockSpec((shards_per, kv_rows_per_shard, width_all), kv_map),
        ],
        out_specs=pl.BlockSpec((rows, out_cols), lambda j, info: (0, 0)),
        scratch_shapes=[
            pltpu.VMEM((groups, rows_all, 1), jnp.float32),
            pltpu.VMEM((groups, rows_all, 1), jnp.float32),
            pltpu.VMEM((groups, rows_all, head_size), jnp.float32),
        ],
    )
    return pl.pallas_call(
        attention_kernel,
        out_shape=jax.ShapeDtypeStruct((rows, out_cols), jnp.bfloat16),
        grid_spec=grid_spec,
        compiler_params=pltpu.CompilerParams(dimension_semantics=("arbitrary",)),
    )(info, q_grouped, q_last, q_first, gathered)


def body(
    layer_input,
    norm_gain,
    w_query,
    key_weight,
    value_weight,
    w_out,
    query_gain,
    key_gain,
    seg_ids,
    positions,
    post_gain,
    w_gate,
    w_up,
    w_down,
):
    rows = layer_input.shape[0]
    head_size = query_gain.shape[0]
    query_local = w_query.shape[1] // head_size
    kv_local = key_weight.shape[1] // head_size
    kv_cols = kv_local * head_size
    head_group = query_local // kv_local
    scale = 1.0 / math.sqrt(head_size)
    shards = lax.axis_size("seq")
    xf = layer_input.astype(jnp.float32)
    normed_input = rms(xf, norm_gain).astype(jnp.bfloat16)
    query_matrix = jnp.dot(normed_input, w_query, preferred_element_type=jnp.float32).reshape(
        rows, query_local, head_size
    )
    query_matrix = rope(rms(query_matrix, query_gain), positions).astype(jnp.bfloat16)
    key_matrix = jnp.dot(normed_input, key_weight, preferred_element_type=jnp.float32).reshape(
        rows, kv_local, head_size
    )
    key_matrix = rope(rms(key_matrix, key_gain), positions).astype(jnp.bfloat16)
    key_cache = key_matrix.reshape(rows, kv_cols)
    value_cache = jnp.dot(normed_input, value_weight, preferred_element_type=jnp.float32).astype(
        jnp.bfloat16
    )

    width_all = 2 * kv_cols
    ff_rows, ff_local = w_gate.shape
    rest = ff_local - width_all
    down_t = w_down.T
    kv_packed = jnp.concatenate([key_cache, value_cache], axis=0)
    kv_gathered = lax.all_gather(kv_packed, "seq", axis=0, tiled=False)
    weights_packed = jnp.concatenate([w_gate, w_up, down_t], axis=1)

    me = lax.axis_index("seq")
    first = me * rows
    my_last = first + rows - 1
    q_index = first + jnp.arange(rows, dtype=jnp.int32)
    q_start = q_index - positions
    shards_per = 1
    for trial in range(1, max(1, 1024 // rows) + 1):
        if shards % trial == 0:
            shards_per = trial
    width = rows * shards_per
    info = jnp.stack([q_start[0] // width, my_last // width, q_start[rows - 1], first])
    q_grouped = (
        query_matrix.reshape(rows, kv_local, head_group, head_size)
        .transpose(1, 2, 0, 3)
        .reshape(kv_local, head_group * rows, head_size)
    )
    lanes = 128
    q_last = jnp.broadcast_to(jnp.tile(q_index, head_group)[:, None], (head_group * rows, lanes))
    q_first = jnp.broadcast_to(jnp.tile(q_start, head_group)[:, None], (head_group * rows, lanes))
    kv_gathered, weights_packed, q_grouped, q_last, q_first, info = lax.optimization_barrier(
        (kv_gathered, weights_packed, q_grouped, q_last, q_first, info)
    )
    w_gathered = lax.all_gather(weights_packed, "seq", axis=0, tiled=False).reshape(
        shards * ff_rows, weights_packed.shape[1]
    )
    attended = attention(q_grouped, q_last, q_first, kv_gathered, info, rows, 2 * rows, shards_per)
    partial_out = jnp.dot(attended, w_out, preferred_element_type=jnp.float32)
    summed = tp_sum(partial_out.astype(jnp.bfloat16), 0).astype(jnp.float32)
    mid = (xf + summed).astype(jnp.bfloat16)
    mid_f = mid.astype(jnp.float32)
    post_normed = lax.optimization_barrier(rms(mid_f, post_gain).astype(jnp.bfloat16))
    gate_up = jnp.dot(post_normed, w_gathered[:, : 2 * ff_local], preferred_element_type=jnp.float32)
    act = (jax.nn.silu(gate_up[:, :ff_local]) * gate_up[:, ff_local:]).astype(jnp.bfloat16)
    terms = lax.dot_general(
        act,
        w_gathered[:, 2 * ff_local : 3 * ff_local],
        (((1,), (1,)), ((), ())),
        preferred_element_type=jnp.float32,
    )
    hidden = tp_sum(terms.astype(jnp.bfloat16), 1, mid)
    return (hidden, key_cache, value_cache)


def solution(mesh):
    in_specs = (
        P("seq", None),
        P(),
        P(None, "tp"),
        P(None, "tp"),
        P(None, "tp"),
        P("tp", None),
        P(),
        P(),
        P("seq"),
        P("seq"),
        P(),
        P("seq", "tp"),
        P("seq", "tp"),
        P("tp", "seq"),
    )
    out_specs = (P("seq", None), P("seq", "tp"), P("seq", "tp"))
    return jax.shard_map(body, mesh=mesh, in_specs=in_specs, out_specs=out_specs, check_vma=False)
```

```python
import functools
import math

import jax
import jax.numpy as jnp
from jax import lax
from jax.experimental import pallas as pl
from jax.experimental.pallas import tpu as pltpu
from jax.sharding import PartitionSpec as P

MESH = pl.DeviceIdType.MESH


def rms(v, gain):
    return v * lax.rsqrt(jnp.mean(v * v, axis=-1, keepdims=True) + 1e-06) * gain


def rope(v, place):
    half = v.shape[-1] // 2
    freqs = 1000000.0 ** (-2.0 * jnp.arange(half, dtype=jnp.float32) / v.shape[-1])
    angle = place.astype(jnp.float32)[:, None] * freqs[None, :]
    cosine = jnp.cos(angle)[:, None, :]
    sine = jnp.sin(angle)[:, None, :]
    block_start = v[..., :half]
    second = v[..., half:]
    return jnp.concatenate(
        [block_start * cosine - second * sine, second * cosine + block_start * sine], axis=-1
    )


def tp_sum_kernel(n, parts, with_base, *refs):
    if with_base:
        x_ref, base_ref, out_ref, slots, reduced, send1, recv1, send2, recv2 = refs
    else:
        x_ref, out_ref, slots, reduced, send1, recv1, send2, recv2 = refs
    me = lax.axis_index("tp")
    row = lax.axis_index("seq")
    cols = x_ref.shape[1] // n
    rows_p = x_ref.shape[0] // parts

    barrier = pltpu.get_barrier_semaphore()
    for k in range(1, n):
        pl.semaphore_signal(barrier, inc=1, device_id=(row, lax.rem(me + k, n)), device_id_type=MESH)
    pl.semaphore_wait(barrier, n - 1)

    def cols_of(owner):
        return pl.ds(pl.multiple_of(owner * cols, cols), cols)

    def rows_of(c):
        return pl.ds(c * rows_p, rows_p)

    first = []
    for c in range(parts):
        part = []
        for k in range(1, n):
            peer = lax.rem(me + k, n)
            copy = pltpu.make_async_remote_copy(
                src_ref=x_ref.at[rows_of(c), cols_of(peer)],
                dst_ref=slots.at[k, rows_of(c)],
                send_sem=send1.at[c, k],
                recv_sem=recv1.at[c, k],
                device_id=(row, peer),
                device_id_type=MESH,
            )
            copy.start()
            part.append(copy)
        first.append(part)

    second = []
    for c in range(parts):
        for copy in first[c]:
            copy.wait()
        total = x_ref[rows_of(c), cols_of(me)].astype(jnp.float32)
        for k in range(1, n):
            total = total + slots[k, rows_of(c)].astype(jnp.float32)
        reduced[rows_of(c)] = total.astype(reduced.dtype)
        out_ref[rows_of(c), cols_of(me)] = reduced[rows_of(c)]
        for k in range(1, n):
            peer = lax.rem(me + k, n)
            copy = pltpu.make_async_remote_copy(
                src_ref=reduced.at[rows_of(c)],
                dst_ref=out_ref.at[rows_of(c), cols_of(me)],
                send_sem=send2.at[c, k],
                recv_sem=recv2.at[c, k],
                device_id=(row, peer),
                device_id_type=MESH,
            )
            copy.start()
            second.append(copy)
    for copy in second:
        copy.wait()
    if with_base:
        out_ref[...] = (base_ref[...].astype(jnp.float32) + out_ref[...].astype(jnp.float32)).astype(
            out_ref.dtype
        )


def tp_sum(x, collective_id, base=None):
    n = lax.axis_size("tp")
    rows, width = x.shape
    cols = width // n
    operands = (x,) if base is None else (x, base)
    parts = 4 if rows % 64 == 0 else 1
    return pl.pallas_call(
        functools.partial(tp_sum_kernel, n, parts, base is not None),
        out_shape=jax.ShapeDtypeStruct((rows, width), x.dtype),
        in_specs=[pl.BlockSpec(memory_space=pltpu.VMEM)] * len(operands),
        out_specs=pl.BlockSpec(memory_space=pltpu.VMEM),
        scratch_shapes=[
            pltpu.VMEM((n, rows, cols), x.dtype),
            pltpu.VMEM((rows, cols), x.dtype),
            pltpu.SemaphoreType.DMA((parts, n)),
            pltpu.SemaphoreType.DMA((parts, n)),
            pltpu.SemaphoreType.DMA((parts, n)),
            pltpu.SemaphoreType.DMA((parts, n)),
        ],
        compiler_params=pltpu.CompilerParams(collective_id=collective_id, has_side_effects=True),
    )(*operands)


def attention_kernel(info, q_ref, q_last_ref, q_first_ref, kv_ref, o_ref, top_ref, total_ref, acc_ref):
    step = pl.program_id(0)
    groups, rows_all, head_size = q_ref.shape
    shards_per, both, _ = kv_ref.shape
    rows = both // 2
    width = shards_per * rows
    rows_q = o_ref.shape[0]
    per_group = rows_all // rows_q
    scale = 1.0 / math.sqrt(head_size)

    @pl.when(step == 0)
    def _():
        top_ref[...] = jnp.full(top_ref.shape, -1e30, jnp.float32)
        total_ref[...] = jnp.zeros(total_ref.shape, jnp.float32)
        acc_ref[...] = jnp.zeros(acc_ref.shape, jnp.float32)

    offset = step * width
    needed = (step >= info[0]) & (step <= info[1])
    whole = (offset >= info[2]) & (offset + width - 1 <= info[3])

    def run(masked):
        for g in range(groups):
            q = q_ref[g]
            k = kv_ref[:, :rows, g * head_size : (g + 1) * head_size].reshape(width, head_size)
            v = kv_ref[:, rows:, g * head_size : (g + 1) * head_size].reshape(width, head_size)
            s = lax.dot_general(q, k, (((1,), (1,)), ((), ())), preferred_element_type=jnp.float32) * scale
            if masked:
                k_index = offset + lax.broadcasted_iota(jnp.int32, s.shape, 1)
                allowed = (k_index <= q_last_ref[:, :1]) & (k_index >= q_first_ref[:, :1])
                s = jnp.where(allowed, s, -1e30)
            top = top_ref[g]
            new_top = jnp.maximum(top, jnp.max(s, axis=-1, keepdims=True))
            p = jnp.exp(s - new_top)
            if masked:
                p = jnp.where(allowed, p, 0.0)
            decay = jnp.exp(top - new_top)
            total_ref[g] = total_ref[g] * decay + jnp.sum(p, axis=-1, keepdims=True)
            acc_ref[g] = acc_ref[g] * decay + jnp.dot(
                p.astype(jnp.bfloat16), v, preferred_element_type=jnp.float32
            )
            top_ref[g] = new_top

    @pl.when(needed & whole)
    def _():
        run(False)

    @pl.when(needed & jnp.logical_not(whole))
    def _():
        run(True)

    @pl.when(step == pl.num_programs(0) - 1)
    def _():
        for g in range(groups):
            out = acc_ref[g] / total_ref[g]
            for h in range(per_group):
                col = (g * per_group + h) * head_size
                o_ref[:, col : col + head_size] = out[h * rows_q : (h + 1) * rows_q].astype(o_ref.dtype)


def attention(q_grouped, q_last, q_first, gathered, info, rows, kv_rows_per_shard, shards_per):
    groups, rows_all, head_size = q_grouped.shape
    shards, _, width_all = gathered.shape
    blocks = shards // shards_per
    out_cols = rows_all // rows * groups * head_size

    def kv_map(j, info):
        return (jnp.minimum(jnp.maximum(j, info[0]), info[1]), 0, 0)

    grid_spec = pltpu.PrefetchScalarGridSpec(
        num_scalar_prefetch=1,
        grid=(blocks,),
        in_specs=[
            pl.BlockSpec((groups, rows_all, head_size), lambda j, info: (0, 0, 0)),
            pl.BlockSpec(q_last.shape, lambda j, info: (0, 0)),
            pl.BlockSpec(q_first.shape, lambda j, info: (0, 0)),
            pl.BlockSpec((shards_per, kv_rows_per_shard, width_all), kv_map),
        ],
        out_specs=pl.BlockSpec((rows, out_cols), lambda j, info: (0, 0)),
        scratch_shapes=[
            pltpu.VMEM((groups, rows_all, 1), jnp.float32),
            pltpu.VMEM((groups, rows_all, 1), jnp.float32),
            pltpu.VMEM((groups, rows_all, head_size), jnp.float32),
        ],
    )
    return pl.pallas_call(
        attention_kernel,
        out_shape=jax.ShapeDtypeStruct((rows, out_cols), jnp.bfloat16),
        grid_spec=grid_spec,
        compiler_params=pltpu.CompilerParams(dimension_semantics=("arbitrary",)),
    )(info, q_grouped, q_last, q_first, gathered)


def body(
    layer_input,
    norm_gain,
    w_query,
    key_weight,
    value_weight,
    w_out,
    query_gain,
    key_gain,
    seg_ids,
    positions,
    post_gain,
    w_gate,
    w_up,
    w_down,
):
    rows = layer_input.shape[0]
    head_size = query_gain.shape[0]
    query_local = w_query.shape[1] // head_size
    kv_local = key_weight.shape[1] // head_size
    kv_cols = kv_local * head_size
    head_group = query_local // kv_local
    scale = 1.0 / math.sqrt(head_size)
    shards = lax.axis_size("seq")
    xf = layer_input.astype(jnp.float32)
    normed_input = rms(xf, norm_gain).astype(jnp.bfloat16)
    query_matrix = jnp.dot(normed_input, w_query, preferred_element_type=jnp.float32).reshape(
        rows, query_local, head_size
    )
    query_matrix = rope(rms(query_matrix, query_gain), positions).astype(jnp.bfloat16)
    key_matrix = jnp.dot(normed_input, key_weight, preferred_element_type=jnp.float32).reshape(
        rows, kv_local, head_size
    )
    key_matrix = rope(rms(key_matrix, key_gain), positions).astype(jnp.bfloat16)
    key_cache = key_matrix.reshape(rows, kv_cols)
    value_cache = jnp.dot(normed_input, value_weight, preferred_element_type=jnp.float32).astype(
        jnp.bfloat16
    )

    width_all = 2 * kv_cols
    ff_rows, ff_local = w_gate.shape
    rest = ff_local - width_all
    down_t = w_down.T
    kv_packed = jnp.concatenate([key_cache, value_cache], axis=0)
    kv_gathered = lax.all_gather(kv_packed, "seq", axis=0, tiled=False)
    weights_packed = jnp.concatenate([w_gate, w_up, down_t], axis=1)

    me = lax.axis_index("seq")
    first = me * rows
    my_last = first + rows - 1
    q_index = first + jnp.arange(rows, dtype=jnp.int32)
    q_start = q_index - positions
    shards_per = 1
    for trial in range(1, max(1, 1024 // rows) + 1):
        if shards % trial == 0:
            shards_per = trial
    width = rows * shards_per
    info = jnp.stack([q_start[0] // width, my_last // width, q_start[rows - 1], first])
    q_grouped = (
        query_matrix.reshape(rows, kv_local, head_group, head_size)
        .transpose(1, 2, 0, 3)
        .reshape(kv_local, head_group * rows, head_size)
    )
    lanes = 128
    q_last = jnp.broadcast_to(jnp.tile(q_index, head_group)[:, None], (head_group * rows, lanes))
    q_first = jnp.broadcast_to(jnp.tile(q_start, head_group)[:, None], (head_group * rows, lanes))
    kv_gathered, weights_packed, q_grouped, q_last, q_first, info = lax.optimization_barrier(
        (kv_gathered, weights_packed, q_grouped, q_last, q_first, info)
    )
    w_gathered = lax.all_gather(weights_packed, "seq", axis=0, tiled=False).reshape(
        shards * ff_rows, weights_packed.shape[1]
    )
    attended = attention(q_grouped, q_last, q_first, kv_gathered, info, rows, 2 * rows, shards_per)
    partial_out = jnp.dot(attended, w_out, preferred_element_type=jnp.float32)
    summed = tp_sum(partial_out.astype(jnp.bfloat16), 0).astype(jnp.float32)
    mid = (xf + summed).astype(jnp.bfloat16)
    mid_f = mid.astype(jnp.float32)
    post_normed = lax.optimization_barrier(rms(mid_f, post_gain).astype(jnp.bfloat16))
    gate_up = jnp.dot(post_normed, w_gathered[:, : 2 * ff_local], preferred_element_type=jnp.float32)
    act = (jax.nn.silu(gate_up[:, :ff_local]) * gate_up[:, ff_local:]).astype(jnp.bfloat16)
    terms = lax.dot_general(
        act,
        w_gathered[:, 2 * ff_local : 3 * ff_local],
        (((1,), (1,)), ((), ())),
        preferred_element_type=jnp.float32,
    )
    hidden = tp_sum(terms.astype(jnp.bfloat16), 1, mid)
    return (hidden, key_cache, value_cache)


def solution(mesh):
    in_specs = (
        P("seq", None),
        P(),
        P(None, "tp"),
        P(None, "tp"),
        P(None, "tp"),
        P("tp", None),
        P(),
        P(),
        P("seq"),
        P("seq"),
        P(),
        P("seq", "tp"),
        P("seq", "tp"),
        P("tp", "seq"),
    )
    out_specs = (P("seq", None), P("seq", "tp"), P("seq", "tp"))
    return jax.shard_map(body, mesh=mesh, in_specs=in_specs, out_specs=out_specs, check_vma=False)
```

```python
import functools
import math

import jax
import jax.numpy as jnp
from jax import lax
from jax.experimental import pallas as pl
from jax.experimental.pallas import tpu as pltpu
from jax.sharding import PartitionSpec as P

MESH = pl.DeviceIdType.MESH


def rms(v, gain):
    return v * lax.rsqrt(jnp.mean(v * v, axis=-1, keepdims=True) + 1e-06) * gain


def rope(v, place):
    half = v.shape[-1] // 2
    freqs = 1000000.0 ** (-2.0 * jnp.arange(half, dtype=jnp.float32) / v.shape[-1])
    angle = place.astype(jnp.float32)[:, None] * freqs[None, :]
    cosine = jnp.cos(angle)[:, None, :]
    sine = jnp.sin(angle)[:, None, :]
    block_start = v[..., :half]
    second = v[..., half:]
    return jnp.concatenate(
        [block_start * cosine - second * sine, second * cosine + block_start * sine], axis=-1
    )


def tp_sum_kernel(n, parts, with_base, *refs):
    if with_base:
        x_ref, base_ref, out_ref, slots, reduced, send1, recv1, send2, recv2 = refs
    else:
        x_ref, out_ref, slots, reduced, send1, recv1, send2, recv2 = refs
    me = lax.axis_index("tp")
    row = lax.axis_index("seq")
    cols = x_ref.shape[1] // n
    rows_p = x_ref.shape[0] // parts

    barrier = pltpu.get_barrier_semaphore()
    for k in range(1, n):
        pl.semaphore_signal(barrier, inc=1, device_id=(row, lax.rem(me + k, n)), device_id_type=MESH)
    pl.semaphore_wait(barrier, n - 1)

    def cols_of(owner):
        return pl.ds(pl.multiple_of(owner * cols, cols), cols)

    def rows_of(c):
        return pl.ds(c * rows_p, rows_p)

    first = []
    for c in range(parts):
        part = []
        for k in range(1, n):
            peer = lax.rem(me + k, n)
            copy = pltpu.make_async_remote_copy(
                src_ref=x_ref.at[rows_of(c), cols_of(peer)],
                dst_ref=slots.at[k, rows_of(c)],
                send_sem=send1.at[c, k],
                recv_sem=recv1.at[c, k],
                device_id=(row, peer),
                device_id_type=MESH,
            )
            copy.start()
            part.append(copy)
        first.append(part)

    second = []
    for c in range(parts):
        for copy in first[c]:
            copy.wait()
        total = x_ref[rows_of(c), cols_of(me)].astype(jnp.float32)
        for k in range(1, n):
            total = total + slots[k, rows_of(c)].astype(jnp.float32)
        reduced[rows_of(c)] = total.astype(reduced.dtype)
        out_ref[rows_of(c), cols_of(me)] = reduced[rows_of(c)]
        for k in range(1, n):
            peer = lax.rem(me + k, n)
            copy = pltpu.make_async_remote_copy(
                src_ref=reduced.at[rows_of(c)],
                dst_ref=out_ref.at[rows_of(c), cols_of(me)],
                send_sem=send2.at[c, k],
                recv_sem=recv2.at[c, k],
                device_id=(row, peer),
                device_id_type=MESH,
            )
            copy.start()
            second.append(copy)
    for copy in second:
        copy.wait()
    if with_base:
        out_ref[...] = (base_ref[...].astype(jnp.float32) + out_ref[...].astype(jnp.float32)).astype(
            out_ref.dtype
        )


def tp_sum(x, collective_id, base=None):
    n = lax.axis_size("tp")
    rows, width = x.shape
    cols = width // n
    operands = (x,) if base is None else (x, base)
    parts = 2 if rows % 32 == 0 else 1
    return pl.pallas_call(
        functools.partial(tp_sum_kernel, n, parts, base is not None),
        out_shape=jax.ShapeDtypeStruct((rows, width), x.dtype),
        in_specs=[pl.BlockSpec(memory_space=pltpu.VMEM)] * len(operands),
        out_specs=pl.BlockSpec(memory_space=pltpu.VMEM),
        scratch_shapes=[
            pltpu.VMEM((n, rows, cols), x.dtype),
            pltpu.VMEM((rows, cols), x.dtype),
            pltpu.SemaphoreType.DMA((parts, n)),
            pltpu.SemaphoreType.DMA((parts, n)),
            pltpu.SemaphoreType.DMA((parts, n)),
            pltpu.SemaphoreType.DMA((parts, n)),
        ],
        compiler_params=pltpu.CompilerParams(collective_id=collective_id, has_side_effects=True),
    )(*operands)


def attention_kernel(info, q_ref, q_last_ref, q_first_ref, kv_ref, o_ref, top_ref, total_ref, acc_ref):
    step = pl.program_id(0)
    groups, rows_all, head_size = q_ref.shape
    shards_per, both, _ = kv_ref.shape
    rows = both // 2
    width = shards_per * rows
    rows_q = o_ref.shape[0]
    per_group = rows_all // rows_q
    scale = 1.0 / math.sqrt(head_size)

    @pl.when(step == 0)
    def _():
        top_ref[...] = jnp.full(top_ref.shape, -1e30, jnp.float32)
        total_ref[...] = jnp.zeros(total_ref.shape, jnp.float32)
        acc_ref[...] = jnp.zeros(acc_ref.shape, jnp.float32)

    offset = step * width
    needed = (step >= info[0]) & (step <= info[1])
    whole = (offset >= info[2]) & (offset + width - 1 <= info[3])

    def run(masked):
        for g in range(groups):
            q = q_ref[g]
            k = kv_ref[:, :rows, g * head_size : (g + 1) * head_size].reshape(width, head_size)
            v = kv_ref[:, rows:, g * head_size : (g + 1) * head_size].reshape(width, head_size)
            s = lax.dot_general(q, k, (((1,), (1,)), ((), ())), preferred_element_type=jnp.float32) * scale
            if masked:
                k_index = offset + lax.broadcasted_iota(jnp.int32, s.shape, 1)
                allowed = (k_index <= q_last_ref[:, :1]) & (k_index >= q_first_ref[:, :1])
                s = jnp.where(allowed, s, -1e30)
            top = top_ref[g]
            new_top = jnp.maximum(top, jnp.max(s, axis=-1, keepdims=True))
            p = jnp.exp(s - new_top)
            if masked:
                p = jnp.where(allowed, p, 0.0)
            decay = jnp.exp(top - new_top)
            total_ref[g] = total_ref[g] * decay + jnp.sum(p, axis=-1, keepdims=True)
            acc_ref[g] = acc_ref[g] * decay + jnp.dot(
                p.astype(jnp.bfloat16), v, preferred_element_type=jnp.float32
            )
            top_ref[g] = new_top

    @pl.when(needed & whole)
    def _():
        run(False)

    @pl.when(needed & jnp.logical_not(whole))
    def _():
        run(True)

    @pl.when(step == pl.num_programs(0) - 1)
    def _():
        for g in range(groups):
            out = acc_ref[g] / total_ref[g]
            for h in range(per_group):
                col = (g * per_group + h) * head_size
                o_ref[:, col : col + head_size] = out[h * rows_q : (h + 1) * rows_q].astype(o_ref.dtype)


def attention(q_grouped, q_last, q_first, gathered, info, rows, kv_rows_per_shard, shards_per):
    groups, rows_all, head_size = q_grouped.shape
    shards, _, width_all = gathered.shape
    blocks = shards // shards_per
    out_cols = rows_all // rows * groups * head_size

    def kv_map(j, info):
        return (jnp.minimum(jnp.maximum(j, info[0]), info[1]), 0, 0)

    grid_spec = pltpu.PrefetchScalarGridSpec(
        num_scalar_prefetch=1,
        grid=(blocks,),
        in_specs=[
            pl.BlockSpec((groups, rows_all, head_size), lambda j, info: (0, 0, 0)),
            pl.BlockSpec(q_last.shape, lambda j, info: (0, 0)),
            pl.BlockSpec(q_first.shape, lambda j, info: (0, 0)),
            pl.BlockSpec((shards_per, kv_rows_per_shard, width_all), kv_map),
        ],
        out_specs=pl.BlockSpec((rows, out_cols), lambda j, info: (0, 0)),
        scratch_shapes=[
            pltpu.VMEM((groups, rows_all, 1), jnp.float32),
            pltpu.VMEM((groups, rows_all, 1), jnp.float32),
            pltpu.VMEM((groups, rows_all, head_size), jnp.float32),
        ],
    )
    return pl.pallas_call(
        attention_kernel,
        out_shape=jax.ShapeDtypeStruct((rows, out_cols), jnp.bfloat16),
        grid_spec=grid_spec,
        compiler_params=pltpu.CompilerParams(dimension_semantics=("arbitrary",)),
    )(info, q_grouped, q_last, q_first, gathered)


def body(
    layer_input,
    norm_gain,
    w_query,
    key_weight,
    value_weight,
    w_out,
    query_gain,
    key_gain,
    seg_ids,
    positions,
    post_gain,
    w_gate,
    w_up,
    w_down,
):
    rows = layer_input.shape[0]
    head_size = query_gain.shape[0]
    query_local = w_query.shape[1] // head_size
    kv_local = key_weight.shape[1] // head_size
    kv_cols = kv_local * head_size
    head_group = query_local // kv_local
    scale = 1.0 / math.sqrt(head_size)
    shards = lax.axis_size("seq")
    xf = layer_input.astype(jnp.float32)
    normed_input = rms(xf, norm_gain).astype(jnp.bfloat16)
    query_matrix = jnp.dot(normed_input, w_query, preferred_element_type=jnp.float32).reshape(
        rows, query_local, head_size
    )
    query_matrix = rope(rms(query_matrix, query_gain), positions).astype(jnp.bfloat16)
    key_matrix = jnp.dot(normed_input, key_weight, preferred_element_type=jnp.float32).reshape(
        rows, kv_local, head_size
    )
    key_matrix = rope(rms(key_matrix, key_gain), positions).astype(jnp.bfloat16)
    key_cache = key_matrix.reshape(rows, kv_cols)
    value_cache = jnp.dot(normed_input, value_weight, preferred_element_type=jnp.float32).astype(
        jnp.bfloat16
    )

    width_all = 2 * kv_cols
    ff_rows, ff_local = w_gate.shape
    rest = ff_local - width_all
    down_t = w_down.T
    kv_packed = jnp.concatenate([key_cache, value_cache], axis=0)
    kv_gathered = lax.all_gather(kv_packed, "seq", axis=0, tiled=False)
    weights_packed = jnp.concatenate([w_gate, w_up, down_t], axis=1)

    me = lax.axis_index("seq")
    first = me * rows
    my_last = first + rows - 1
    q_index = first + jnp.arange(rows, dtype=jnp.int32)
    q_start = q_index - positions
    shards_per = 1
    for trial in range(1, max(1, 1024 // rows) + 1):
        if shards % trial == 0:
            shards_per = trial
    width = rows * shards_per
    info = jnp.stack([q_start[0] // width, my_last // width, q_start[rows - 1], first])
    q_grouped = (
        query_matrix.reshape(rows, kv_local, head_group, head_size)
        .transpose(1, 2, 0, 3)
        .reshape(kv_local, head_group * rows, head_size)
    )
    lanes = 128
    q_last = jnp.broadcast_to(jnp.tile(q_index, head_group)[:, None], (head_group * rows, lanes))
    q_first = jnp.broadcast_to(jnp.tile(q_start, head_group)[:, None], (head_group * rows, lanes))
    weights_packed, q_grouped, q_last, q_first, info = lax.optimization_barrier(
        (weights_packed, q_grouped, q_last, q_first, info)
    )
    w_gathered = lax.all_gather(weights_packed, "seq", axis=0, tiled=False).reshape(
        shards * ff_rows, weights_packed.shape[1]
    )
    attended = attention(q_grouped, q_last, q_first, kv_gathered, info, rows, 2 * rows, shards_per)
    partial_out = jnp.dot(attended, w_out, preferred_element_type=jnp.float32)
    summed = tp_sum(partial_out.astype(jnp.bfloat16), 0).astype(jnp.float32)
    mid = (xf + summed).astype(jnp.bfloat16)
    mid_f = mid.astype(jnp.float32)
    post_normed = lax.optimization_barrier(rms(mid_f, post_gain).astype(jnp.bfloat16))
    gate_up = jnp.dot(post_normed, w_gathered[:, : 2 * ff_local], preferred_element_type=jnp.float32)
    act = (jax.nn.silu(gate_up[:, :ff_local]) * gate_up[:, ff_local:]).astype(jnp.bfloat16)
    terms = lax.dot_general(
        act,
        w_gathered[:, 2 * ff_local : 3 * ff_local],
        (((1,), (1,)), ((), ())),
        preferred_element_type=jnp.float32,
    )
    hidden = tp_sum(terms.astype(jnp.bfloat16), 1, mid)
    return (hidden, key_cache, value_cache)


def solution(mesh):
    in_specs = (
        P("seq", None),
        P(),
        P(None, "tp"),
        P(None, "tp"),
        P(None, "tp"),
        P("tp", None),
        P(),
        P(),
        P("seq"),
        P("seq"),
        P(),
        P("seq", "tp"),
        P("seq", "tp"),
        P("tp", "seq"),
    )
    out_specs = (P("seq", None), P("seq", "tp"), P("seq", "tp"))
    return jax.shard_map(body, mesh=mesh, in_specs=in_specs, out_specs=out_specs, check_vma=False)
```

```python
import functools
import math

import jax
import jax.numpy as jnp
from jax import lax
from jax.experimental import pallas as pl
from jax.experimental.pallas import tpu as pltpu
from jax.sharding import PartitionSpec as P

MESH = pl.DeviceIdType.MESH


def rms(v, gain):
    return v * lax.rsqrt(jnp.mean(v * v, axis=-1, keepdims=True) + 1e-06) * gain


def rope(v, place):
    half = v.shape[-1] // 2
    freqs = 1000000.0 ** (-2.0 * jnp.arange(half, dtype=jnp.float32) / v.shape[-1])
    angle = place.astype(jnp.float32)[:, None] * freqs[None, :]
    cosine = jnp.cos(angle)[:, None, :]
    sine = jnp.sin(angle)[:, None, :]
    block_start = v[..., :half]
    second = v[..., half:]
    return jnp.concatenate(
        [block_start * cosine - second * sine, second * cosine + block_start * sine], axis=-1
    )


def tp_sum_kernel(n, parts, with_base, *refs):
    if with_base:
        x_ref, base_ref, out_ref, slots, reduced, send1, recv1, send2, recv2 = refs
    else:
        x_ref, out_ref, slots, reduced, send1, recv1, send2, recv2 = refs
    me = lax.axis_index("tp")
    row = lax.axis_index("seq")
    cols = x_ref.shape[1] // n
    rows_p = x_ref.shape[0] // parts

    barrier = pltpu.get_barrier_semaphore()
    for k in range(1, n):
        pl.semaphore_signal(barrier, inc=1, device_id=(row, lax.rem(me + k, n)), device_id_type=MESH)
    pl.semaphore_wait(barrier, n - 1)

    def cols_of(owner):
        return pl.ds(pl.multiple_of(owner * cols, cols), cols)

    def rows_of(c):
        return pl.ds(c * rows_p, rows_p)

    first = []
    for c in range(parts):
        part = []
        for k in range(1, n):
            peer = lax.rem(me + k, n)
            copy = pltpu.make_async_remote_copy(
                src_ref=x_ref.at[rows_of(c), cols_of(peer)],
                dst_ref=slots.at[k, rows_of(c)],
                send_sem=send1.at[c, k],
                recv_sem=recv1.at[c, k],
                device_id=(row, peer),
                device_id_type=MESH,
            )
            copy.start()
            part.append(copy)
        first.append(part)

    second = []
    for c in range(parts):
        for copy in first[c]:
            copy.wait()
        total = x_ref[rows_of(c), cols_of(me)].astype(jnp.float32)
        for k in range(1, n):
            total = total + slots[k, rows_of(c)].astype(jnp.float32)
        reduced[rows_of(c)] = total.astype(reduced.dtype)
        out_ref[rows_of(c), cols_of(me)] = reduced[rows_of(c)]
        for k in range(1, n):
            peer = lax.rem(me + k, n)
            copy = pltpu.make_async_remote_copy(
                src_ref=reduced.at[rows_of(c)],
                dst_ref=out_ref.at[rows_of(c), cols_of(me)],
                send_sem=send2.at[c, k],
                recv_sem=recv2.at[c, k],
                device_id=(row, peer),
                device_id_type=MESH,
            )
            copy.start()
            second.append(copy)
    for copy in second:
        copy.wait()
    if with_base:
        out_ref[...] = (base_ref[...].astype(jnp.float32) + out_ref[...].astype(jnp.float32)).astype(
            out_ref.dtype
        )


def tp_sum(x, collective_id, base=None):
    n = lax.axis_size("tp")
    rows, width = x.shape
    cols = width // n
    operands = (x,) if base is None else (x, base)
    parts = 2 if rows % 32 == 0 else 1
    return pl.pallas_call(
        functools.partial(tp_sum_kernel, n, parts, base is not None),
        out_shape=jax.ShapeDtypeStruct((rows, width), x.dtype),
        in_specs=[pl.BlockSpec(memory_space=pltpu.VMEM)] * len(operands),
        out_specs=pl.BlockSpec(memory_space=pltpu.VMEM),
        scratch_shapes=[
            pltpu.VMEM((n, rows, cols), x.dtype),
            pltpu.VMEM((rows, cols), x.dtype),
            pltpu.SemaphoreType.DMA((parts, n)),
            pltpu.SemaphoreType.DMA((parts, n)),
            pltpu.SemaphoreType.DMA((parts, n)),
            pltpu.SemaphoreType.DMA((parts, n)),
        ],
        compiler_params=pltpu.CompilerParams(collective_id=collective_id, has_side_effects=True),
    )(*operands)


def attention_kernel(info, q_ref, q_last_ref, q_first_ref, kv_ref, o_ref, top_ref, total_ref, acc_ref):
    step = pl.program_id(0)
    groups, rows_all, head_size = q_ref.shape
    shards_per, both, _ = kv_ref.shape
    rows = both // 2
    width = shards_per * rows
    rows_q = o_ref.shape[0]
    per_group = rows_all // rows_q
    scale = 1.0 / math.sqrt(head_size)

    @pl.when(step == 0)
    def _():
        top_ref[...] = jnp.full(top_ref.shape, -1e30, jnp.float32)
        total_ref[...] = jnp.zeros(total_ref.shape, jnp.float32)
        acc_ref[...] = jnp.zeros(acc_ref.shape, jnp.float32)

    offset = step * width
    needed = (step >= info[0]) & (step <= info[1])
    whole = (offset >= info[2]) & (offset + width - 1 <= info[3])

    def run(masked):
        for g in range(groups):
            q = q_ref[g]
            k = kv_ref[:, :rows, g * head_size : (g + 1) * head_size].reshape(width, head_size)
            v = kv_ref[:, rows:, g * head_size : (g + 1) * head_size].reshape(width, head_size)
            s = lax.dot_general(q, k, (((1,), (1,)), ((), ())), preferred_element_type=jnp.float32) * scale
            if masked:
                k_index = offset + lax.broadcasted_iota(jnp.int32, s.shape, 1)
                allowed = (k_index <= q_last_ref[:, :1]) & (k_index >= q_first_ref[:, :1])
                s = jnp.where(allowed, s, -1e30)
            top = top_ref[g]
            new_top = jnp.maximum(top, jnp.max(s, axis=-1, keepdims=True))
            p = jnp.exp(s - new_top)
            if masked:
                p = jnp.where(allowed, p, 0.0)
            decay = jnp.exp(top - new_top)
            total_ref[g] = total_ref[g] * decay + jnp.sum(p, axis=-1, keepdims=True)
            acc_ref[g] = acc_ref[g] * decay + jnp.dot(
                p.astype(jnp.bfloat16), v, preferred_element_type=jnp.float32
            )
            top_ref[g] = new_top

    @pl.when(needed & whole)
    def _():
        run(False)

    @pl.when(needed & jnp.logical_not(whole))
    def _():
        run(True)

    @pl.when(step == pl.num_programs(0) - 1)
    def _():
        for g in range(groups):
            out = acc_ref[g] / total_ref[g]
            for h in range(per_group):
                col = (g * per_group + h) * head_size
                o_ref[:, col : col + head_size] = out[h * rows_q : (h + 1) * rows_q].astype(o_ref.dtype)


def attention(q_grouped, q_last, q_first, gathered, info, rows, kv_rows_per_shard, shards_per):
    groups, rows_all, head_size = q_grouped.shape
    shards, _, width_all = gathered.shape
    blocks = shards // shards_per
    out_cols = rows_all // rows * groups * head_size

    def kv_map(j, info):
        return (jnp.minimum(jnp.maximum(j, info[0]), info[1]), 0, 0)

    grid_spec = pltpu.PrefetchScalarGridSpec(
        num_scalar_prefetch=1,
        grid=(blocks,),
        in_specs=[
            pl.BlockSpec((groups, rows_all, head_size), lambda j, info: (0, 0, 0)),
            pl.BlockSpec(q_last.shape, lambda j, info: (0, 0)),
            pl.BlockSpec(q_first.shape, lambda j, info: (0, 0)),
            pl.BlockSpec((shards_per, kv_rows_per_shard, width_all), kv_map),
        ],
        out_specs=pl.BlockSpec((rows, out_cols), lambda j, info: (0, 0)),
        scratch_shapes=[
            pltpu.VMEM((groups, rows_all, 1), jnp.float32),
            pltpu.VMEM((groups, rows_all, 1), jnp.float32),
            pltpu.VMEM((groups, rows_all, head_size), jnp.float32),
        ],
    )
    return pl.pallas_call(
        attention_kernel,
        out_shape=jax.ShapeDtypeStruct((rows, out_cols), jnp.bfloat16),
        grid_spec=grid_spec,
        compiler_params=pltpu.CompilerParams(dimension_semantics=("arbitrary",)),
    )(info, q_grouped, q_last, q_first, gathered)


def body(
    layer_input,
    norm_gain,
    w_query,
    key_weight,
    value_weight,
    w_out,
    query_gain,
    key_gain,
    seg_ids,
    positions,
    post_gain,
    w_gate,
    w_up,
    w_down,
):
    rows = layer_input.shape[0]
    head_size = query_gain.shape[0]
    query_local = w_query.shape[1] // head_size
    kv_local = key_weight.shape[1] // head_size
    kv_cols = kv_local * head_size
    head_group = query_local // kv_local
    scale = 1.0 / math.sqrt(head_size)
    shards = lax.axis_size("seq")
    xf = layer_input.astype(jnp.float32)
    normed_input = rms(xf, norm_gain).astype(jnp.bfloat16)
    query_matrix = jnp.dot(normed_input, w_query, preferred_element_type=jnp.float32).reshape(
        rows, query_local, head_size
    )
    query_matrix = rope(rms(query_matrix, query_gain), positions).astype(jnp.bfloat16)
    key_value = jnp.dot(
        normed_input,
        jnp.concatenate([key_weight, value_weight], axis=1),
        preferred_element_type=jnp.float32,
    )
    key_matrix = key_value[:, :kv_cols].reshape(rows, kv_local, head_size)
    key_matrix = rope(rms(key_matrix, key_gain), positions).astype(jnp.bfloat16)
    key_cache = key_matrix.reshape(rows, kv_cols)
    value_cache = key_value[:, kv_cols:].astype(jnp.bfloat16)

    width_all = 2 * kv_cols
    ff_rows, ff_local = w_gate.shape
    rest = ff_local - width_all
    down_t = w_down.T
    kv_packed = jnp.concatenate([key_cache, value_cache], axis=0)
    kv_gathered = lax.all_gather(kv_packed, "seq", axis=0, tiled=False)
    weights_packed = jnp.concatenate([w_gate, w_up, down_t], axis=1)

    me = lax.axis_index("seq")
    first = me * rows
    my_last = first + rows - 1
    q_index = first + jnp.arange(rows, dtype=jnp.int32)
    q_start = q_index - positions
    shards_per = 1
    for trial in range(1, max(1, 1024 // rows) + 1):
        if shards % trial == 0:
            shards_per = trial
    width = rows * shards_per
    info = jnp.stack([q_start[0] // width, my_last // width, q_start[rows - 1], first])
    q_grouped = (
        query_matrix.reshape(rows, kv_local, head_group, head_size)
        .transpose(1, 2, 0, 3)
        .reshape(kv_local, head_group * rows, head_size)
    )
    lanes = 128
    q_last = jnp.broadcast_to(jnp.tile(q_index, head_group)[:, None], (head_group * rows, lanes))
    q_first = jnp.broadcast_to(jnp.tile(q_start, head_group)[:, None], (head_group * rows, lanes))
    weights_packed, q_grouped, q_last, q_first, info = lax.optimization_barrier(
        (weights_packed, q_grouped, q_last, q_first, info)
    )
    w_gathered = lax.all_gather(weights_packed, "seq", axis=0, tiled=False).reshape(
        shards * ff_rows, weights_packed.shape[1]
    )
    attended = attention(q_grouped, q_last, q_first, kv_gathered, info, rows, 2 * rows, shards_per)
    partial_out = jnp.dot(attended, w_out, preferred_element_type=jnp.float32)
    summed = tp_sum(partial_out.astype(jnp.bfloat16), 0).astype(jnp.float32)
    mid = (xf + summed).astype(jnp.bfloat16)
    mid_f = mid.astype(jnp.float32)
    post_normed = lax.optimization_barrier(rms(mid_f, post_gain).astype(jnp.bfloat16))
    gate_up = jnp.dot(post_normed, w_gathered[:, : 2 * ff_local], preferred_element_type=jnp.float32)
    act = (jax.nn.silu(gate_up[:, :ff_local]) * gate_up[:, ff_local:]).astype(jnp.bfloat16)
    terms = lax.dot_general(
        act,
        w_gathered[:, 2 * ff_local : 3 * ff_local],
        (((1,), (1,)), ((), ())),
        preferred_element_type=jnp.float32,
    )
    hidden = tp_sum(terms.astype(jnp.bfloat16), 1, mid)
    return (hidden, key_cache, value_cache)


def solution(mesh):
    in_specs = (
        P("seq", None),
        P(),
        P(None, "tp"),
        P(None, "tp"),
        P(None, "tp"),
        P("tp", None),
        P(),
        P(),
        P("seq"),
        P("seq"),
        P(),
        P("seq", "tp"),
        P("seq", "tp"),
        P("tp", "seq"),
    )
    out_specs = (P("seq", None), P("seq", "tp"), P("seq", "tp"))
    return jax.shard_map(body, mesh=mesh, in_specs=in_specs, out_specs=out_specs, check_vma=False)
```

```python
import functools
import math

import jax
import jax.numpy as jnp
from jax import lax
from jax.experimental import pallas as pl
from jax.experimental.pallas import tpu as pltpu
from jax.sharding import PartitionSpec as P

MESH = pl.DeviceIdType.MESH


def rms(v, gain):
    return v * lax.rsqrt(jnp.mean(v * v, axis=-1, keepdims=True) + 1e-06) * gain


def rope(v, place):
    half = v.shape[-1] // 2
    freqs = 1000000.0 ** (-2.0 * jnp.arange(half, dtype=jnp.float32) / v.shape[-1])
    angle = place.astype(jnp.float32)[:, None] * freqs[None, :]
    cosine = jnp.cos(angle)[:, None, :]
    sine = jnp.sin(angle)[:, None, :]
    block_start = v[..., :half]
    second = v[..., half:]
    return jnp.concatenate(
        [block_start * cosine - second * sine, second * cosine + block_start * sine], axis=-1
    )


def tp_sum_kernel(n, parts, with_base, *refs):
    if with_base:
        x_ref, base_ref, out_ref, slots, reduced, send1, recv1, send2, recv2 = refs
    else:
        x_ref, out_ref, slots, reduced, send1, recv1, send2, recv2 = refs
    me = lax.axis_index("tp")
    row = lax.axis_index("seq")
    cols = x_ref.shape[1] // n
    rows_p = x_ref.shape[0] // parts

    barrier = pltpu.get_barrier_semaphore()
    for k in range(1, n):
        pl.semaphore_signal(barrier, inc=1, device_id=(row, lax.rem(me + k, n)), device_id_type=MESH)
    pl.semaphore_wait(barrier, n - 1)

    def cols_of(owner):
        return pl.ds(pl.multiple_of(owner * cols, cols), cols)

    def rows_of(c):
        return pl.ds(c * rows_p, rows_p)

    first = []
    for c in range(parts):
        part = []
        for k in range(1, n):
            peer = lax.rem(me + k, n)
            copy = pltpu.make_async_remote_copy(
                src_ref=x_ref.at[rows_of(c), cols_of(peer)],
                dst_ref=slots.at[k, rows_of(c)],
                send_sem=send1.at[c, k],
                recv_sem=recv1.at[c, k],
                device_id=(row, peer),
                device_id_type=MESH,
            )
            copy.start()
            part.append(copy)
        first.append(part)

    second = []
    for c in range(parts):
        for copy in first[c]:
            copy.wait()
        total = x_ref[rows_of(c), cols_of(me)].astype(jnp.float32)
        for k in range(1, n):
            total = total + slots[k, rows_of(c)].astype(jnp.float32)
        reduced[rows_of(c)] = total.astype(reduced.dtype)
        out_ref[rows_of(c), cols_of(me)] = reduced[rows_of(c)]
        for k in range(1, n):
            peer = lax.rem(me + k, n)
            copy = pltpu.make_async_remote_copy(
                src_ref=reduced.at[rows_of(c)],
                dst_ref=out_ref.at[rows_of(c), cols_of(me)],
                send_sem=send2.at[c, k],
                recv_sem=recv2.at[c, k],
                device_id=(row, peer),
                device_id_type=MESH,
            )
            copy.start()
            second.append(copy)
    for copy in second:
        copy.wait()
    if with_base:
        out_ref[...] = (base_ref[...].astype(jnp.float32) + out_ref[...].astype(jnp.float32)).astype(
            out_ref.dtype
        )


def tp_sum(x, collective_id, base=None):
    n = lax.axis_size("tp")
    rows, width = x.shape
    cols = width // n
    operands = (x,) if base is None else (x, base)
    parts = 2 if rows % 32 == 0 else 1
    return pl.pallas_call(
        functools.partial(tp_sum_kernel, n, parts, base is not None),
        out_shape=jax.ShapeDtypeStruct((rows, width), x.dtype),
        in_specs=[pl.BlockSpec(memory_space=pltpu.VMEM)] * len(operands),
        out_specs=pl.BlockSpec(memory_space=pltpu.VMEM),
        scratch_shapes=[
            pltpu.VMEM((n, rows, cols), x.dtype),
            pltpu.VMEM((rows, cols), x.dtype),
            pltpu.SemaphoreType.DMA((parts, n)),
            pltpu.SemaphoreType.DMA((parts, n)),
            pltpu.SemaphoreType.DMA((parts, n)),
            pltpu.SemaphoreType.DMA((parts, n)),
        ],
        compiler_params=pltpu.CompilerParams(collective_id=collective_id, has_side_effects=True),
    )(*operands)


def attention_kernel(info, q_ref, q_last_ref, q_first_ref, kv_ref, o_ref, top_ref, total_ref, acc_ref):
    step = pl.program_id(0)
    groups, rows_all, head_size = q_ref.shape
    shards_per, both, _ = kv_ref.shape
    rows = both // 2
    width = shards_per * rows
    rows_q = o_ref.shape[0]
    per_group = rows_all // rows_q
    scale = 1.0 / math.sqrt(head_size)

    @pl.when(step == 0)
    def _():
        top_ref[...] = jnp.full(top_ref.shape, -1e30, jnp.float32)
        total_ref[...] = jnp.zeros(total_ref.shape, jnp.float32)
        acc_ref[...] = jnp.zeros(acc_ref.shape, jnp.float32)

    offset = step * width
    needed = (step >= info[0]) & (step <= info[1])
    whole = (offset >= info[2]) & (offset + width - 1 <= info[3])

    def run(masked):
        for g in range(groups):
            q = q_ref[g]
            k = kv_ref[:, :rows, g * head_size : (g + 1) * head_size].reshape(width, head_size)
            v = kv_ref[:, rows:, g * head_size : (g + 1) * head_size].reshape(width, head_size)
            s = lax.dot_general(q, k, (((1,), (1,)), ((), ())), preferred_element_type=jnp.float32) * scale
            if masked:
                k_index = offset + lax.broadcasted_iota(jnp.int32, s.shape, 1)
                allowed = (k_index <= q_last_ref[:, :1]) & (k_index >= q_first_ref[:, :1])
                s = jnp.where(allowed, s, -1e30)
            top = top_ref[g]
            new_top = jnp.maximum(top, jnp.max(s, axis=-1, keepdims=True))
            p = jnp.exp(s - new_top)
            if masked:
                p = jnp.where(allowed, p, 0.0)
            decay = jnp.exp(top - new_top)
            total_ref[g] = total_ref[g] * decay + jnp.sum(p, axis=-1, keepdims=True)
            acc_ref[g] = acc_ref[g] * decay + jnp.dot(
                p.astype(jnp.bfloat16), v, preferred_element_type=jnp.float32
            )
            top_ref[g] = new_top

    @pl.when(needed & whole)
    def _():
        run(False)

    @pl.when(needed & jnp.logical_not(whole))
    def _():
        run(True)

    @pl.when(step == pl.num_programs(0) - 1)
    def _():
        for g in range(groups):
            out = acc_ref[g] / total_ref[g]
            for h in range(per_group):
                col = (g * per_group + h) * head_size
                o_ref[:, col : col + head_size] = out[h * rows_q : (h + 1) * rows_q].astype(o_ref.dtype)


def attention(q_grouped, q_last, q_first, gathered, info, rows, kv_rows_per_shard, shards_per):
    groups, rows_all, head_size = q_grouped.shape
    shards, _, width_all = gathered.shape
    blocks = shards // shards_per
    out_cols = rows_all // rows * groups * head_size

    def kv_map(j, info):
        return (jnp.minimum(jnp.maximum(j, info[0]), info[1]), 0, 0)

    grid_spec = pltpu.PrefetchScalarGridSpec(
        num_scalar_prefetch=1,
        grid=(blocks,),
        in_specs=[
            pl.BlockSpec((groups, rows_all, head_size), lambda j, info: (0, 0, 0)),
            pl.BlockSpec(q_last.shape, lambda j, info: (0, 0)),
            pl.BlockSpec(q_first.shape, lambda j, info: (0, 0)),
            pl.BlockSpec((shards_per, kv_rows_per_shard, width_all), kv_map),
        ],
        out_specs=pl.BlockSpec((rows, out_cols), lambda j, info: (0, 0)),
        scratch_shapes=[
            pltpu.VMEM((groups, rows_all, 1), jnp.float32),
            pltpu.VMEM((groups, rows_all, 1), jnp.float32),
            pltpu.VMEM((groups, rows_all, head_size), jnp.float32),
        ],
    )
    return pl.pallas_call(
        attention_kernel,
        out_shape=jax.ShapeDtypeStruct((rows, out_cols), jnp.bfloat16),
        grid_spec=grid_spec,
        compiler_params=pltpu.CompilerParams(dimension_semantics=("arbitrary",)),
    )(info, q_grouped, q_last, q_first, gathered)


def body(
    layer_input,
    norm_gain,
    w_query,
    key_weight,
    value_weight,
    w_out,
    query_gain,
    key_gain,
    seg_ids,
    positions,
    post_gain,
    w_gate,
    w_up,
    w_down,
):
    rows = layer_input.shape[0]
    head_size = query_gain.shape[0]
    query_local = w_query.shape[1] // head_size
    kv_local = key_weight.shape[1] // head_size
    kv_cols = kv_local * head_size
    head_group = query_local // kv_local
    scale = 1.0 / math.sqrt(head_size)
    shards = lax.axis_size("seq")
    xf = layer_input.astype(jnp.float32)
    normed_input = rms(xf, norm_gain).astype(jnp.bfloat16)
    query_matrix = jnp.dot(normed_input, w_query, preferred_element_type=jnp.float32).reshape(
        rows, query_local, head_size
    )
    query_matrix = rope(rms(query_matrix, query_gain), positions).astype(jnp.bfloat16)
    key_matrix = jnp.dot(normed_input, key_weight, preferred_element_type=jnp.float32).reshape(
        rows, kv_local, head_size
    )
    key_matrix = rope(rms(key_matrix, key_gain), positions).astype(jnp.bfloat16)
    key_cache = key_matrix.reshape(rows, kv_cols)
    value_cache = jnp.dot(normed_input, value_weight, preferred_element_type=jnp.float32).astype(
        jnp.bfloat16
    )

    width_all = 2 * kv_cols
    ff_rows, ff_local = w_gate.shape
    rest = ff_local - width_all
    down_t = w_down.T
    kv_packed = jnp.concatenate([key_cache, value_cache], axis=0)
    kv_gathered = lax.all_gather(kv_packed, "seq", axis=0, tiled=False)
    weights_packed = jnp.concatenate([w_gate, w_up, down_t], axis=1)

    me = lax.axis_index("seq")
    first = me * rows
    my_last = first + rows - 1
    q_index = first + jnp.arange(rows, dtype=jnp.int32)
    q_start = q_index - positions
    shards_per = 1
    for trial in range(1, max(1, 1024 // rows) + 1):
        if shards % trial == 0:
            shards_per = trial
    width = rows * shards_per
    info = jnp.stack([q_start[0] // width, my_last // width, q_start[rows - 1], first])
    q_grouped = (
        query_matrix.reshape(rows, kv_local, head_group, head_size)
        .transpose(1, 2, 0, 3)
        .reshape(kv_local, head_group * rows, head_size)
    )
    lanes = 128
    q_last = jnp.broadcast_to(jnp.tile(q_index, head_group)[:, None], (head_group * rows, lanes))
    q_first = jnp.broadcast_to(jnp.tile(q_start, head_group)[:, None], (head_group * rows, lanes))
    weights_packed, q_grouped, q_last, q_first, info = lax.optimization_barrier(
        (weights_packed, q_grouped, q_last, q_first, info)
    )
    w_gathered = lax.all_gather(weights_packed, "seq", axis=0, tiled=False).reshape(
        shards * ff_rows, weights_packed.shape[1]
    )
    attended = attention(q_grouped, q_last, q_first, kv_gathered, info, rows, 2 * rows, shards_per)
    partial_out = jnp.dot(attended, w_out, preferred_element_type=jnp.float32)
    mid = tp_sum(partial_out.astype(jnp.bfloat16), 0, layer_input)
    mid_f = mid.astype(jnp.float32)
    post_normed = lax.optimization_barrier(rms(mid_f, post_gain).astype(jnp.bfloat16))
    gate_up = jnp.dot(post_normed, w_gathered[:, : 2 * ff_local], preferred_element_type=jnp.float32)
    act = (jax.nn.silu(gate_up[:, :ff_local]) * gate_up[:, ff_local:]).astype(jnp.bfloat16)
    terms = lax.dot_general(
        act,
        w_gathered[:, 2 * ff_local : 3 * ff_local],
        (((1,), (1,)), ((), ())),
        preferred_element_type=jnp.float32,
    )
    hidden = tp_sum(terms.astype(jnp.bfloat16), 1, mid)
    return (hidden, key_cache, value_cache)


def solution(mesh):
    in_specs = (
        P("seq", None),
        P(),
        P(None, "tp"),
        P(None, "tp"),
        P(None, "tp"),
        P("tp", None),
        P(),
        P(),
        P("seq"),
        P("seq"),
        P(),
        P("seq", "tp"),
        P("seq", "tp"),
        P("tp", "seq"),
    )
    out_specs = (P("seq", None), P("seq", "tp"), P("seq", "tp"))
    return jax.shard_map(body, mesh=mesh, in_specs=in_specs, out_specs=out_specs, check_vma=False)
```
